512 devices in a mesh: depth: 16 (over z_hi, x), rows: 32 (over z_lo, y, core).
Axes of the slice: x: 4, y: 4, z: 16 (z_hi: 4, z_lo: 4; z = z_hi * 4 + z_lo), core: 2. Of those that a mesh axis runs over, the one named last changes fastest.
Arguments:
- hologram: bfloat16 [4096, 4096], P('rows'), may hold values from 0.25 to 1.75
- background: bfloat16 [4096, 4096], P('rows'), may hold values from 0.5 to 2
Outputs:
- focus: float32 [4096, 4096], P('rows')
The draws below stay inside these ranges and needn't reach their ends.
All inputs are finite; a program needn't handle non-finite values.
Results may differ from the reference program's by a relative error of at most 0.025.
Values may be sent and summed in bfloat16 or wider, within the bound.
A program may use at most 64 MiB of HBM per device.

```python
import math
import jax
import jax.numpy as jnp
from jax import lax

N = 4096
RADIX = 64
PLANES = 16


def block_scale(stream_key, shape, split, low, largest):
    def one(position, blocks):
        steps = jax.random.uniform(jax.random.fold_in(jax.random.fold_in(stream_key, 6), position), (blocks,), jnp.float32, low / len(split), largest / len(split))
        return jnp.repeat(jnp.exp(steps), shape[position] // blocks).reshape((-1,) + (1,) * (len(shape) - position - 1))

    gain = one(*split[0])
    for cut in split[1:]:
        gain = gain * one(*cut)
    return gain


def setup_inputs(seed: int = 0) -> dict:
    seeds = jax.random.split(jax.random.key(seed), 3)
    hologram = jnp.clip(0.25 + 1.5 * jax.random.uniform(seeds[0], (N, N), jnp.float32) ** block_scale(seeds[0], (N, N), ((0, 32),), -0.2, 0.2), 0.25, 1.75).astype(jnp.bfloat16)
    background = jnp.clip(jnp.exp(math.log(2.0) - 1.3862944 * jax.random.uniform(seeds[1], (N, N), jnp.float32) ** block_scale(seeds[1], (N, N), ((0, 32),), -0.2, 0.2)), 0.5, 2.0).astype(jnp.bfloat16)
    return dict(hologram=hologram, background=background)


wave_number = 0.6
depth_start = 8.0
depth_step = 2.0

def fourier_tables(radix_size, sign_value):
    indices = jnp.arange(radix_size, dtype=jnp.int32)
    products = indices[:, None] * indices[None, :] % radix_size
    angles = products.astype(jnp.float32) * (sign_value * 2.0 * math.pi / radix_size)
    scaling = 1.0 / math.sqrt(radix_size)
    cosine_part = jnp.cos(angles) * scaling
    sine_part = jnp.sin(angles) * scaling
    matrix = jnp.stack([jnp.stack([cosine_part, -sine_part]), jnp.stack([sine_part, cosine_part])])
    return matrix.astype(jnp.bfloat16)

def twiddle_table(radix_size, sign_value):
    indices = jnp.arange(radix_size, dtype=jnp.int32)
    total = radix_size * radix_size
    products = indices[:, None] * indices[None, :] % total
    angles = products.astype(jnp.float32) * (sign_value * 2.0 * math.pi / total)
    return (jnp.cos(angles), jnp.sin(angles))

def rotate(data, cosine_part, sine_part):
    return jnp.stack([data[0] * cosine_part - data[1] * sine_part, data[0] * sine_part + data[1] * cosine_part])

def contract(form, matrix, data):
    return jnp.einsum(form, matrix.astype(jnp.float32), data.astype(jnp.float32))

def forward_last(data):
    batch_size = data.shape[1]
    shaped = data.reshape(2, batch_size, RADIX, RADIX)
    matrix = fourier_tables(RADIX, -1.0)
    cosine_part, sine_part = twiddle_table(RADIX, -1.0)
    opening = contract('ocka,cmab->omkb', matrix, shaped)
    sectioned = rotate(opening, cosine_part, sine_part).astype(jnp.bfloat16)
    closing = contract('ocjb,cmkb->omkj', matrix, sectioned)
    return closing.reshape(2, batch_size, N).astype(jnp.bfloat16)

def forward_first(data):
    batch_size = data.shape[2]
    shaped = data.reshape(2, RADIX, RADIX, batch_size)
    matrix = fourier_tables(RADIX, -1.0)
    cosine_part, sine_part = twiddle_table(RADIX, -1.0)
    opening = contract('ocka,cabm->okbm', matrix, shaped)
    sectioned = rotate(opening, cosine_part[:, :, None], sine_part[:, :, None]).astype(jnp.bfloat16)
    closing = contract('ocjb,ckbm->okjm', matrix, sectioned)
    return closing.reshape(2, N, batch_size).astype(jnp.bfloat16)

def inverse_last(data):
    batch_size = data.shape[1]
    shaped = data.reshape(2, batch_size, RADIX, RADIX)
    matrix = fourier_tables(RADIX, 1.0)
    cosine_part, sine_part = twiddle_table(RADIX, 1.0)
    opening = contract('ocbj,cmkj->omkb', matrix, shaped)
    sectioned = rotate(opening, cosine_part, sine_part).astype(jnp.bfloat16)
    closing = contract('ocak,cmkb->omab', matrix, sectioned)
    return closing.reshape(2, batch_size, N)

def inverse_first(data):
    batch_size = data.shape[2]
    shaped = data.reshape(2, RADIX, RADIX, batch_size)
    matrix = fourier_tables(RADIX, 1.0)
    cosine_part, sine_part = twiddle_table(RADIX, 1.0)
    opening = contract('ocbj,ckjm->okbm', matrix, shaped)
    sectioned = rotate(opening, cosine_part[:, :, None], sine_part[:, :, None]).astype(jnp.bfloat16)
    closing = contract('ocak,ckbm->oabm', matrix, sectioned)
    return closing.reshape(2, N, batch_size)

def frequencies(positions):
    natural = positions // RADIX + RADIX * (positions % RADIX)
    signed_freq = jnp.where(natural >= N // 2, natural - N, natural)
    return signed_freq.astype(jnp.float32) / N

def propagator(freq_rows, freq_cols, distance):
    radial = freq_rows[:, None] ** 2 + freq_cols[None, :] ** 2
    limit = wave_number * wave_number
    amplitude = jnp.exp(-2.0 * math.pi * distance * jnp.sqrt(jnp.maximum(radial - limit, 0.0)))
    phase_angle = 2.0 * math.pi * distance * (jnp.sqrt(jnp.maximum(limit - radial, 0.0)) - wave_number)
    return (amplitude * jnp.cos(phase_angle), amplitude * jnp.sin(phase_angle))

def propagate(spectrum, cosine_part, sine_part):
    return rotate(spectrum.astype(jnp.float32), cosine_part, sine_part).astype(jnp.bfloat16)

def sharpness(lower_plane, centre_block, upper_plane, north_row, south_row):
    centre = centre_block.astype(jnp.float32)
    east_col = jnp.concatenate([centre[..., 1:], centre[..., -1:]], axis=-1)
    west_col = jnp.concatenate([centre[..., :1], centre[..., :-1]], axis=-1)
    depth_diff = upper_plane.astype(jnp.float32) - lower_plane.astype(jnp.float32)
    row_diff = south_row.astype(jnp.float32) - north_row.astype(jnp.float32)
    col_diff = east_col - west_col
    return (depth_diff * depth_diff + row_diff * row_diff + col_diff * col_diff) / 8.0

def reference(hologram, background):
    contrast = (hologram.astype(jnp.float32) / background.astype(jnp.float32) - 1.0).astype(jnp.bfloat16)
    hologram_field = jnp.stack([contrast, jnp.zeros_like(contrast)])
    spectrum = forward_first(forward_last(hologram_field))
    positions = jnp.arange(N, dtype=jnp.int32)
    freq_all = frequencies(positions)

    def intensity_of(plane_slot):
        distance = depth_start + depth_step * plane_slot.astype(jnp.float32)
        cosine_part, sine_part = propagator(freq_all, freq_all, distance)
        propagated = propagate(spectrum, cosine_part, sine_part)
        halfway = inverse_first(propagated).astype(jnp.bfloat16)
        result_field = inverse_last(halfway)
        return (result_field[0] * result_field[0] + result_field[1] * result_field[1]).astype(jnp.bfloat16)
    opening_plane = intensity_of(jnp.int32(0))

    def advance(carry, plane_slot):
        previous, current, sharpest = carry
        following = intensity_of(jnp.minimum(plane_slot + 1, PLANES - 1).astype(jnp.int32))
        north_row = jnp.concatenate([current[:1], current[:-1]], axis=0)
        south_row = jnp.concatenate([current[1:], current[-1:]], axis=0)
        scores = sharpness(previous, current, following, north_row, south_row)
        return ((current, following, jnp.maximum(sharpest, scores)), None)
    start = (opening_plane, opening_plane, jnp.zeros((N, N), jnp.float32))
    final, unused = lax.scan(advance, start, jnp.arange(PLANES, dtype=jnp.int32))
    return final[2]
```

```python
import functools
import math

import jax
import jax.numpy as jnp
from jax import lax
from jax.experimental import pallas as pl
from jax.experimental.pallas import tpu as pltpu
from jax.sharding import Mesh
from jax.sharding import PartitionSpec as P

N = 4096
RADIX = 64
PLANES = 16
AXES = ("zh", "x", "zl", "y", "c")
SIZES = (4, 4, 4, 4, 2)
MESH = pl.DeviceIdType.MESH

wave_number = 0.6
depth_start = 8.0
depth_step = 2.0


def fourier_tables(radix_size, sign_value):
    indices = jnp.arange(radix_size, dtype=jnp.int32)
    products = indices[:, None] * indices[None, :] % radix_size
    angles = products.astype(jnp.float32) * (sign_value * 2.0 * math.pi / radix_size)
    scaling = 1.0 / math.sqrt(radix_size)
    cosine_part = jnp.cos(angles) * scaling
    sine_part = jnp.sin(angles) * scaling
    matrix = jnp.stack([jnp.stack([cosine_part, -sine_part]), jnp.stack([sine_part, cosine_part])])
    return matrix.astype(jnp.bfloat16)


def twiddle_table(radix_size, sign_value):
    indices = jnp.arange(radix_size, dtype=jnp.int32)
    total = radix_size * radix_size
    products = indices[:, None] * indices[None, :] % total
    angles = products.astype(jnp.float32) * (sign_value * 2.0 * math.pi / total)
    return (jnp.cos(angles), jnp.sin(angles))


def rotate(data, cosine_part, sine_part):
    return jnp.stack(
        [data[0] * cosine_part - data[1] * sine_part, data[0] * sine_part + data[1] * cosine_part]
    )


def contract(form, matrix, data):
    return jnp.einsum(form, matrix, data, preferred_element_type=jnp.float32)


def forward_first(data):
    batch_size = data.shape[2]
    shaped = data.reshape(2, RADIX, RADIX, batch_size)
    matrix = fourier_tables(RADIX, -1.0)
    cosine_part, sine_part = twiddle_table(RADIX, -1.0)
    opening = contract("ocka,cabm->okbm", matrix, shaped)
    sectioned = rotate(opening, cosine_part[:, :, None], sine_part[:, :, None]).astype(jnp.bfloat16)
    closing = contract("ocjb,ckbm->okjm", matrix, sectioned)
    return closing.reshape(2, N, batch_size).astype(jnp.bfloat16)


def inverse_first(data):
    batch_size = data.shape[2]
    shaped = data.reshape(2, RADIX, RADIX, batch_size)
    matrix = fourier_tables(RADIX, 1.0)
    cosine_part, sine_part = twiddle_table(RADIX, 1.0)
    opening = contract("ocbj,ckjm->okbm", matrix, shaped)
    sectioned = rotate(opening, cosine_part[:, :, None], sine_part[:, :, None]).astype(jnp.bfloat16)
    closing = contract("ocak,ckbm->oabm", matrix, sectioned)
    return closing.reshape(2, N, batch_size)


def row_sections(contrast, first):
    batch_size = contrast.shape[0]
    shaped = contrast.T.reshape(RADIX, RADIX, batch_size)
    matrix = fourier_tables(RADIX, -1.0)
    cosine_part, sine_part = twiddle_table(RADIX, -1.0)
    part = functools.partial(lax.dynamic_slice_in_dim, start_index=first, slice_size=16)
    opening = contract("oka,abm->okbm", part(matrix[:, 0], axis=1), shaped)
    cosine_part, sine_part = part(cosine_part, axis=0), part(sine_part, axis=0)
    sectioned = rotate(opening, cosine_part[:, :, None], sine_part[:, :, None]).astype(jnp.bfloat16)
    closing = contract("ocjb,ckbm->komj", matrix, sectioned).astype(jnp.bfloat16)
    paired = closing.reshape(8, 2, 2, batch_size, RADIX)
    return paired.transpose(0, 2, 3, 1, 4).reshape(8, 2, batch_size, 2 * RADIX)


def place():
    return {name: lax.axis_index(name) for name in AXES}


def remote(source, target, send_sem, recv_sem, device):
    return pltpu.make_async_remote_copy(
        src_ref=source,
        dst_ref=target,
        send_sem=send_sem,
        recv_sem=recv_sem,
        device_id=device,
        device_id_type=MESH,
    )


def greet(sources, count):
    barrier = pltpu.get_barrier_semaphore()
    for device in sources:
        pl.semaphore_signal(barrier, inc=1, device_id=device, device_id_type=MESH)
    pl.semaphore_wait(barrier, count)


def call(kernel, name, number, out_shapes, scratch, args, vmem=None):
    params = {"vmem_limit_bytes": vmem} if vmem else {}
    if number is not None:
        params |= {"collective_id": number, "has_side_effects": True}
    return pl.pallas_call(
        kernel,
        name=name,
        out_shape=out_shapes,
        in_specs=[pl.BlockSpec(memory_space=pltpu.VMEM)] * len(args),
        out_specs=jax.tree.map(lambda _: pl.BlockSpec(memory_space=pltpu.VMEM), out_shapes),
        scratch_shapes=scratch,
        compiler_params=pltpu.CompilerParams(**params),
    )(*args)


def propagate_kernel(sections, columns, k_real, k_imag, send_sem, recv_sem, own_sem):
    at = place()
    x, yc, z = at["x"], at["y"] * 2 + at["c"], at["zh"] * 4 + at["zl"]
    slab = at["zl"] * 8 + yc

    def device(step, turn):
        to, layer = lax.rem(yc + step + 8, 8), lax.rem(z + turn + 16, 16)
        return {
            "zh": layer // 4,
            "x": x,
            "zl": lax.rem(layer, 4),
            "y": to // 2,
            "c": lax.rem(to, 2),
        }

    moves = []
    for turn in (2, 1, -1, 0):
        for step in range(8):
            if (step, turn) != (0, 0):
                moves.append((step, -2 if turn == 2 and step >= 4 else turn))
    greet([device(-step, -turn) for step, turn in moves], len(moves))
    mine = columns.at[:, pl.ds(slab * 128, 128), :]
    copies = []
    for index, (step, turn) in enumerate(moves):
        copies.append(
            remote(
                sections.at[lax.rem(yc + step, 8)],
                mine,
                send_sem.at[index],
                recv_sem.at[slab],
                device(step, turn),
            )
        )
        copies[-1].start()
    own = pltpu.make_async_copy(sections.at[yc], mine, own_sem)
    own.start()

    distance = depth_start + depth_step * z.astype(jnp.float32)
    lane = lax.broadcasted_iota(jnp.int32, (RADIX, 128), 1)
    row = lax.broadcasted_iota(jnp.int32, (RADIX, 128), 0)
    ring = (x * 8 + yc) * 2 + lane // RADIX + RADIX * lax.rem(lane, RADIX)
    ring = jnp.where(ring >= N // 2, ring - N, ring).astype(jnp.float32) / N
    column_part = ring * ring
    base = RADIX * row
    base = jnp.where(base >= N // 2, base - N, base)
    limit = wave_number * wave_number

    def tile(k, carry):
        freq = (base + k).astype(jnp.float32) / N
        radial = freq * freq + column_part
        amplitude = jnp.exp(
            (-2.0 * math.pi * distance) * jnp.sqrt(jnp.maximum(radial - limit, 0.0))
        )
        turns = distance * (jnp.sqrt(jnp.maximum(limit - radial, 0.0)) - wave_number)
        half = (turns - jnp.floor(turns + 0.5)) * math.pi
        square = half * half
        sine, cosine = jnp.full_like(half, 0.0), jnp.full_like(half, 0.0)
        for power in range(6, -1, -1):
            cosine = cosine * square + (-1) ** power / math.factorial(2 * power)
            if power < 6:
                sine = sine * square + (-1) ** power / math.factorial(2 * power + 1)
        sine = sine * half
        k_real[pl.ds(k * RADIX, RADIX), :] = amplitude * (1.0 - 2.0 * sine * sine)
        k_imag[pl.ds(k * RADIX, RADIX), :] = amplitude * (2.0 * sine * cosine)
        return carry

    lax.fori_loop(0, RADIX, tile, 0)

    own.wait()
    for copy in copies:
        copy.wait_send()
    for step, turn in moves:
        origin = lax.rem(lax.rem(z - turn + 16, 16), 4) * 8 + lax.rem(yc - step + 8, 8)
        slot = columns.at[:, pl.ds(origin * 128, 128), :]
        remote(slot, slot, own_sem, recv_sem.at[origin], device(-step, -turn)).wait_recv()


def layer_kernel(halfway, gathered, send_sem, recv_sem, own_sem):
    at = place()
    me = at["x"] * 8 + at["y"] * 2 + at["c"]

    def device(other):
        return {
            "zh": at["zh"],
            "x": other // 8,
            "zl": at["zl"],
            "y": lax.rem(other // 2, 4),
            "c": lax.rem(other, 2),
        }

    others = [lax.rem(me + step, 32) for step in range(1, 32)]
    greet([device(other) for other in others], 31)
    copies = []
    for other in others:
        copies.append(
            remote(
                halfway.at[:, :, lax.rem(other, 8), other // 8],
                gathered.at[me],
                send_sem.at[other],
                recv_sem.at[me],
                device(other),
            )
        )
        copies[-1].start()
    own = pltpu.make_async_copy(
        halfway.at[:, :, lax.rem(me, 8), me // 8], gathered.at[me], own_sem
    )
    own.start()
    own.wait()
    for copy in copies:
        copy.wait_send()
    for other in others:
        slot = gathered.at[other]
        remote(slot, slot, own_sem, recv_sem.at[other], device(other)).wait_recv()


def inverse_rows_kernel(gathered, first, second, cosines, sines, eye, out, middle, turned):
    def opening(s, carry):
        data = jnp.concatenate([gathered[s, 0], gathered[s, 1]], axis=1)
        made = lax.dot_general(
            first[...], data, (((1,), (1,)), ((), ())), preferred_element_type=jnp.float32
        )
        real, imag = made[:128], made[128:]
        cosine_part, sine_part = cosines[s], sines[s]
        parts = (
            real * cosine_part - imag * sine_part,
            real * sine_part + imag * cosine_part,
        )
        for which, part in enumerate(parts):
            for half in range(2):
                middle[pl.ds(which * RADIX + 2 * s + half, RADIX, stride=128), :] = part[
                    half * RADIX : (half + 1) * RADIX
                ]
        return carry

    lax.fori_loop(0, 32, opening, 0)

    def closing(b, carry):
        block = middle[pl.ds(b * 128, 128), :].astype(jnp.bfloat16)
        made = jnp.dot(second[...], block, preferred_element_type=jnp.float32)
        real, imag = made[:RADIX], made[RADIX:]
        turned[pl.ds(b, RADIX, stride=RADIX), :] = real * real + imag * imag
        return carry

    lax.fori_loop(0, RADIX, closing, 0)

    for t in range(32):
        block = turned[t * 128 : (t + 1) * 128, :].astype(jnp.bfloat16)
        made = lax.dot_general(
            eye[...], block, (((1,), (1,)), ((), ())), preferred_element_type=jnp.float32
        )
        out[:, :, t * 128 : (t + 1) * 128] = made.reshape(16, 8, 128).astype(jnp.bfloat16)


def depth_kernel(planes, stack, send_sem, recv_sem, own_sem):
    at = place()
    z = at["zh"] * 4 + at["zl"]

    def device(layer):
        return {**at, "zh": layer // 4, "zl": lax.rem(layer, 4)}

    def piece(layer):
        return planes.at[lax.rem(layer, 4) * 4 + layer // 4]

    others = [lax.rem(z + step, 16) for step in (8, 7, 9, 6, 10, 5, 11, 4, 12, 3, 13, 2, 14, 1, 15)]
    greet([device(other) for other in others], 15)
    copies = []
    for other in others:
        copies.append(
            remote(
                piece(other), stack.at[z], send_sem.at[other], recv_sem.at[z], device(other)
            )
        )
        copies[-1].start()
    own = pltpu.make_async_copy(piece(z), stack.at[z], own_sem)
    own.start()
    own.wait()
    for copy in copies:
        copy.wait_send()
    for other in others:
        slot = stack.at[other]
        remote(slot, slot, own_sem, recv_sem.at[other], device(other)).wait_recv()


def edge_kernel(low, high, north, south, send_sem, recv_sem):
    at = place()
    q = (((at["zl"] * 4 + at["y"]) * 2 + at["c"]) * 4 + at["x"]) * 4 + at["zh"]

    def device(other):
        return {
            "zh": lax.rem(other, 4),
            "x": lax.rem(other // 4, 4),
            "zl": other // 128,
            "y": lax.rem(other // 32, 4),
            "c": lax.rem(other // 16, 2),
        }

    ahead, behind = device(lax.rem(q + 1, 512)), device(lax.rem(q + 511, 512))
    greet([ahead, behind], 2)
    copies = [
        remote(high, north, send_sem.at[0], recv_sem.at[0], ahead),
        remote(low, south, send_sem.at[1], recv_sem.at[1], behind),
    ]
    for copy in copies:
        copy.start()
    for copy in copies:
        copy.wait()


def spread_kernel(piece, out, send_sem, recv_sem, own_sem):
    at = place()
    x, zh = at["x"], at["zh"]

    def across(step):
        return {**at, "x": lax.rem(x + step + 4, 4)}

    def along(step):
        return {**at, "zh": lax.rem(zh + step + 4, 4)}

    greet([across(s) for s in (1, 2, 3)] + [along(s) for s in (1, 2, 3)], 6)
    copies = []

    def send(source, level, device):
        copies.append(
            remote(
                source,
                out.at[x, level],
                send_sem.at[len(copies)],
                recv_sem.at[x, level],
                device,
            )
        )
        copies[-1].start()

    for step in (2, 1, 3):
        send(piece, zh, along(step))
    for step in (2, 1, 3):
        send(piece, zh, across(step))
    own = pltpu.make_async_copy(piece, out.at[x, zh], own_sem)
    own.start()
    for step in (1, 3, 2):
        level = lax.rem(zh + step, 4)
        slot = out.at[x, level]
        remote(slot, slot, own_sem, recv_sem.at[x, level], along(step)).wait_recv()
        for turn in (2, 1, 3):
            send(slot, level, across(turn))
    own.wait()
    for step in (1, 2, 3):
        for level in range(4):
            slot = out.at[lax.rem(x + step, 4), level]
            remote(
                slot, slot, own_sem, recv_sem.at[lax.rem(x + step, 4), level], across(step)
            ).wait_recv()
    for copy in copies:
        copy.wait_send()


def scores_of(stack, north, south):
    centre = stack.astype(jnp.float32)
    lower = jnp.concatenate([centre[:1], centre[:-1]], axis=0)
    upper = jnp.concatenate([centre[1:], centre[-1:]], axis=0)
    above = jnp.concatenate([north[:, None].astype(jnp.float32), centre[:, :-1]], axis=1)
    below = jnp.concatenate([centre[:, 1:], south[:, None].astype(jnp.float32)], axis=1)
    east = jnp.concatenate([centre[..., 1:], centre[..., -1:]], axis=-1)
    west = jnp.concatenate([centre[..., :1], centre[..., :-1]], axis=-1)
    depth_diff, row_diff, col_diff = upper - lower, below - above, east - west
    scores = (depth_diff * depth_diff + row_diff * row_diff + col_diff * col_diff) / 8.0
    return jnp.max(scores, axis=0)


def inverse_row_tables():
    matrix = fourier_tables(RADIX, 1.0)
    pair = jnp.eye(2, dtype=jnp.bfloat16)
    first = jnp.einsum("ocbj,kl->okbclj", matrix, pair).reshape(256, 256)
    second = jnp.einsum("ocak->oack", matrix).reshape(128, 128)
    cosine_part, sine_part = twiddle_table(RADIX, 1.0)
    wide = lambda part: jnp.broadcast_to(part.reshape(32, 128, 1), (32, 128, 128))
    return first, second, wide(cosine_part), wide(sine_part), jnp.eye(128, dtype=jnp.bfloat16)


def shards(hologram, background):
    at = place()
    bf16, f32 = jnp.bfloat16, jnp.float32
    shape = jax.ShapeDtypeStruct
    dma = pltpu.SemaphoreType.DMA
    contrast = (hologram.astype(f32) / background.astype(f32) - 1.0).astype(bf16)
    sections = row_sections(contrast, at["x"] * 16)
    columns, k_real, k_imag = call(
        propagate_kernel,
        "columns",
        0,
        (shape((2, N, 128), bf16), shape((N, 128), f32), shape((N, 128), f32)),
        [dma((31,)), dma((32,)), dma],
        (sections,),
    )
    spectrum = forward_first(columns)
    propagated = rotate(spectrum.astype(f32), k_real, k_imag).astype(bf16)
    halfway = inverse_first(propagated).astype(bf16)
    gathered = call(
        layer_kernel,
        "layer",
        1,
        shape((32, 2, 4, 32, 128), bf16),
        [dma((32,)), dma((32,)), dma],
        (halfway.reshape(2, 4, 8, 4, 32, 128),),
    )
    planes = call(
        inverse_rows_kernel,
        "rows",
        None,
        shape((16, 8, N), bf16),
        [pltpu.VMEM((RADIX * 128, 128), f32), pltpu.VMEM((N, 128), f32)],
        (gathered.reshape(32, 2, 128, 128), *inverse_row_tables()),
        48 << 20,
    )
    stack = call(
        depth_kernel,
        "depth",
        2,
        shape((PLANES, 8, N), bf16),
        [dma((16,)), dma((16,)), dma],
        (planes,),
    )
    north, south = call(
        edge_kernel,
        "edges",
        3,
        (shape((PLANES, N), bf16), shape((PLANES, N), bf16)),
        [dma((2,)), dma((2,))],
        (stack[:, 0], stack[:, 7]),
    )
    q = (((at["zl"] * 4 + at["y"]) * 2 + at["c"]) * 4 + at["x"]) * 4 + at["zh"]
    north = jnp.where(q == 0, stack[:, 0], north)
    south = jnp.where(q == 511, stack[:, 7], south)
    sharpest = scores_of(stack, north, south).astype(bf16)
    merged = call(
        spread_kernel,
        "spread",
        4,
        shape((4, 4, 8, N), bf16),
        [dma((15,)), dma((4, 4)), dma],
        (sharpest,),
    )
    return merged.reshape(128, N).astype(f32)


def solution(mesh):
    fine = Mesh(mesh.devices.reshape(SIZES), AXES)
    spec = P(("zl", "y", "c"), None)
    return jax.shard_map(
        shards, mesh=fine, in_specs=(spec, spec), out_specs=spec, check_vma=False
    )
```

```python
import functools
import math

import jax
import jax.numpy as jnp
import numpy as np
from jax import lax
from jax.experimental import pallas as pl
from jax.experimental.pallas import tpu as pltpu
from jax.sharding import Mesh
from jax.sharding import PartitionSpec as P

N = 4096
RADIX = 64
PLANES = 16
AXES = ("zh", "x", "zl", "y", "c")
SIZES = (4, 4, 4, 4, 2)
MESH = pl.DeviceIdType.MESH
NT = (((1,), (1,)), ((), ()))
F32 = jnp.float32
BF16 = jnp.bfloat16

wave_number = 0.6
depth_start = 8.0
depth_step = 2.0


def fourier_tables(sign_value):
    indices = np.arange(RADIX)
    angles = (indices[:, None] * indices[None, :] % RADIX) * (sign_value * 2.0 * math.pi / RADIX)
    real, imag = np.cos(angles) / math.sqrt(RADIX), np.sin(angles) / math.sqrt(RADIX)
    matrix = np.stack([np.stack([real, -imag]), np.stack([imag, real])])
    return matrix.astype(np.float32)


def twiddle_table(sign_value):
    indices = np.arange(RADIX)
    angles = (indices[:, None] * indices[None, :]) * (sign_value * 2.0 * math.pi / N)
    return np.cos(angles).astype(np.float32), np.sin(angles).astype(np.float32)


def pass_tables():
    ahead, back = fourier_tables(-1.0), fourier_tables(1.0)
    flat = lambda table: table.transpose(0, 2, 1, 3).reshape(128, 128)
    both = np.zeros((2, 2, 2, RADIX, 2, 128), np.float32)
    for lane in range(128):
        far, j = divmod(lane, RADIX)
        both[1, :, far, :, :, lane] = back[:, :, :, RADIX - 1 - j if far else j].transpose(0, 2, 1)
        if j >= RADIX // 2:
            half, j = 1, (95 - j if far else j - 32)
        else:
            half, j = 0, ((RADIX - j if j else 32) if far else j)
        both[0, :, half, :, :, lane] = back[:, :, :, j].transpose(0, 2, 1)
    tables = (
        ahead[:, 0].reshape(128, RADIX),
        flat(ahead),
        flat(back),
        both.reshape(2, 256, 256),
        np.eye(128, dtype=np.float32),
    )
    return [jnp.asarray(table, BF16) for table in tables]


def row_sections(contrast, x):
    batch_size = contrast.shape[0]
    shaped = contrast.T.reshape(RADIX, RADIX, batch_size)
    matrix = jnp.asarray(fourier_tables(-1.0), BF16)
    cosine_part, sine_part = (jnp.asarray(part) for part in twiddle_table(-1.0))

    def part(table, axis):
        own = lax.dynamic_slice_in_dim(table, x * 8, 8, axis=axis)
        return jnp.concatenate([own, lax.slice_in_dim(table, 32, 33, axis=axis)], axis=axis)

    contract = functools.partial(jnp.einsum, preferred_element_type=F32)
    opening = contract("oka,abm->okbm", part(matrix[:, 0], 1), shaped)
    cosine_part, sine_part = part(cosine_part, 0)[:, :, None], part(sine_part, 0)[:, :, None]
    sectioned = jnp.stack(
        [
            opening[0] * cosine_part - opening[1] * sine_part,
            opening[0] * sine_part + opening[1] * cosine_part,
        ]
    ).astype(BF16)
    closing = contract("ocjb,ckbm->kmoj", matrix, sectioned).astype(BF16)
    zero, middle = closing[0], closing[8]
    packed = jnp.concatenate(
        [
            jnp.stack([zero[:, 0, :1], zero[:, 0, 32:33]], axis=1),
            zero[:, :, 1:32],
            middle[:, :, :32],
        ],
        axis=2,
    )
    chosen = jnp.where(x == 0, packed, zero)
    return jnp.concatenate([chosen[None], closing[1:8]]).reshape(8, batch_size, 128)


def remote(source, target, send_sem, recv_sem, device):
    return pltpu.make_async_remote_copy(
        src_ref=source,
        dst_ref=target,
        send_sem=send_sem,
        recv_sem=recv_sem,
        device_id=device,
        device_id_type=MESH,
    )


def sine_cosine(turns):
    half = (turns - jnp.floor(turns + 0.5)) * math.pi
    square = half * half
    sine, cosine = jnp.zeros_like(half), jnp.zeros_like(half)
    for power in range(6, -1, -1):
        cosine = cosine * square + (-1) ** power / math.factorial(2 * power)
        if power < 6:
            sine = sine * square + (-1) ** power / math.factorial(2 * power + 1)
    sine = sine * half
    return 2.0 * sine * cosine, 1.0 - 2.0 * sine * sine


def make_tables(me, z, cosines, sines, k_real, k_imag):
    distance = depth_start + depth_step * z.astype(F32)
    lane = lax.broadcasted_iota(jnp.int32, (RADIX, 128), 1)
    row = lax.broadcasted_iota(jnp.int32, (RADIX, 128), 0)
    j = lax.rem(lane, RADIX)
    general = me + RADIX * j
    lone = jnp.where(j == 0, jnp.where(lane >= RADIX, N // 2, 0), RADIX * j)
    lone = jnp.where(j >= RADIX // 2, 32 + RADIX * (j - RADIX // 2), lone)
    natural = jnp.where(me == 0, lone, general)
    freq = jnp.where(natural >= N // 2, natural - N, natural).astype(F32) / N
    column_part = freq * freq
    base = jnp.where(row >= RADIX // 2, RADIX * row - N, RADIX * row)
    limit = wave_number * wave_number

    def tile(k, carry):
        here = pl.ds(k * RADIX, RADIX)
        sine, cosine = sine_cosine((row * k).astype(F32) / N)
        cosines[k], sines[k] = cosine, sine
        freq = (base + k).astype(F32) / N
        radial = freq * freq + column_part
        amplitude = jnp.exp(
            (-2.0 * math.pi * distance) * jnp.sqrt(jnp.maximum(radial - limit, 0.0))
        )
        turns = distance * (jnp.sqrt(jnp.maximum(limit - radial, 0.0)) - wave_number)
        sine, cosine = sine_cosine(turns)
        k_real[here, :] = amplitude * cosine
        k_imag[here, :] = amplitude * sine
        return carry

    lax.fori_loop(0, RADIX, tile, 0)


def matmul(matrix, data):
    return jnp.dot(matrix[...], data, preferred_element_type=F32)


def column_pass(me, tables, wide, middle, other, k_real, k_imag, cosines, sines):
    open_ahead, ahead, back = tables
    lane = lax.broadcasted_iota(jnp.int32, (RADIX, 128), 1)
    low = lane < RADIX
    alone = (me == 0) & (lax.rem(lane, RADIX) == 0)

    def first(b, carry):
        made = matmul(open_ahead, wide[pl.ds(b, RADIX, stride=RADIX), :].astype(BF16))
        real, imag = made[:RADIX], made[RADIX:]
        cosine, sine = cosines[b], sines[b]
        middle[pl.ds(b, RADIX, stride=128), :] = real * cosine + imag * sine
        middle[pl.ds(RADIX + b, RADIX, stride=128), :] = imag * cosine - real * sine
        return carry

    lax.fori_loop(0, RADIX, first, 0, unroll=8)

    def second(k, carry):
        made = matmul(ahead, middle[pl.ds(k * 128, 128), :].astype(BF16))
        real, imag = made[:RADIX], made[RADIX:]
        real_turn, imag_turn = pltpu.roll(real, RADIX, 1), pltpu.roll(imag, RADIX, 1)
        spectrum_real = jnp.where(low, real - imag_turn, real_turn + imag)
        spectrum_imag = jnp.where(low, imag + real_turn, imag_turn - real)
        spectrum_real = jnp.where(alone, real, spectrum_real).astype(BF16).astype(F32)
        spectrum_imag = jnp.where(alone, imag, spectrum_imag).astype(BF16).astype(F32)
        here = pl.ds(k * RADIX, RADIX)
        kernel_real, kernel_imag = k_real[here, :], k_imag[here, :]
        propagated = jnp.concatenate(
            [
                spectrum_real * kernel_real - spectrum_imag * kernel_imag,
                spectrum_real * kernel_imag + spectrum_imag * kernel_real,
            ]
        )
        made = matmul(back, propagated.astype(BF16))
        real, imag = made[:RADIX], made[RADIX:]
        cosine, sine = cosines[k], sines[k]
        other[pl.ds(k, RADIX, stride=128), :] = real * cosine - imag * sine
        other[pl.ds(RADIX + k, RADIX, stride=128), :] = real * sine + imag * cosine
        return carry

    lax.fori_loop(0, RADIX, second, 0, unroll=8)

    def third(b, carry):
        made = matmul(back, other[pl.ds(b * 128, 128), :].astype(BF16))
        middle[pl.ds(b, RADIX, stride=RADIX), :] = made[:RADIX]
        middle[pl.ds(N + b, RADIX, stride=RADIX), :] = made[RADIX:]
        return carry

    lax.fori_loop(0, RADIX, third, 0, unroll=8)


def pack_blocks(middle, blocks):
    def one(yc, carry):
        for part in range(2):
            for slab in range(4):
                start = part * N + slab * 1024 + yc * 128
                for x in range(4):
                    rows = [
                        middle[pl.ds(start + zh * 32 + (x - slab) % 4 * 8, 8), :]
                        for zh in range(4)
                    ]
                    blocks[x * 8 + yc, part, slab] = jnp.concatenate(rows).astype(BF16)
        return carry

    lax.fori_loop(0, 8, one, 0)


def open_rows(s, both, gathered, middle, cosines, sines):
    real, imag = (gathered[s, part].reshape(128, 128) for part in range(2))
    which = jnp.minimum(s, 1)
    data = jnp.concatenate([real, imag], axis=1)
    made = lax.dot_general(both[which], data, NT, preferred_element_type=F32)
    for half in range(2):
        k = jnp.where(s == 0, 32, RADIX - s) if half else s
        real = made[half * RADIX : (half + 1) * RADIX]
        imag = made[128 + half * RADIX : 128 + (half + 1) * RADIX]
        cosine, sine = cosines[k], sines[k]
        middle[pl.ds(k, RADIX, stride=128), :] = real * cosine - imag * sine
        middle[pl.ds(RADIX + k, RADIX, stride=128), :] = real * sine + imag * cosine


def close_rows(back, eye, middle, wide, planes):
    def closing(b, carry):
        made = matmul(back, middle[pl.ds(b * 128, 128), :].astype(BF16))
        real, imag = made[:RADIX], made[RADIX:]
        wide[pl.ds(b, RADIX, stride=RADIX), :] = real * real + imag * imag
        return carry

    lax.fori_loop(0, RADIX, closing, 0, unroll=8)
    for t in range(32):
        block = wide[t * 128 : (t + 1) * 128, :].astype(BF16)
        made = lax.dot_general(eye[...], block, NT, preferred_element_type=F32)
        planes[:, :, t * 128 : (t + 1) * 128] = made.reshape(16, 8, 128).astype(BF16)


def edge_rows(stack, low, high):
    rows = lax.broadcasted_iota(jnp.int32, (PLANES, N), 0)
    bottom, top = jnp.zeros((PLANES, N), F32), jnp.zeros((PLANES, N), F32)
    for g in range(PLANES):
        plane = stack[g].astype(F32)
        bottom = jnp.where(rows == g, plane[0:1], bottom)
        top = jnp.where(rows == g, plane[7:8], top)
    low[...] = bottom.astype(BF16)
    high[...] = top.astype(BF16)


def inner_scores(stack, scores):
    lane = lax.broadcasted_iota(jnp.int32, (8, N), 1)

    def one(g, carry):
        centre = stack[g].astype(F32)
        lower = stack[jnp.maximum(g - 1, 0)].astype(F32)
        upper = stack[jnp.minimum(g + 1, PLANES - 1)].astype(F32)
        east = jnp.where(lane == N - 1, centre, pltpu.roll(centre, N - 1, 1))
        west = jnp.where(lane == 0, centre, pltpu.roll(centre, 1, 1))
        scores[g] = (upper - lower) * (upper - lower) + (east - west) * (east - west)
        return carry

    lax.fori_loop(0, PLANES, one, 0)


def full_scores(stack, scores, north, south, first, last, piece):
    row = lax.broadcasted_iota(jnp.int32, (8, N), 0)
    best = jnp.zeros((8, N), F32)
    norths, souths = north[...].astype(F32), south[...].astype(F32)
    for g in range(PLANES):
        centre = stack[g].astype(F32)
        before = jnp.where(first, centre[0:1], norths[g : g + 1])
        after = jnp.where(last, centre[7:8], souths[g : g + 1])
        above = jnp.where(row == 0, before, pltpu.roll(centre, 1, 0))
        below = jnp.where(row == 7, after, pltpu.roll(centre, 7, 0))
        best = jnp.maximum(best, (scores[g] + (below - above) * (below - above)) / 8.0)
    piece[...] = best.astype(BF16)


def whole_kernel(
    sections, open_ahead, ahead, back, both, eye, out,
    columns, wide, middle, other, cosines, sines, k_real, k_imag,
    blocks, staged, gathered, planes, stack, scores, low, high, north, south, piece,
    send1, recv1, send2, recv2, relay_send, relay_recv, send3, recv3, send4, recv4,
    send5, recv5, own_sem,
):
    at = {name: lax.axis_index(name) for name in AXES}
    x, y, c, zh, zl = at["x"], at["y"], at["c"], at["zh"], at["zl"]
    yc, z = y * 2 + c, zh * 4 + zl
    me, slab = x * 8 + yc, zl * 8 + yc
    xs = lax.rem(x - zl + 4, 4)
    q = (slab * 4 + zh) * 4 + xs

    def near(step, turn):
        to, layer = lax.rem(yc + step + 8, 8), lax.rem(z + turn + 16, 16)
        return {
            "zh": layer // 4,
            "x": x,
            "zl": lax.rem(layer, 4),
            "y": to // 2,
            "c": lax.rem(to, 2),
        }

    def level(dx, dy, dc):
        return {
            "zh": zh,
            "x": lax.rem(x + dx + 4, 4),
            "zl": zl,
            "y": lax.rem(y + dy + 4, 4),
            "c": lax.rem(c + dc, 2),
        }

    def number(device):
        return device["x"] * 8 + device["y"] * 2 + device["c"]

    def above(layer):
        return {**at, "zh": layer // 4, "zl": lax.rem(layer, 4)}

    def block_owner(index):
        owner = index // 16
        low_z = owner // 8
        return {
            "zh": lax.rem(index // 4, 4),
            "x": lax.rem(lax.rem(index, 4) + low_z, 4),
            "zl": low_z,
            "y": lax.rem(owner // 2, 4),
            "c": lax.rem(owner, 2),
        }

    moves = []
    for turn in (2, 1, -1, 0):
        for step in range(8):
            if (step, turn) != (0, 0):
                moves.append((step, -2 if turn == 2 and step >= 4 else turn))
    relayed, direct = [], []
    for dx in (2, 1, 3, 0):
        for dy in (2, 1, 3, 0):
            for dc in (1, 0):
                if 2 in (dx, dy):
                    side = -1 if dc else 1
                    hop = [side if d == 2 else (-1 if d == 3 else d) for d in (dx, dy)]
                    rest = [side if d == 2 else 0 for d in (dx, dy)]
                    relayed.append((hop[0], hop[1], dc, rest[0], rest[1]))
                elif (dx, dy, dc) != (0, 0, 0):
                    direct.append((-1 if dx == 3 else dx, -1 if dy == 3 else dy, dc))
    turns = (8, 7, 9, 6, 10, 5, 11, 4, 12, 3, 13, 2, 14, 1, 15)
    layers = [lax.rem(z + turn, 16) for turn in turns]
    ahead_q, behind_q = block_owner(lax.rem(q + 1, 512)), block_owner(lax.rem(q + 511, 512))

    barrier = pltpu.get_barrier_semaphore()
    everyone = [near(-step, -turn) for step, turn in moves]
    everyone += [level(dx, dy, dc) for dx in range(4) for dy in range(4) for dc in range(2)][1:]
    everyone += [above(layer) for layer in layers]
    everyone += [ahead_q, behind_q]
    for device in everyone:
        pl.semaphore_signal(barrier, inc=1, device_id=device, device_id_type=MESH)
    pl.semaphore_wait(barrier, len(everyone))

    sent = []
    for index, (step, turn) in enumerate(moves):
        sent.append(
            remote(
                sections.at[lax.rem(yc + step, 8)],
                columns.at[slab],
                send1.at[index],
                recv1.at[slab],
                near(step, turn),
            )
        )
        sent[-1].start()
    own = pltpu.make_async_copy(sections.at[yc], columns.at[slab], own_sem)
    own.start()
    make_tables(me, z, cosines, sines, k_real, k_imag)
    own.wait()
    wide[pl.ds(slab * 128, 128), :] = columns[slab].astype(F32)
    for copy in sent:
        copy.wait_send()
    for step, turn in reversed(moves):
        origin = lax.rem(lax.rem(z - turn + 16, 16), 4) * 8 + lax.rem(yc - step + 8, 8)
        slot = columns.at[origin]
        remote(slot, slot, own_sem, recv1.at[origin], near(-step, -turn)).wait_recv()
        wide[pl.ds(origin * 128, 128), :] = columns[origin].astype(F32)

    tables = (open_ahead, ahead, back)
    column_pass(me, tables, wide, middle, other, k_real, k_imag, cosines, sines)
    pack_blocks(middle, blocks)

    sent = []
    for index, (hx, hy, dc, rx, ry) in enumerate(relayed):
        target = number(level(hx + rx, hy + ry, dc))
        sent.append(
            remote(
                blocks.at[target],
                staged.at[index],
                relay_send.at[index],
                relay_recv.at[index],
                level(hx, hy, dc),
            )
        )
        sent[-1].start()
    for index, (dx, dy, dc) in enumerate(direct):
        device = level(dx, dy, dc)
        sent.append(
            remote(
                blocks.at[number(device)],
                gathered.at[me],
                send2.at[index],
                recv2.at[me],
                device,
            )
        )
        sent[-1].start()
    own = pltpu.make_async_copy(blocks.at[me], gathered.at[me], own_sem)
    own.start()
    own.wait()
    open_rows(me, both, gathered, middle, cosines, sines)
    for index, (hx, hy, dc, rx, ry) in enumerate(relayed):
        source = level(-hx, -hy, dc)
        slot = staged.at[index]
        remote(slot, slot, own_sem, relay_recv.at[index], source).wait_recv()
        sent.append(
            remote(
                slot,
                gathered.at[number(source)],
                send2.at[len(direct) + index],
                recv2.at[number(source)],
                level(rx, ry, 0),
            )
        )
        sent[-1].start()

    arrivals = [(-dx, -dy, dc) for dx, dy, dc in direct]
    arrivals += [(-hx - rx, -hy - ry, dc) for hx, hy, dc, rx, ry in relayed]
    for dx, dy, dc in arrivals:
        device = level(dx, dy, dc)
        source = number(device)
        slot = gathered.at[source]
        remote(slot, slot, own_sem, recv2.at[source], device).wait_recv()
        open_rows(source, both, gathered, middle, cosines, sines)
    for copy in sent:
        copy.wait_send()
    close_rows(back, eye, middle, wide, planes)

    def part(layer):
        return planes.at[lax.rem(layer, 4) * 4 + layer // 4]

    sent = []
    for index, layer in enumerate(layers):
        sent.append(
            remote(part(layer), stack.at[z], send3.at[index], recv3.at[z], above(layer))
        )
        sent[-1].start()
    own = pltpu.make_async_copy(part(z), stack.at[z], own_sem)
    own.start()
    own.wait()
    for copy in sent:
        copy.wait_send()
    for layer in layers:
        slot = stack.at[layer]
        remote(slot, slot, own_sem, recv3.at[layer], above(layer)).wait_recv()

    edge_rows(stack, low, high)
    sent = [
        remote(high, north, send4.at[0], recv4.at[0], ahead_q),
        remote(low, south, send4.at[1], recv4.at[1], behind_q),
    ]
    for copy in sent:
        copy.start()
    inner_scores(stack, scores)
    for copy in sent:
        copy.wait()
    full_scores(stack, scores, north, south, q == 0, q == 511, piece)

    left, right = pl.ds(0, N // 2), pl.ds(N // 2, N // 2)
    halves = (left, right)
    sent = []

    def across(step):
        return {**at, "x": lax.rem(x + step + 4, 4)}

    def along(step):
        return {**at, "zh": lax.rem(zh + step + 4, 4)}

    def row_of(place):
        return lax.rem(place - zl + 4, 4)

    def send(source, target, sem, device):
        sent.append(remote(source, target, send5.at[len(sent)], sem, device))
        sent[-1].start()

    def arrive(place, high_z, half, device):
        slot = out.at[high_z, row_of(place)]
        slot = slot if half is None else slot.at[:, halves[half]]
        sem = recv5.at[place, high_z, half or 0]
        remote(slot, slot, own_sem, sem, device).wait_recv()

    for step in (1, -1):
        send(piece, out.at[zh, xs], recv5.at[x, zh, 0], along(step))
    for step in (1, -1):
        send(piece, out.at[zh, xs], recv5.at[x, zh, 0], across(step))
    own = pltpu.make_async_copy(piece, out.at[zh, xs], own_sem)
    own.start()
    for half, step in enumerate((1, -1)):
        from_z = lax.rem(zh - step + 4, 4)
        arrive(x, from_z, None, along(-step))
        slot = out.at[from_z, xs, :, halves[half]]
        send(slot, slot, recv5.at[x, from_z, half], along(step))
        for turn in (1, -1):
            slot = out.at[from_z, xs]
            send(slot, slot, recv5.at[x, from_z, 0], across(turn))
    far_z = lax.rem(zh + 2, 4)
    for high_z in (zh, lax.rem(zh + 3, 4), lax.rem(zh + 1, 4), far_z):
        if high_z is far_z:
            for half, step in enumerate((1, -1)):
                arrive(x, far_z, half, along(-step))
            for turn in (1, -1):
                slot = out.at[far_z, xs]
                send(slot, slot, recv5.at[x, far_z, 0], across(turn))
        for half, step in enumerate((1, -1)):
            place = lax.rem(x - step + 4, 4)
            arrive(place, high_z, None, across(-step))
            slot = out.at[high_z, row_of(place), :, halves[half]]
            send(slot, slot, recv5.at[place, high_z, half], across(step))
    for high_z in (zh, lax.rem(zh + 3, 4), lax.rem(zh + 1, 4), far_z):
        for half, step in enumerate((1, -1)):
            arrive(lax.rem(x + 2, 4), high_z, half, across(-step))
    own.wait()
    for copy in sent:
        copy.wait_send()


def shards(hologram, background):
    contrast = (hologram.astype(F32) / background.astype(F32) - 1.0).astype(BF16)
    sections = row_sections(contrast, lax.axis_index("x"))
    vmem, dma = pltpu.VMEM, pltpu.SemaphoreType.DMA
    table = vmem((RADIX, RADIX, 128), F32)
    merged = pl.pallas_call(
        whole_kernel,
        name="whole",
        out_shape=jax.ShapeDtypeStruct((4, 4, 8, N), BF16),
        in_specs=[pl.BlockSpec(memory_space=vmem)] * 6,
        out_specs=pl.BlockSpec(memory_space=vmem),
        scratch_shapes=[
            vmem((32, 128, 128), BF16),
            vmem((N, 128), F32),
            vmem((2 * N, 128), F32),
            vmem((2 * N, 128), F32),
            table,
            table,
            vmem((N, 128), F32),
            vmem((N, 128), F32),
            vmem((32, 2, 4, 32, 128), BF16),
            vmem((14, 2, 4, 32, 128), BF16),
            vmem((32, 2, 4, 32, 128), BF16),
            vmem((16, 8, N), BF16),
            vmem((PLANES, 8, N), BF16),
            vmem((PLANES, 8, N), F32),
            *[vmem((PLANES, N), BF16)] * 4,
            vmem((8, N), BF16),
            dma((31,)),
            dma((32,)),
            dma((31,)),
            dma((32,)),
            dma((14,)),
            dma((14,)),
            dma((15,)),
            dma((16,)),
            dma((2,)),
            dma((2,)),
            dma((20,)),
            dma((4, 4, 2)),
            dma,
        ],
        compiler_params=pltpu.CompilerParams(
            collective_id=0, has_side_effects=True, vmem_limit_bytes=56 << 20
        ),
    )(sections, *pass_tables())
    return merged.reshape(128, N).astype(F32)


def solution(mesh):
    fine = Mesh(mesh.devices.reshape(SIZES), AXES)
    spec = P(("zl", "y", "c"), None)
    return jax.shard_map(
        shards, mesh=fine, in_specs=(spec, spec), out_specs=spec, check_vma=False
    )
```

```python
import math

import jax
import jax.numpy as jnp
import numpy as np
from jax import lax
from jax.experimental import pallas as pl
from jax.experimental.pallas import tpu as pltpu
from jax.sharding import Mesh
from jax.sharding import PartitionSpec as P

N = 4096
RADIX = 64
PLANES = 16
WIDE = 72
DEEP = 136
HALF = N // 2
AXES = ("zh", "x", "zl", "y", "c")
SIZES = (4, 4, 4, 4, 2)
MESH = pl.DeviceIdType.MESH
NT = (((1,), (1,)), ((), ()))
F32 = jnp.float32
BF16 = jnp.bfloat16

wave_number = 0.6
depth_start = 8.0
depth_step = 2.0


def fourier_tables(sign_value):
    indices = np.arange(RADIX)
    angles = (indices[:, None] * indices[None, :] % RADIX) * (sign_value * 2.0 * math.pi / RADIX)
    real, imag = np.cos(angles) / math.sqrt(RADIX), np.sin(angles) / math.sqrt(RADIX)
    matrix = np.stack([np.stack([real, -imag]), np.stack([imag, real])])
    return matrix.astype(np.float32)


def twiddle_table(sign_value):
    indices = np.arange(RADIX)
    angles = (indices[:, None] * indices[None, :]) * (sign_value * 2.0 * math.pi / N)
    return np.cos(angles).astype(np.float32), np.sin(angles).astype(np.float32)


def pass_tables():
    ahead, back = fourier_tables(-1.0), fourier_tables(1.0)
    flat = lambda table: table.transpose(0, 2, 1, 3).reshape(128, 128)
    natural = np.eye(128, dtype=np.float32).reshape(2, 2, 32, 128).swapaxes(0, 1).reshape(128, 128)
    both = np.zeros((2, 2, 2, RADIX, 2, 128), np.float32)
    for lane in range(128):
        far, j = divmod(lane, RADIX)
        both[1, :, far, :, :, lane] = back[:, :, :, RADIX - 1 - j if far else j].transpose(0, 2, 1)
        if j >= RADIX // 2:
            half, j = 1, (95 - j if far else j - 32)
        else:
            half, j = 0, ((RADIX - j if j else 32) if far else j)
        both[0, :, half, :, :, lane] = back[:, :, :, j].transpose(0, 2, 1)
    tables = (
        flat(ahead),
        flat(back),
        both.reshape(2, 256, 256),
        np.eye(128, dtype=np.float32),
        natural,
    )
    return [jnp.asarray(ahead[:, 0].reshape(128, RADIX), F32)] + [
        jnp.asarray(table, BF16) for table in tables
    ]


def row_pass(x, hologram, background, open_exact, ahead, eye, wide, middle, sections):
    for t in range(32):
        here = slice(t * 128, (t + 1) * 128)
        ratio = hologram[:, here].astype(F32) / background[:, here].astype(F32)
        contrast = (ratio - 1.0).astype(BF16)
        made = lax.dot_general(eye[...], contrast, NT, preferred_element_type=F32)
        wide[2 * t * WIDE : 2 * t * WIDE + RADIX, :] = made[:RADIX]
        wide[(2 * t + 1) * WIDE : (2 * t + 1) * WIDE + RADIX, :] = made[RADIX:]
    own = pl.multiple_of(x * 8, 8)
    chosen = [open_exact[pl.ds(own, 8), :], open_exact[32:40, :]]
    chosen += [open_exact[pl.ds(RADIX + own, 8), :], open_exact[RADIX + 32 : RADIX + 40, :]]
    matrix = jnp.concatenate(chosen).astype(BF16)
    row = lax.broadcasted_iota(jnp.int32, (16, 128), 0)
    k = jnp.where(row < 8, x * 8 + row, row + 24).astype(F32)

    def opening(b, carry):
        data = wide[pl.ds(b, RADIX, stride=WIDE), :].astype(BF16)
        made = jnp.dot(matrix, data, preferred_element_type=F32)
        real, imag = made[:16], made[16:]
        sine, cosine = sine_cosine(k * (b.astype(F32) / N))
        middle[pl.ds(b, 16, stride=DEEP), :] = real * cosine + imag * sine
        middle[pl.ds(RADIX + b, 16, stride=DEEP), :] = imag * cosine - real * sine
        return carry

    lax.fori_loop(0, RADIX, opening, 0, unroll=8)

    def section(index):
        made = matmul(ahead, middle[index * DEEP : index * DEEP + 128, :].astype(BF16))
        return lax.dot_general(eye[...], made.astype(BF16), NT, preferred_element_type=F32)

    lane = lax.broadcasted_iota(jnp.int32, (128, 128), 1)
    zero, half = section(0), section(8)
    turned = pltpu.roll(zero, 32, 1)
    packed = jnp.where(lax.rem(lane, RADIX) >= 32, pltpu.roll(half, 32, 1), zero)
    packed = jnp.where(lane == RADIX, turned, packed)
    sections[0] = jnp.where(x == 0, packed, zero).astype(BF16)
    for index in range(1, 8):
        sections[index] = section(index).astype(BF16)


def remote(source, target, send_sem, recv_sem, device):
    return pltpu.make_async_remote_copy(
        src_ref=source,
        dst_ref=target,
        send_sem=send_sem,
        recv_sem=recv_sem,
        device_id=device,
        device_id_type=MESH,
    )


def sine_cosine(turns):
    half = (turns - jnp.floor(turns + 0.5)) * math.pi
    square = half * half
    sine, cosine = jnp.zeros_like(half), jnp.zeros_like(half)
    for power in range(6, -1, -1):
        cosine = cosine * square + (-1) ** power / math.factorial(2 * power)
        if power < 6:
            sine = sine * square + (-1) ** power / math.factorial(2 * power + 1)
    sine = sine * half
    return 2.0 * sine * cosine, 1.0 - 2.0 * sine * sine


def make_tables(me, z, cosines, sines, k_real, k_imag):
    distance = depth_start + depth_step * z.astype(F32)
    lane = lax.broadcasted_iota(jnp.int32, (RADIX, 128), 1)
    row = lax.broadcasted_iota(jnp.int32, (RADIX, 128), 0)
    j = lax.rem(lane, RADIX)
    general = me + RADIX * j
    lone = jnp.where(j == 0, jnp.where(lane >= RADIX, N // 2, 0), RADIX * j)
    lone = jnp.where(j >= RADIX // 2, 32 + RADIX * (j - RADIX // 2), lone)
    natural = jnp.where(me == 0, lone, general)
    freq = jnp.where(natural >= N // 2, natural - N, natural).astype(F32) / N
    column_part = freq * freq
    base = jnp.where(row >= RADIX // 2, RADIX * row - N, RADIX * row)
    limit = wave_number * wave_number

    def tile(k, carry):
        here = pl.ds(k * RADIX, RADIX)
        sine, cosine = sine_cosine((row * k).astype(F32) / N)
        cosines[k], sines[k] = cosine, sine
        freq = (base + k).astype(F32) / N
        radial = freq * freq + column_part
        amplitude = jnp.exp(
            (-2.0 * math.pi * distance) * jnp.sqrt(jnp.maximum(radial - limit, 0.0))
        )
        turns = distance * (jnp.sqrt(jnp.maximum(limit - radial, 0.0)) - wave_number)
        sine, cosine = sine_cosine(turns)
        k_real[here, :] = amplitude * cosine
        k_imag[here, :] = amplitude * sine
        return carry

    lax.fori_loop(0, RADIX, tile, 0)


def widen(slab, columns, wide):
    for half in range(2):
        rows = columns[slab, pl.ds(half * RADIX, RADIX), :]
        wide[pl.ds((2 * slab + half) * WIDE, RADIX), :] = rows.astype(F32)


def matmul(matrix, data):
    return jnp.dot(matrix[...], data, preferred_element_type=F32)


def matmul_right(data, matrix):
    return jnp.dot(data, matrix[...], preferred_element_type=F32)


def column_pass(me, tables, wide, middle, other, k_real, k_imag, cosines, sines):
    open_exact, ahead, back = tables
    lane = lax.broadcasted_iota(jnp.int32, (RADIX, 128), 1)
    low = lane < RADIX
    alone = (me == 0) & (lax.rem(lane, RADIX) == 0)

    open_ahead = open_exact[...].astype(BF16)

    def first(b, carry):
        made = matmul(open_ahead, wide[pl.ds(b, RADIX, stride=WIDE), :].astype(BF16))
        real, imag = made[:RADIX], made[RADIX:]
        cosine, sine = cosines[b], sines[b]
        middle[pl.ds(b, RADIX, stride=DEEP), :] = real * cosine + imag * sine
        middle[pl.ds(RADIX + b, RADIX, stride=DEEP), :] = imag * cosine - real * sine
        return carry

    lax.fori_loop(0, RADIX, first, 0, unroll=8)

    def second(k, carry):
        made = matmul(ahead, middle[pl.ds(k * DEEP, 128), :].astype(BF16))
        real, imag = made[:RADIX], made[RADIX:]
        real_turn, imag_turn = pltpu.roll(real, RADIX, 1), pltpu.roll(imag, RADIX, 1)
        spectrum_real = jnp.where(low, real - imag_turn, real_turn + imag)
        spectrum_imag = jnp.where(low, imag + real_turn, imag_turn - real)
        spectrum_real = jnp.where(alone, real, spectrum_real).astype(BF16).astype(F32)
        spectrum_imag = jnp.where(alone, imag, spectrum_imag).astype(BF16).astype(F32)
        here = pl.ds(k * RADIX, RADIX)
        kernel_real, kernel_imag = k_real[here, :], k_imag[here, :]
        propagated = jnp.concatenate(
            [
                spectrum_real * kernel_real - spectrum_imag * kernel_imag,
                spectrum_real * kernel_imag + spectrum_imag * kernel_real,
            ]
        )
        made = matmul(back, propagated.astype(BF16))
        real, imag = made[:RADIX], made[RADIX:]
        cosine, sine = cosines[k], sines[k]
        other[pl.ds(k, RADIX, stride=DEEP), :] = real * cosine - imag * sine
        other[pl.ds(RADIX + k, RADIX, stride=DEEP), :] = real * sine + imag * cosine
        return carry

    lax.fori_loop(0, RADIX, second, 0, unroll=8)

    def third(b, carry):
        made = matmul(back, other[pl.ds(b * DEEP, 128), :].astype(BF16))
        middle[pl.ds(b, RADIX, stride=WIDE), :] = made[:RADIX]
        middle[pl.ds(RADIX * WIDE + b, RADIX, stride=WIDE), :] = made[RADIX:]
        return carry

    lax.fori_loop(0, RADIX, third, 0, unroll=8)


def block_rows(middle, part, x, yc):
    rows = []
    for low_z in range(4):
        start = (part * RADIX + low_z * 16 + yc * 2) * WIDE + lax.rem(x - low_z + 4, 4) * 8
        for zh in range(4):
            offset = pl.multiple_of(start + zh // 2 * WIDE + zh % 2 * 32, 8)
            rows.append(middle[pl.ds(offset, 8), :])
    return jnp.concatenate(rows).astype(BF16)


def partner(k):
    return jnp.where(k == 0, 32, RADIX - k)


def make_block(me, target, both, middle, cosines, sines, blocks):
    x, yc = target // 8, lax.rem(target, 8)
    data = jnp.concatenate([block_rows(middle, part, x, yc) for part in range(2)], axis=1)
    made = lax.dot_general(both[jnp.minimum(me, 1)], data, NT, preferred_element_type=F32)
    for half in range(2):
        k = partner(me) if half else me
        real = made[half * RADIX : (half + 1) * RADIX]
        imag = made[128 + half * RADIX : 128 + (half + 1) * RADIX]
        cosine, sine = cosines[k], sines[k]
        turned = (real * cosine - imag * sine, real * sine + imag * cosine)
        for part in range(2):
            for chunk in range(2):
                rows = turned[part][chunk * 32 : (chunk + 1) * 32]
                blocks[target, chunk, part * 2 + half] = rows.astype(BF16)


def place_block(source, chunk, gathered, other):
    for part in range(2):
        for half in range(2):
            k = partner(source) if half else source
            rows = gathered[source, chunk, part * 2 + half].astype(F32)
            start = chunk * 32 * DEEP + part * RADIX + k
            other[pl.ds(start, 32, stride=DEEP), :] = rows


def close_rows(chunk, back, eye, other, wide, planes):
    def closing(index, carry):
        b = chunk * 32 + index
        made = matmul(back, other[pl.ds(b * DEEP, 128), :].astype(BF16))
        real, imag = made[:RADIX], made[RADIX:]
        wide[pl.ds(b, RADIX, stride=WIDE), :] = real * real + imag * imag
        return carry

    lax.fori_loop(0, 32, closing, 0, unroll=8)
    for t in range(16):
        rows = [
            wide[a * WIDE + chunk * 32 : a * WIDE + chunk * 32 + 32, :]
            for a in range(4 * t, 4 * t + 4)
        ]
        block = jnp.concatenate(rows).astype(BF16)
        made = lax.dot_general(eye[...], block, NT, preferred_element_type=F32)
        here = slice(t * 128, (t + 1) * 128)
        planes[chunk, :, :, here] = made.reshape(16, 8, 128).astype(BF16)


def edge_rows(chunk, stack, low, high):
    rows = lax.broadcasted_iota(jnp.int32, (PLANES, HALF), 0)
    bottom, top = jnp.zeros((PLANES, HALF), F32), jnp.zeros((PLANES, HALF), F32)
    for g in range(PLANES):
        plane = stack[chunk, g].astype(F32)
        bottom = jnp.where(rows == g, plane[0:1], bottom)
        top = jnp.where(rows == g, plane[7:8], top)
    low[chunk] = bottom.astype(BF16)
    high[chunk] = top.astype(BF16)


def depth_scores(chunk, stack, scores):
    def one(g, carry):
        lower = stack[chunk, jnp.maximum(g - 1, 0)].astype(F32)
        upper = stack[chunk, jnp.minimum(g + 1, PLANES - 1)].astype(F32)
        scores[chunk, g] = (upper - lower) * (upper - lower)
        return carry

    lax.fori_loop(0, PLANES, one, 0, unroll=2)


def row_scores(chunk, stack, scores, north, south, first, last):
    row = lax.broadcasted_iota(jnp.int32, (8, HALF), 0)
    norths, souths = north[chunk].astype(F32), south[chunk].astype(F32)
    for g in range(PLANES):
        centre = stack[chunk, g].astype(F32)
        before = jnp.where(first, centre[0:1], norths[g : g + 1])
        after = jnp.where(last, centre[7:8], souths[g : g + 1])
        above = jnp.where(row == 0, before, pltpu.roll(centre, 1, 0))
        below = jnp.where(row == 7, after, pltpu.roll(centre, 7, 0))
        scores[chunk, g] = scores[chunk, g] + (below - above) * (below - above)


def side_scores(stack, scores):
    lane = lax.broadcasted_iota(jnp.int32, (8, HALF), 1)
    start, end = lax.rem(lane, 32) == 0, lax.rem(lane, 32) == 31

    def one(g, carry):
        left, right = stack[0, g].astype(F32), stack[1, g].astype(F32)
        left_before, left_after = pltpu.roll(left, 1, 1), pltpu.roll(left, HALF - 1, 1)
        right_before, right_after = pltpu.roll(right, 1, 1), pltpu.roll(right, HALF - 1, 1)
        west = jnp.where(start, jnp.where(lane == 0, left, right_before), left_before)
        east = jnp.where(end, pltpu.roll(right, 31, 1), left_after)
        scores[0, g] = scores[0, g] + (east - west) * (east - west)
        west = jnp.where(start, pltpu.roll(left, HALF - 31, 1), right_before)
        east = jnp.where(end, jnp.where(lane == HALF - 1, right, left_after), right_after)
        scores[1, g] = scores[1, g] + (east - west) * (east - west)
        return carry

    lax.fori_loop(0, PLANES, one, 0)


def sharpest(scores, natural, piece):
    best = [jnp.max(scores[chunk], axis=0) / 8.0 for chunk in range(2)]
    lane = lax.broadcasted_iota(jnp.int32, (8, 128), 1)
    tiles = []
    for t in range(16):
        here = slice(t * 128, (t + 1) * 128)
        first, second = best[0][:, here], best[1][:, here]
        tiles.append(jnp.where(lane < RADIX, first, pltpu.roll(second, RADIX, 1)))
        tiles.append(jnp.where(lane < RADIX, pltpu.roll(first, RADIX, 1), second))
    made = matmul_right(jnp.concatenate(tiles).astype(BF16), natural)
    for t in range(32):
        piece[:, t * 128 : (t + 1) * 128] = made[t * 8 : (t + 1) * 8].astype(BF16)


def whole_kernel(
    hologram, background, open_exact, ahead, back, both, eye, natural, out,
    sections, columns, passing, wide, middle, other, cosines, sines, k_real, k_imag,
    blocks, staged, gathered, planes, opposite, stack, scores, low, high, north, south, piece,
    send1, recv1, relay1_send, relay1_recv, send2, recv2, relay_send, relay_recv,
    send3, recv3, far_send, far_recv, send4, recv4, send5, recv5, own_sem,
):
    at = {name: lax.axis_index(name) for name in AXES}
    x, y, c, zh, zl = at["x"], at["y"], at["c"], at["zh"], at["zl"]
    yc, z = y * 2 + c, zh * 4 + zl
    me, slab = x * 8 + yc, zl * 8 + yc
    xs = lax.rem(x - zl + 4, 4)
    q = (slab * 4 + zh) * 4 + xs

    def near(dy, dc, turn):
        layer = lax.rem(z + turn + 16, 16)
        return {
            "zh": layer // 4,
            "x": x,
            "zl": lax.rem(layer, 4),
            "y": lax.rem(y + dy + 4, 4),
            "c": lax.rem(c + dc, 2),
        }

    def level(dx, dy, dc):
        return {
            "zh": zh,
            "x": lax.rem(x + dx + 4, 4),
            "zl": zl,
            "y": lax.rem(y + dy + 4, 4),
            "c": lax.rem(c + dc, 2),
        }

    def number(device):
        return device["x"] * 8 + device["y"] * 2 + device["c"]

    def slab_of(device):
        return device["zl"] * 8 + device["y"] * 2 + device["c"]

    def above(layer):
        return {**at, "zh": layer // 4, "zl": lax.rem(layer, 4)}

    def up(turn):
        return lax.rem(z + turn + 16, 16)

    def block_owner(index):
        owner = index // 16
        low_z = owner // 8
        return {
            "zh": lax.rem(index // 4, 4),
            "x": lax.rem(lax.rem(index, 4) + low_z, 4),
            "zl": low_z,
            "y": lax.rem(owner // 2, 4),
            "c": lax.rem(owner, 2),
        }

    moves, hops = [], []
    for turn in (2, 1, -1, 0):
        for dc in (1, 0):
            toward = -2 if turn == 2 and dc else turn
            hops.append((-1 if dc else 1, dc, toward))
            for dy in (1, -1, 0):
                if (dy, dc, turn) != (0, 0, 0):
                    moves.append((dy, dc, toward))
    relayed, direct = [], []
    for dx in (2, 1, 3, 0):
        for dy in (2, 1, 3, 0):
            for dc in (1, 0):
                if 2 in (dx, dy):
                    side = -1 if dc else 1
                    hop = [side if d == 2 else (-1 if d == 3 else d) for d in (dx, dy)]
                    rest = [side if d == 2 else 0 for d in (dx, dy)]
                    relayed.append((hop[0], hop[1], dc, rest[0], rest[1]))
                elif (dx, dy, dc) != (0, 0, 0):
                    direct.append((-1 if dx == 3 else dx, -1 if dy == 3 else dy, dc))
    turns = (7, -7, 6, -6, 5, -5, 4, -4, 3, -3, 2, -2, 1, -1)
    ahead_q, behind_q = block_owner(lax.rem(q + 1, 512)), block_owner(lax.rem(q + 511, 512))

    barrier = pltpu.get_barrier_semaphore()
    everyone = [near(-dy, dc, -turn) for dy, dc, turn in moves + hops]
    everyone += [level(dx, dy, dc) for dx in range(4) for dy in range(4) for dc in range(2)][1:]
    everyone += [above(up(turn)) for turn in turns]
    everyone += [ahead_q, behind_q]
    for device in everyone:
        pl.semaphore_signal(barrier, inc=1, device_id=device, device_id_type=MESH)
    row_pass(x, hologram, background, open_exact, ahead, eye, wide, middle, sections)
    pl.semaphore_wait(barrier, len(everyone))

    sent = []
    for index, (side, dc, turn) in enumerate(hops):
        target = near(2, dc, turn)
        sent.append(
            remote(
                sections.at[target["y"] * 2 + target["c"]],
                passing.at[index],
                relay1_send.at[index],
                relay1_recv.at[index],
                near(side, dc, turn),
            )
        )
        sent[-1].start()
    for index, (dy, dc, turn) in enumerate(moves):
        target = near(dy, dc, turn)
        sent.append(
            remote(
                sections.at[target["y"] * 2 + target["c"]],
                columns.at[slab],
                send1.at[index],
                recv1.at[slab],
                target,
            )
        )
        sent[-1].start()
    own = pltpu.make_async_copy(sections.at[yc], columns.at[slab], own_sem)
    own.start()
    make_tables(me, z, cosines, sines, k_real, k_imag)
    own.wait()
    widen(slab, columns, wide)
    for index, (side, dc, turn) in enumerate(hops):
        source = near(-side, dc, -turn)
        slot = passing.at[index]
        remote(slot, slot, own_sem, relay1_recv.at[index], source).wait_recv()
        sent.append(
            remote(
                slot,
                columns.at[slab_of(source)],
                send1.at[len(moves) + index],
                recv1.at[slab_of(source)],
                level(0, side, 0),
            )
        )
        sent[-1].start()
    arrivals = [(-dy, dc, -turn) for dy, dc, turn in reversed(moves)]
    arrivals += [(2, dc, -turn) for side, dc, turn in hops]
    for dy, dc, turn in arrivals:
        source = near(dy, dc, turn)
        origin = slab_of(source)
        slot = columns.at[origin]
        remote(slot, slot, own_sem, recv1.at[origin], source).wait_recv()
        widen(origin, columns, wide)
    for copy in sent:
        copy.wait_send()

    tables = (open_exact, ahead, back)
    column_pass(me, tables, wide, middle, other, k_real, k_imag, cosines, sines)

    sent = []

    def send_relayed(chunk, index):
        hx, hy, dc, rx, ry = relayed[index]
        sent.append(
            remote(
                blocks.at[number(level(hx + rx, hy + ry, dc)), chunk],
                staged.at[chunk, index],
                relay_send.at[chunk, index],
                relay_recv.at[chunk, index],
                level(hx, hy, dc),
            )
        )
        sent[-1].start()

    def send_direct(chunk, index):
        device = level(*direct[index])
        sent.append(
            remote(
                blocks.at[number(device), chunk],
                gathered.at[me, chunk],
                send2.at[chunk, index],
                recv2.at[me, chunk],
                device,
            )
        )
        sent[-1].start()

    def make(device):
        make_block(me, number(device), both, middle, cosines, sines, blocks)

    for index, (hx, hy, dc, rx, ry) in enumerate(relayed):
        make(level(hx + rx, hy + ry, dc))
        if index % 2:
            send_relayed(0, index - 1)
            send_relayed(0, index)
    for index, offset in enumerate(direct):
        make(level(*offset))
        if index % 2:
            send_direct(0, index - 1)
            send_direct(0, index)
    send_direct(0, len(direct) - 1)
    for index in range(len(relayed)):
        send_relayed(1, index)
    for index in range(len(direct)):
        send_direct(1, index)
    make(level(0, 0, 0))
    own = pltpu.make_async_copy(blocks.at[me], gathered.at[me], own_sem)
    own.start()
    own.wait()

    def part(chunk, layer):
        return planes.at[chunk, lax.rem(layer, 4) * 4 + layer // 4]

    lanes = (pl.ds(0, HALF // 2), pl.ds(HALF // 2, HALF // 2))

    def forward_far(chunk):
        for side, turn in enumerate((4, -4)):
            slot = opposite.at[chunk, side]
            remote(slot, slot, own_sem, far_recv.at[chunk, side], above(up(-turn))).wait_recv()
            sent.append(
                remote(
                    slot,
                    stack.at[chunk, up(-turn), :, lanes[side]],
                    far_send.at[chunk, 2 + side],
                    recv3.at[chunk, up(-turn), side],
                    above(up(turn)),
                )
            )
            sent[-1].start()

    for chunk in range(2):
        for index, (hx, hy, dc, rx, ry) in enumerate(relayed):
            source = level(-hx, -hy, dc)
            slot = staged.at[chunk, index]
            remote(slot, slot, own_sem, relay_recv.at[chunk, index], source).wait_recv()
            sent.append(
                remote(
                    slot,
                    gathered.at[number(source), chunk],
                    send2.at[chunk, len(direct) + index],
                    recv2.at[number(source), chunk],
                    level(rx, ry, 0),
                )
            )
            sent[-1].start()
        place_block(me, chunk, gathered, other)
        arrivals = [(-dx, -dy, dc) for dx, dy, dc in direct]
        arrivals += [(-hx - rx, -hy - ry, dc) for hx, hy, dc, rx, ry in relayed]
        for dx, dy, dc in arrivals:
            device = level(dx, dy, dc)
            source = number(device)
            slot = gathered.at[source, chunk]
            remote(slot, slot, own_sem, recv2.at[source, chunk], device).wait_recv()
            place_block(source, chunk, gathered, other)
        close_rows(chunk, back, eye, other, wide, planes)
        if chunk:
            forward_far(0)
        far = up(8)
        for side, turn in enumerate((4, -4)):
            sent.append(
                remote(
                    part(chunk, far).at[:, lanes[side]],
                    opposite.at[chunk, side],
                    far_send.at[chunk, side],
                    far_recv.at[chunk, side],
                    above(up(turn)),
                )
            )
            sent[-1].start()
        for index, turn in enumerate(turns):
            layer = up(turn)
            sent.append(
                remote(
                    part(chunk, layer),
                    stack.at[chunk, z],
                    send3.at[chunk, index],
                    recv3.at[chunk, z, 0],
                    above(layer),
                )
            )
            sent[-1].start()
        own = pltpu.make_async_copy(part(chunk, z), stack.at[chunk, z], own_sem)
        own.start()
        own.wait()
    forward_far(1)

    def edges(chunk):
        edge_rows(chunk, stack, low, high)
        pair = [
            remote(
                high.at[chunk], north.at[chunk],
                send4.at[chunk, 0], recv4.at[chunk, 0], ahead_q,
            ),
            remote(
                low.at[chunk], south.at[chunk],
                send4.at[chunk, 1], recv4.at[chunk, 1], behind_q,
            ),
        ]
        for copy in pair:
            copy.start()
        return pair

    for chunk in range(2):
        for turn in reversed(turns):
            slot = stack.at[chunk, up(turn)]
            remote(slot, slot, own_sem, recv3.at[chunk, up(turn), 0], above(up(turn))).wait_recv()
        for side, turn in enumerate((-4, 4)):
            slot = stack.at[chunk, up(8), :, lanes[side]]
            remote(slot, slot, own_sem, recv3.at[chunk, up(8), side], above(up(turn))).wait_recv()
        pair = edges(chunk)
        depth_scores(chunk, stack, scores)
        if chunk:
            side_scores(stack, scores)
        for copy in pair:
            copy.wait()
        row_scores(chunk, stack, scores, north, south, q == 0, q == 511)
    for copy in sent:
        copy.wait_send()
    sharpest(scores, natural, piece)

    left, right = pl.ds(0, N // 2), pl.ds(N // 2, N // 2)
    halves = (left, right)
    sent = []

    def across(step):
        return {**at, "x": lax.rem(x + step + 4, 4)}

    def along(step):
        return {**at, "zh": lax.rem(zh + step + 4, 4)}

    def row_of(place):
        return lax.rem(place - zl + 4, 4)

    def send(source, target, sem, device):
        sent.append(remote(source, target, send5.at[len(sent)], sem, device))
        sent[-1].start()

    def arrive(place, high_z, half, device):
        slot = out.at[high_z, row_of(place)]
        slot = slot if half is None else slot.at[:, halves[half]]
        sem = recv5.at[place, high_z, half or 0]
        remote(slot, slot, own_sem, sem, device).wait_recv()

    for step in (1, -1):
        send(piece, out.at[zh, xs], recv5.at[x, zh, 0], along(step))
    for step in (1, -1):
        send(piece, out.at[zh, xs], recv5.at[x, zh, 0], across(step))
    own = pltpu.make_async_copy(piece, out.at[zh, xs], own_sem)
    own.start()
    for half, step in enumerate((1, -1)):
        from_z = lax.rem(zh - step + 4, 4)
        arrive(x, from_z, None, along(-step))
        slot = out.at[from_z, xs, :, halves[half]]
        send(slot, slot, recv5.at[x, from_z, half], along(step))
        for turn in (1, -1):
            slot = out.at[from_z, xs]
            send(slot, slot, recv5.at[x, from_z, 0], across(turn))
    far_z = lax.rem(zh + 2, 4)
    for high_z in (zh, lax.rem(zh + 3, 4), lax.rem(zh + 1, 4), far_z):
        if high_z is far_z:
            for half, step in enumerate((1, -1)):
                arrive(x, far_z, half, along(-step))
            for turn in (1, -1):
                slot = out.at[far_z, xs]
                send(slot, slot, recv5.at[x, far_z, 0], across(turn))
        for half, step in enumerate((1, -1)):
            place = lax.rem(x - step + 4, 4)
            arrive(place, high_z, None, across(-step))
            slot = out.at[high_z, row_of(place), :, halves[half]]
            send(slot, slot, recv5.at[place, high_z, half], across(step))
    for high_z in (zh, lax.rem(zh + 3, 4), lax.rem(zh + 1, 4), far_z):
        for half, step in enumerate((1, -1)):
            arrive(lax.rem(x + 2, 4), high_z, half, across(-step))
    own.wait()
    for copy in sent:
        copy.wait_send()


def shards(hologram, background):
    vmem, dma = pltpu.VMEM, pltpu.SemaphoreType.DMA
    table = vmem((RADIX, RADIX, 128), F32)
    merged = pl.pallas_call(
        whole_kernel,
        name="whole",
        out_shape=jax.ShapeDtypeStruct((4, 4, 8, N), BF16),
        in_specs=[pl.BlockSpec(memory_space=vmem)] * 8,
        out_specs=pl.BlockSpec(memory_space=vmem),
        scratch_shapes=[
            vmem((8, 128, 128), BF16),
            vmem((32, 128, 128), BF16),
            vmem((8, 128, 128), BF16),
            vmem((RADIX * WIDE, 128), F32),
            vmem((2 * RADIX * WIDE, 128), F32),
            vmem((2 * RADIX * WIDE, 128), F32),
            table,
            table,
            vmem((N, 128), F32),
            vmem((N, 128), F32),
            vmem((32, 2, 4, 32, 128), BF16),
            vmem((2, 14, 4, 32, 128), BF16),
            vmem((32, 2, 4, 32, 128), BF16),
            vmem((2, 16, 8, HALF), BF16),
            vmem((2, 2, 8, HALF // 2), BF16),
            vmem((2, PLANES, 8, HALF), BF16),
            vmem((2, PLANES, 8, HALF), F32),
            *[vmem((2, PLANES, HALF), BF16)] * 4,
            vmem((8, N), BF16),
            dma((31,)),
            dma((32,)),
            dma((8,)),
            dma((8,)),
            dma((2, 31)),
            dma((32, 2)),
            dma((2, 14)),
            dma((2, 14)),
            dma((2, 14)),
            dma((2, 16, 2)),
            dma((2, 4)),
            dma((2, 2)),
            dma((2, 2)),
            dma((2, 2)),
            dma((20,)),
            dma((4, 4, 2)),
            dma,
        ],
        compiler_params=pltpu.CompilerParams(
            collective_id=0, has_side_effects=True, vmem_limit_bytes=56 << 20
        ),
    )(hologram, background, *pass_tables())
    return merged.reshape(128, N).astype(F32)


def solution(mesh):
    fine = Mesh(mesh.devices.reshape(SIZES), AXES)
    spec = P(("zl", "y", "c"), None)
    return jax.shard_map(
        shards, mesh=fine, in_specs=(spec, spec), out_specs=spec, check_vma=False
    )
```

```python
import math

import jax
import jax.numpy as jnp
import numpy as np
from jax import lax
from jax.experimental import pallas as pl
from jax.experimental.pallas import tpu as pltpu
from jax.sharding import Mesh
from jax.sharding import PartitionSpec as P

N = 4096
RADIX = 64
PLANES = 16
WIDE = 72
DEEP = 136
CHUNKS = 4
PART = RADIX // CHUNKS
LANES = N // CHUNKS
AXES = ("zh", "x", "zl", "y", "c")
SIZES = (4, 4, 4, 4, 2)
MESH = pl.DeviceIdType.MESH
NT = (((1,), (1,)), ((), ()))
F32 = jnp.float32
BF16 = jnp.bfloat16

wave_number = 0.6
depth_start = 8.0
depth_step = 2.0


def fourier_tables(sign_value):
    indices = np.arange(RADIX)
    angles = (indices[:, None] * indices[None, :] % RADIX) * (sign_value * 2.0 * math.pi / RADIX)
    real, imag = np.cos(angles) / math.sqrt(RADIX), np.sin(angles) / math.sqrt(RADIX)
    matrix = np.stack([np.stack([real, -imag]), np.stack([imag, real])])
    return matrix.astype(np.float32)


def twiddle_table(sign_value):
    indices = np.arange(RADIX)
    angles = (indices[:, None] * indices[None, :]) * (sign_value * 2.0 * math.pi / N)
    return np.cos(angles).astype(np.float32), np.sin(angles).astype(np.float32)


def pass_tables():
    ahead, back = fourier_tables(-1.0), fourier_tables(1.0)
    flat = lambda table: table.transpose(0, 2, 1, 3).reshape(128, 128)
    natural = np.eye(128, dtype=np.float32).reshape(2, CHUNKS, PART, 128)
    natural = natural.swapaxes(0, 1).reshape(128, 128)
    both = np.zeros((2, 2, 2, RADIX, 2, 128), np.float32)
    for lane in range(128):
        far, j = divmod(lane, RADIX)
        both[1, :, far, :, :, lane] = back[:, :, :, RADIX - 1 - j if far else j].transpose(0, 2, 1)
        if j >= RADIX // 2:
            half, j = 1, (95 - j if far else j - 32)
        else:
            half, j = 0, ((RADIX - j if j else 32) if far else j)
        both[0, :, half, :, :, lane] = back[:, :, :, j].transpose(0, 2, 1)
    tables = (
        flat(ahead),
        flat(back),
        both.reshape(2, 256, 256),
        np.eye(128, dtype=np.float32),
        natural,
    )
    return [jnp.asarray(ahead[:, 0].reshape(128, RADIX), F32)] + [
        jnp.asarray(table, BF16) for table in tables
    ]


def row_pass(x, hologram, background, open_exact, ahead, eye, wide, middle, sections):
    for t in range(32):
        here = slice(t * 128, (t + 1) * 128)
        ratio = hologram[:, here].astype(F32) / background[:, here].astype(F32)
        contrast = (ratio - 1.0).astype(BF16)
        made = lax.dot_general(eye[...], contrast, NT, preferred_element_type=F32)
        wide[2 * t * WIDE : 2 * t * WIDE + RADIX, :] = made[:RADIX]
        wide[(2 * t + 1) * WIDE : (2 * t + 1) * WIDE + RADIX, :] = made[RADIX:]
    own = pl.multiple_of(x * 8, 8)
    chosen = [open_exact[pl.ds(own, 8), :], open_exact[32:40, :]]
    chosen += [open_exact[pl.ds(RADIX + own, 8), :], open_exact[RADIX + 32 : RADIX + 40, :]]
    matrix = jnp.concatenate(chosen).astype(BF16)
    row = lax.broadcasted_iota(jnp.int32, (16, 128), 0)
    k = jnp.where(row < 8, x * 8 + row, row + 24).astype(F32)

    def opening(b, carry):
        data = wide[pl.ds(b, RADIX, stride=WIDE), :].astype(BF16)
        made = jnp.dot(matrix, data, preferred_element_type=F32)
        real, imag = made[:16], made[16:]
        sine, cosine = sine_cosine(k * (b.astype(F32) / N))
        middle[pl.ds(b, 16, stride=DEEP), :] = real * cosine + imag * sine
        middle[pl.ds(RADIX + b, 16, stride=DEEP), :] = imag * cosine - real * sine
        return carry

    lax.fori_loop(0, RADIX, opening, 0, unroll=16)

    def section(index):
        made = matmul(ahead, middle[index * DEEP : index * DEEP + 128, :].astype(BF16))
        return lax.dot_general(eye[...], made.astype(BF16), NT, preferred_element_type=F32)

    lane = lax.broadcasted_iota(jnp.int32, (128, 128), 1)
    zero, half = section(0), section(8)
    turned = pltpu.roll(zero, 32, 1)
    packed = jnp.where(lax.rem(lane, RADIX) >= 32, pltpu.roll(half, 32, 1), zero)
    packed = jnp.where(lane == RADIX, turned, packed)
    sections[0] = jnp.where(x == 0, packed, zero).astype(BF16)
    for index in range(1, 8):
        sections[index] = section(index).astype(BF16)


def remote(source, target, send_sem, recv_sem, device):
    return pltpu.make_async_remote_copy(
        src_ref=source,
        dst_ref=target,
        send_sem=send_sem,
        recv_sem=recv_sem,
        device_id=device,
        device_id_type=MESH,
    )


def sine_cosine(turns):
    half = (turns - jnp.floor(turns + 0.5)) * math.pi
    square = half * half
    sine, cosine = jnp.zeros_like(half), jnp.zeros_like(half)
    for power in range(6, -1, -1):
        cosine = cosine * square + (-1) ** power / math.factorial(2 * power)
        if power < 6:
            sine = sine * square + (-1) ** power / math.factorial(2 * power + 1)
    sine = sine * half
    return 2.0 * sine * cosine, 1.0 - 2.0 * sine * sine


def make_tables(me, z, cosines, sines, k_real, k_imag):
    distance = depth_start + depth_step * z.astype(F32)
    lane = lax.broadcasted_iota(jnp.int32, (RADIX, 128), 1)
    row = lax.broadcasted_iota(jnp.int32, (RADIX, 128), 0)
    j = lax.rem(lane, RADIX)
    general = me + RADIX * j
    lone = jnp.where(j == 0, jnp.where(lane >= RADIX, N // 2, 0), RADIX * j)
    lone = jnp.where(j >= RADIX // 2, 32 + RADIX * (j - RADIX // 2), lone)
    natural = jnp.where(me == 0, lone, general)
    freq = jnp.where(natural >= N // 2, natural - N, natural).astype(F32) / N
    column_part = freq * freq
    base = jnp.where(row >= RADIX // 2, RADIX * row - N, RADIX * row)
    limit = wave_number * wave_number

    def tile(k, carry):
        here = pl.ds(k * RADIX, RADIX)
        sine, cosine = sine_cosine((row * k).astype(F32) / N)
        cosines[k], sines[k] = cosine, sine
        freq = (base + k).astype(F32) / N
        radial = freq * freq + column_part
        amplitude = jnp.exp(
            (-2.0 * math.pi * distance) * jnp.sqrt(jnp.maximum(radial - limit, 0.0))
        )
        turns = distance * (jnp.sqrt(jnp.maximum(limit - radial, 0.0)) - wave_number)
        sine, cosine = sine_cosine(turns)
        k_real[here, :] = amplitude * cosine
        k_imag[here, :] = amplitude * sine
        return carry

    lax.fori_loop(0, RADIX, tile, 0)


def widen(slab, columns, wide):
    for half in range(2):
        rows = columns[slab, pl.ds(half * RADIX, RADIX), :]
        wide[pl.ds((2 * slab + half) * WIDE, RADIX), :] = rows.astype(F32)


def matmul(matrix, data):
    return jnp.dot(matrix[...], data, preferred_element_type=F32)


def matmul_right(data, matrix):
    return jnp.dot(data, matrix[...], preferred_element_type=F32)


def column_pass(me, tables, wide, middle, other, k_real, k_imag, cosines, sines):
    open_exact, ahead, back = tables
    lane = lax.broadcasted_iota(jnp.int32, (RADIX, 128), 1)
    low = lane < RADIX
    alone = (me == 0) & (lax.rem(lane, RADIX) == 0)

    open_ahead = open_exact[...].astype(BF16)

    def first(b, carry):
        made = matmul(open_ahead, wide[pl.ds(b, RADIX, stride=WIDE), :].astype(BF16))
        real, imag = made[:RADIX], made[RADIX:]
        cosine, sine = cosines[b], sines[b]
        middle[pl.ds(b, RADIX, stride=DEEP), :] = real * cosine + imag * sine
        middle[pl.ds(RADIX + b, RADIX, stride=DEEP), :] = imag * cosine - real * sine
        return carry

    lax.fori_loop(0, RADIX, first, 0, unroll=16)

    def second(k, carry):
        made = matmul(ahead, middle[pl.ds(k * DEEP, 128), :].astype(BF16))
        real, imag = made[:RADIX], made[RADIX:]
        real_turn, imag_turn = pltpu.roll(real, RADIX, 1), pltpu.roll(imag, RADIX, 1)
        spectrum_real = jnp.where(low, real - imag_turn, real_turn + imag)
        spectrum_imag = jnp.where(low, imag + real_turn, imag_turn - real)
        spectrum_real = jnp.where(alone, real, spectrum_real).astype(BF16).astype(F32)
        spectrum_imag = jnp.where(alone, imag, spectrum_imag).astype(BF16).astype(F32)
        here = pl.ds(k * RADIX, RADIX)
        kernel_real, kernel_imag = k_real[here, :], k_imag[here, :]
        propagated = jnp.concatenate(
            [
                spectrum_real * kernel_real - spectrum_imag * kernel_imag,
                spectrum_real * kernel_imag + spectrum_imag * kernel_real,
            ]
        )
        made = matmul(back, propagated.astype(BF16))
        real, imag = made[:RADIX], made[RADIX:]
        cosine, sine = cosines[k], sines[k]
        other[pl.ds(k, RADIX, stride=DEEP), :] = real * cosine - imag * sine
        other[pl.ds(RADIX + k, RADIX, stride=DEEP), :] = real * sine + imag * cosine
        return carry

    lax.fori_loop(0, RADIX, second, 0, unroll=16)

    def third(b, carry):
        made = matmul(back, other[pl.ds(b * DEEP, 128), :].astype(BF16))
        middle[pl.ds(b, RADIX, stride=WIDE), :] = made[:RADIX]
        middle[pl.ds(RADIX * WIDE + b, RADIX, stride=WIDE), :] = made[RADIX:]
        return carry

    lax.fori_loop(0, RADIX, third, 0, unroll=16)


def block_rows(middle, part, x, yc):
    rows = []
    for low_z in range(4):
        start = (part * RADIX + low_z * 16 + yc * 2) * WIDE + lax.rem(x - low_z + 4, 4) * 8
        for zh in range(4):
            offset = pl.multiple_of(start + zh // 2 * WIDE + zh % 2 * 32, 8)
            rows.append(middle[pl.ds(offset, 8), :])
    return jnp.concatenate(rows).astype(BF16)


def partner(k):
    return jnp.where(k == 0, 32, RADIX - k)


def make_block(me, target, both, middle, cosines, sines, blocks):
    x, yc = target // 8, lax.rem(target, 8)
    data = jnp.concatenate([block_rows(middle, part, x, yc) for part in range(2)], axis=1)
    made = lax.dot_general(both[jnp.minimum(me, 1)], data, NT, preferred_element_type=F32)
    for half in range(2):
        k = partner(me) if half else me
        real = made[half * RADIX : (half + 1) * RADIX]
        imag = made[128 + half * RADIX : 128 + (half + 1) * RADIX]
        cosine, sine = cosines[k], sines[k]
        turned = (real * cosine - imag * sine, real * sine + imag * cosine)
        for part in range(2):
            for chunk in range(CHUNKS):
                rows = turned[part][chunk * PART : (chunk + 1) * PART]
                blocks[target, chunk, part * 2 + half] = rows.astype(BF16)


def place_block(source, chunk, gathered, other):
    for part in range(2):
        for half in range(2):
            k = partner(source) if half else source
            rows = gathered[source, chunk, part * 2 + half].astype(F32)
            start = chunk * PART * DEEP + part * RADIX + k
            other[pl.ds(start, PART, stride=DEEP), :] = rows


def close_rows(chunk, back, eye, other, wide, planes):
    def closing(index, carry):
        b = chunk * PART + index
        made = matmul(back, other[pl.ds(b * DEEP, 128), :].astype(BF16))
        real, imag = made[:RADIX], made[RADIX:]
        wide[pl.ds(b, RADIX, stride=WIDE), :] = real * real + imag * imag
        return carry

    lax.fori_loop(0, PART, closing, 0, unroll=PART)
    span = 128 // PART
    for t in range(LANES // 128):
        rows = [
            wide[a * WIDE + chunk * PART : a * WIDE + (chunk + 1) * PART, :]
            for a in range(span * t, span * (t + 1))
        ]
        block = jnp.concatenate(rows).astype(BF16)
        made = lax.dot_general(eye[...], block, NT, preferred_element_type=F32)
        here = slice(t * 128, (t + 1) * 128)
        planes[chunk, :, :, here] = made.reshape(16, 8, 128).astype(BF16)


def edge_rows(chunk, stack, low, high):
    rows = lax.broadcasted_iota(jnp.int32, (PLANES, LANES), 0)
    bottom, top = jnp.zeros((PLANES, LANES), F32), jnp.zeros((PLANES, LANES), F32)
    for g in range(PLANES):
        plane = stack[chunk, g].astype(F32)
        bottom = jnp.where(rows == g, plane[0:1], bottom)
        top = jnp.where(rows == g, plane[7:8], top)
    low[chunk] = bottom.astype(BF16)
    high[chunk] = top.astype(BF16)


def depth_scores(chunk, stack, scores):
    def one(g, carry):
        lower = stack[chunk, jnp.maximum(g - 1, 0)].astype(F32)
        upper = stack[chunk, jnp.minimum(g + 1, PLANES - 1)].astype(F32)
        scores[chunk, g] = (upper - lower) * (upper - lower)
        return carry

    lax.fori_loop(0, PLANES, one, 0, unroll=2)


def row_scores(chunk, stack, scores, north, south, first, last):
    row = lax.broadcasted_iota(jnp.int32, (8, LANES), 0)
    norths, souths = north[chunk].astype(F32), south[chunk].astype(F32)
    for g in range(PLANES):
        centre = stack[chunk, g].astype(F32)
        before = jnp.where(first, centre[0:1], norths[g : g + 1])
        after = jnp.where(last, centre[7:8], souths[g : g + 1])
        above = jnp.where(row == 0, before, pltpu.roll(centre, 1, 0))
        below = jnp.where(row == 7, after, pltpu.roll(centre, 7, 0))
        scores[chunk, g] = scores[chunk, g] + (below - above) * (below - above)


def side_scores(chunk, stack, scores):
    lane = lax.broadcasted_iota(jnp.int32, (8, LANES), 1)
    start, end = lax.rem(lane, PART) == 0, lax.rem(lane, PART) == PART - 1

    def one(g, carry):
        centre = stack[chunk, g].astype(F32)
        before = stack[(chunk - 1) % CHUNKS, g].astype(F32)
        after = stack[(chunk + 1) % CHUNKS, g].astype(F32)
        if chunk:
            before = pltpu.roll(before, LANES - PART + 1, 1)
        else:
            before = jnp.where(lane == 0, centre, pltpu.roll(before, 1, 1))
        if chunk < CHUNKS - 1:
            after = pltpu.roll(after, PART - 1, 1)
        else:
            after = jnp.where(lane == LANES - 1, centre, pltpu.roll(after, LANES - 1, 1))
        west = jnp.where(start, before, pltpu.roll(centre, 1, 1))
        east = jnp.where(end, after, pltpu.roll(centre, LANES - 1, 1))
        scores[chunk, g] = scores[chunk, g] + (east - west) * (east - west)
        return carry

    lax.fori_loop(0, PLANES, one, 0, unroll=2)


def sharpest(scores, natural, piece):
    best = [jnp.max(scores[chunk], axis=0) / 8.0 for chunk in range(CHUNKS)]
    width = 128 // CHUNKS
    lane = lax.broadcasted_iota(jnp.int32, (8, 128), 1)
    tiles = []
    for t in range(32):
        here = slice(t // CHUNKS * 128, (t // CHUNKS + 1) * 128)
        made = jnp.zeros((8, 128), F32)
        for chunk in range(CHUNKS):
            shift = (chunk - t) % CHUNKS * width
            moved = best[chunk][:, here]
            moved = pltpu.roll(moved, shift, 1) if shift else moved
            made = jnp.where(lane // width == chunk, moved, made)
        tiles.append(made)
    made = matmul_right(jnp.concatenate(tiles).astype(BF16), natural)
    for t in range(32):
        piece[:, t * 128 : (t + 1) * 128] = made[t * 8 : (t + 1) * 8].astype(BF16)


def whole_kernel(
    hologram, background, open_exact, ahead, back, both, eye, natural, out,
    sections, columns, passing, wide, middle, other, cosines, sines, k_real, k_imag,
    blocks, staged, gathered, planes, opposite, stack, scores, low, high, north, south, piece,
    send1, recv1, relay1_send, relay1_recv, send2, recv2, relay_send, relay_recv,
    send3, recv3, far_send, far_recv, send4, recv4, send5, recv5, own_sem,
):
    at = {name: lax.axis_index(name) for name in AXES}
    x, y, c, zh, zl = at["x"], at["y"], at["c"], at["zh"], at["zl"]
    yc, z = y * 2 + c, zh * 4 + zl
    me, slab = x * 8 + yc, zl * 8 + yc
    xs = lax.rem(x - zl + 4, 4)
    q = (slab * 4 + zh) * 4 + xs

    def near(dy, dc, turn):
        layer = lax.rem(z + turn + 16, 16)
        return {
            "zh": layer // 4,
            "x": x,
            "zl": lax.rem(layer, 4),
            "y": lax.rem(y + dy + 4, 4),
            "c": lax.rem(c + dc, 2),
        }

    def level(dx, dy, dc):
        return {
            "zh": zh,
            "x": lax.rem(x + dx + 4, 4),
            "zl": zl,
            "y": lax.rem(y + dy + 4, 4),
            "c": lax.rem(c + dc, 2),
        }

    def number(device):
        return device["x"] * 8 + device["y"] * 2 + device["c"]

    def slab_of(device):
        return device["zl"] * 8 + device["y"] * 2 + device["c"]

    def above(layer):
        return {**at, "zh": layer // 4, "zl": lax.rem(layer, 4)}

    def up(turn):
        return lax.rem(z + turn + 16, 16)

    def block_owner(index):
        owner = index // 16
        low_z = owner // 8
        return {
            "zh": lax.rem(index // 4, 4),
            "x": lax.rem(lax.rem(index, 4) + low_z, 4),
            "zl": low_z,
            "y": lax.rem(owner // 2, 4),
            "c": lax.rem(owner, 2),
        }

    moves, hops = [], []
    for turn in (2, 1, -1, 0):
        for dc in (1, 0):
            toward = -2 if turn == 2 and dc else turn
            hops.append((-1 if dc else 1, dc, toward))
            for dy in (1, -1, 0):
                if (dy, dc, turn) != (0, 0, 0):
                    moves.append((dy, dc, toward))
    relayed, direct = [], []
    for dx in (2, 1, 3, 0):
        for dy in (2, 1, 3, 0):
            for dc in (1, 0):
                if 2 in (dx, dy):
                    side = -1 if dc else 1
                    hop = [side if d == 2 else (-1 if d == 3 else d) for d in (dx, dy)]
                    rest = [side if d == 2 else 0 for d in (dx, dy)]
                    relayed.append((hop[0], hop[1], dc, rest[0], rest[1]))
                elif (dx, dy, dc) != (0, 0, 0):
                    direct.append((-1 if dx == 3 else dx, -1 if dy == 3 else dy, dc))
    turns = (7, -7, 6, -6, 5, -5, 4, -4, 3, -3, 2, -2, 1, -1)
    ahead_q, behind_q = block_owner(lax.rem(q + 1, 512)), block_owner(lax.rem(q + 511, 512))

    barrier = pltpu.get_barrier_semaphore()
    everyone = [near(-dy, dc, -turn) for dy, dc, turn in moves + hops]
    everyone += [level(dx, dy, dc) for dx in range(4) for dy in range(4) for dc in range(2)][1:]
    everyone += [above(up(turn)) for turn in turns]
    everyone += [ahead_q, behind_q]
    for device in everyone:
        pl.semaphore_signal(barrier, inc=1, device_id=device, device_id_type=MESH)
    with jax.named_scope("row_pass"):
        row_pass(x, hologram, background, open_exact, ahead, eye, wide, middle, sections)
    with jax.named_scope("barrier"):
        pl.semaphore_wait(barrier, len(everyone))

    sent = []
    for index, (side, dc, turn) in enumerate(hops):
        target = near(2, dc, turn)
        sent.append(
            remote(
                sections.at[target["y"] * 2 + target["c"]],
                passing.at[index],
                relay1_send.at[index],
                relay1_recv.at[index],
                near(side, dc, turn),
            )
        )
        sent[-1].start()
    for index, (dy, dc, turn) in enumerate(moves):
        target = near(dy, dc, turn)
        sent.append(
            remote(
                sections.at[target["y"] * 2 + target["c"]],
                columns.at[slab],
                send1.at[index],
                recv1.at[slab],
                target,
            )
        )
        sent[-1].start()
    own = pltpu.make_async_copy(sections.at[yc], columns.at[slab], own_sem)
    own.start()
    with jax.named_scope("tables"):
        make_tables(me, z, cosines, sines, k_real, k_imag)
    own.wait()
    widen(slab, columns, wide)
    for index, (side, dc, turn) in enumerate(hops):
        source = near(-side, dc, -turn)
        slot = passing.at[index]
        remote(slot, slot, own_sem, relay1_recv.at[index], source).wait_recv()
        sent.append(
            remote(
                slot,
                columns.at[slab_of(source)],
                send1.at[len(moves) + index],
                recv1.at[slab_of(source)],
                level(0, side, 0),
            )
        )
        sent[-1].start()
    arrivals = [(-dy, dc, -turn) for dy, dc, turn in reversed(moves)]
    arrivals += [(2, dc, -turn) for side, dc, turn in hops]
    for dy, dc, turn in arrivals:
        source = near(dy, dc, turn)
        origin = slab_of(source)
        slot = columns.at[origin]
        remote(slot, slot, own_sem, recv1.at[origin], source).wait_recv()
        widen(origin, columns, wide)
    for copy in sent:
        copy.wait_send()

    tables = (open_exact, ahead, back)
    with jax.named_scope("column_pass"):
        column_pass(me, tables, wide, middle, other, k_real, k_imag, cosines, sines)

    sent = []

    def send_relayed(chunk, index):
        hx, hy, dc, rx, ry = relayed[index]
        sent.append(
            remote(
                blocks.at[number(level(hx + rx, hy + ry, dc)), chunk],
                staged.at[chunk, index],
                relay_send.at[chunk, index],
                relay_recv.at[chunk, index],
                level(hx, hy, dc),
            )
        )
        sent[-1].start()

    def send_direct(chunk, index):
        device = level(*direct[index])
        sent.append(
            remote(
                blocks.at[number(device), chunk],
                gathered.at[me, chunk],
                send2.at[chunk, index],
                recv2.at[me, chunk],
                device,
            )
        )
        sent[-1].start()

    def make(device):
        make_block(me, number(device), both, middle, cosines, sines, blocks)

    for index, (hx, hy, dc, rx, ry) in enumerate(relayed):
        make(level(hx + rx, hy + ry, dc))
        if index % 2:
            send_relayed(0, index - 1)
            send_relayed(0, index)
    for index, offset in enumerate(direct):
        make(level(*offset))
        if index % 2:
            send_direct(0, index - 1)
            send_direct(0, index)
    send_direct(0, len(direct) - 1)
    for chunk in range(1, CHUNKS):
        for index in range(len(relayed)):
            send_relayed(chunk, index)
        for index in range(len(direct)):
            send_direct(chunk, index)
    make(level(0, 0, 0))
    own = pltpu.make_async_copy(blocks.at[me], gathered.at[me], own_sem)
    own.start()
    own.wait()

    def part(chunk, layer):
        return planes.at[chunk, lax.rem(layer, 4) * 4 + layer // 4]

    lanes = (pl.ds(0, LANES // 2), pl.ds(LANES // 2, LANES // 2))

    def forward_far(chunk):
        for side, turn in enumerate((4, -4)):
            slot = opposite.at[chunk, side]
            remote(slot, slot, own_sem, far_recv.at[chunk, side], above(up(-turn))).wait_recv()
            sent.append(
                remote(
                    slot,
                    stack.at[chunk, up(-turn), :, lanes[side]],
                    far_send.at[chunk, 2 + side],
                    recv3.at[chunk, up(-turn), side],
                    above(up(turn)),
                )
            )
            sent[-1].start()

    for chunk in range(CHUNKS):
        for index, (hx, hy, dc, rx, ry) in enumerate(relayed):
            source = level(-hx, -hy, dc)
            slot = staged.at[chunk, index]
            remote(slot, slot, own_sem, relay_recv.at[chunk, index], source).wait_recv()
            sent.append(
                remote(
                    slot,
                    gathered.at[number(source), chunk],
                    send2.at[chunk, len(direct) + index],
                    recv2.at[number(source), chunk],
                    level(rx, ry, 0),
                )
            )
            sent[-1].start()
        place_block(me, chunk, gathered, other)
        arrivals = [(-dx, -dy, dc) for dx, dy, dc in direct]
        arrivals += [(-hx - rx, -hy - ry, dc) for hx, hy, dc, rx, ry in relayed]
        for dx, dy, dc in arrivals:
            device = level(dx, dy, dc)
            source = number(device)
            slot = gathered.at[source, chunk]
            remote(slot, slot, own_sem, recv2.at[source, chunk], device).wait_recv()
            place_block(source, chunk, gathered, other)
        with jax.named_scope(f"close{chunk}"):
            close_rows(chunk, back, eye, other, wide, planes)
        if chunk:
            forward_far(chunk - 1)
        far = up(8)
        for side, turn in enumerate((4, -4)):
            sent.append(
                remote(
                    part(chunk, far).at[:, lanes[side]],
                    opposite.at[chunk, side],
                    far_send.at[chunk, side],
                    far_recv.at[chunk, side],
                    above(up(turn)),
                )
            )
            sent[-1].start()
        for index, turn in enumerate(turns):
            layer = up(turn)
            sent.append(
                remote(
                    part(chunk, layer),
                    stack.at[chunk, z],
                    send3.at[chunk, index],
                    recv3.at[chunk, z, 0],
                    above(layer),
                )
            )
            sent[-1].start()
        own = pltpu.make_async_copy(part(chunk, z), stack.at[chunk, z], own_sem)
        own.start()
        own.wait()
    forward_far(CHUNKS - 1)

    def edges(chunk):
        edge_rows(chunk, stack, low, high)
        pair = [
            remote(
                high.at[chunk], north.at[chunk],
                send4.at[chunk, 0], recv4.at[chunk, 0], ahead_q,
            ),
            remote(
                low.at[chunk], south.at[chunk],
                send4.at[chunk, 1], recv4.at[chunk, 1], behind_q,
            ),
        ]
        for copy in pair:
            copy.start()
        return pair

    for chunk in range(CHUNKS):
        for turn in reversed(turns):
            slot = stack.at[chunk, up(turn)]
            remote(slot, slot, own_sem, recv3.at[chunk, up(turn), 0], above(up(turn))).wait_recv()
        for side, turn in enumerate((-4, 4)):
            slot = stack.at[chunk, up(8), :, lanes[side]]
            remote(slot, slot, own_sem, recv3.at[chunk, up(8), side], above(up(turn))).wait_recv()
        with jax.named_scope(f"depth{chunk}"):
            pair = edges(chunk)
            depth_scores(chunk, stack, scores)
        if chunk > 1:
            side_scores(chunk - 1, stack, scores)
        if chunk == CHUNKS - 1:
            side_scores(0, stack, scores)
            side_scores(chunk, stack, scores)
        for copy in pair:
            copy.wait()
        with jax.named_scope(f"rows{chunk}"):
            row_scores(chunk, stack, scores, north, south, q == 0, q == 511)
    for copy in sent:
        copy.wait_send()
    with jax.named_scope("sharpest"):
        sharpest(scores, natural, piece)

    left, right = pl.ds(0, N // 2), pl.ds(N // 2, N // 2)
    halves = (left, right)
    sent = []

    def across(step):
        return {**at, "x": lax.rem(x + step + 4, 4)}

    def along(step):
        return {**at, "zh": lax.rem(zh + step + 4, 4)}

    def row_of(place):
        return lax.rem(place - zl + 4, 4)

    def send(source, target, sem, device):
        sent.append(remote(source, target, send5.at[len(sent)], sem, device))
        sent[-1].start()

    def arrive(place, high_z, half, device):
        slot = out.at[high_z, row_of(place)]
        slot = slot if half is None else slot.at[:, halves[half]]
        sem = recv5.at[place, high_z, half or 0]
        remote(slot, slot, own_sem, sem, device).wait_recv()

    for step in (1, -1):
        send(piece, out.at[zh, xs], recv5.at[x, zh, 0], along(step))
    for step in (1, -1):
        send(piece, out.at[zh, xs], recv5.at[x, zh, 0], across(step))
    own = pltpu.make_async_copy(piece, out.at[zh, xs], own_sem)
    own.start()
    for half, step in enumerate((1, -1)):
        from_z = lax.rem(zh - step + 4, 4)
        arrive(x, from_z, None, along(-step))
        slot = out.at[from_z, xs, :, halves[half]]
        send(slot, slot, recv5.at[x, from_z, half], along(step))
        for turn in (1, -1):
            slot = out.at[from_z, xs]
            send(slot, slot, recv5.at[x, from_z, 0], across(turn))
    far_z = lax.rem(zh + 2, 4)
    for high_z in (zh, lax.rem(zh + 3, 4), lax.rem(zh + 1, 4), far_z):
        if high_z is far_z:
            for half, step in enumerate((1, -1)):
                arrive(x, far_z, half, along(-step))
            for turn in (1, -1):
                slot = out.at[far_z, xs]
                send(slot, slot, recv5.at[x, far_z, 0], across(turn))
        for half, step in enumerate((1, -1)):
            place = lax.rem(x - step + 4, 4)
            arrive(place, high_z, None, across(-step))
            slot = out.at[high_z, row_of(place), :, halves[half]]
            send(slot, slot, recv5.at[place, high_z, half], across(step))
    for high_z in (zh, lax.rem(zh + 3, 4), lax.rem(zh + 1, 4), far_z):
        for half, step in enumerate((1, -1)):
            arrive(lax.rem(x + 2, 4), high_z, half, across(-step))
    own.wait()
    for copy in sent:
        copy.wait_send()


def shards(hologram, background):
    vmem, dma = pltpu.VMEM, pltpu.SemaphoreType.DMA
    table = vmem((RADIX, RADIX, 128), F32)
    merged = pl.pallas_call(
        whole_kernel,
        name="whole",
        out_shape=jax.ShapeDtypeStruct((4, 4, 8, N), BF16),
        in_specs=[pl.BlockSpec(memory_space=vmem)] * 8,
        out_specs=pl.BlockSpec(memory_space=vmem),
        scratch_shapes=[
            vmem((8, 128, 128), BF16),
            vmem((32, 128, 128), BF16),
            vmem((8, 128, 128), BF16),
            vmem((RADIX * WIDE, 128), F32),
            vmem((2 * RADIX * WIDE, 128), F32),
            vmem((2 * RADIX * WIDE, 128), F32),
            table,
            table,
            vmem((N, 128), F32),
            vmem((N, 128), F32),
            vmem((32, CHUNKS, 4, PART, 128), BF16),
            vmem((CHUNKS, 14, 4, PART, 128), BF16),
            vmem((32, CHUNKS, 4, PART, 128), BF16),
            vmem((CHUNKS, 16, 8, LANES), BF16),
            vmem((CHUNKS, 2, 8, LANES // 2), BF16),
            vmem((CHUNKS, PLANES, 8, LANES), BF16),
            vmem((CHUNKS, PLANES, 8, LANES), F32),
            *[vmem((CHUNKS, PLANES, LANES), BF16)] * 4,
            vmem((8, N), BF16),
            dma((31,)),
            dma((32,)),
            dma((8,)),
            dma((8,)),
            dma((CHUNKS, 31)),
            dma((32, CHUNKS)),
            dma((CHUNKS, 14)),
            dma((CHUNKS, 14)),
            dma((CHUNKS, 14)),
            dma((CHUNKS, 16, 2)),
            dma((CHUNKS, 4)),
            dma((CHUNKS, 2)),
            dma((CHUNKS, 2)),
            dma((CHUNKS, 2)),
            dma((20,)),
            dma((4, 4, 2)),
            dma,
        ],
        compiler_params=pltpu.CompilerParams(
            collective_id=0, has_side_effects=True, vmem_limit_bytes=44 << 20
        ),
    )(hologram, background, *pass_tables())
    return merged.reshape(128, N).astype(F32)


def solution(mesh):
    fine = Mesh(mesh.devices.reshape(SIZES), AXES)
    spec = P(("zl", "y", "c"), None)
    return jax.shard_map(
        shards, mesh=fine, in_specs=(spec, spec), out_specs=spec, check_vma=False
    )
```

```python
import math

import jax
import jax.numpy as jnp
import numpy as np
from jax import lax
from jax.experimental import pallas as pl
from jax.experimental.pallas import tpu as pltpu
from jax.sharding import Mesh
from jax.sharding import PartitionSpec as P

N = 4096
RADIX = 64
PLANES = 16
WIDE = 72
DEEP = 136
CHUNKS = 2
PART = RADIX // CHUNKS
LANES = N // CHUNKS
AXES = ("zh", "x", "zl", "y", "c")
SIZES = (4, 4, 4, 4, 2)
MESH = pl.DeviceIdType.MESH
NT = (((1,), (1,)), ((), ()))
F32 = jnp.float32
BF16 = jnp.bfloat16

wave_number = 0.6
depth_start = 8.0
depth_step = 2.0


def fourier_tables(sign_value):
    indices = np.arange(RADIX)
    angles = (indices[:, None] * indices[None, :] % RADIX) * (sign_value * 2.0 * math.pi / RADIX)
    real, imag = np.cos(angles) / math.sqrt(RADIX), np.sin(angles) / math.sqrt(RADIX)
    matrix = np.stack([np.stack([real, -imag]), np.stack([imag, real])])
    return matrix.astype(np.float32)


def twiddle_table(sign_value):
    indices = np.arange(RADIX)
    angles = (indices[:, None] * indices[None, :]) * (sign_value * 2.0 * math.pi / N)
    return np.cos(angles).astype(np.float32), np.sin(angles).astype(np.float32)


def pass_tables():
    ahead, back = fourier_tables(-1.0), fourier_tables(1.0)
    flat = lambda table: table.transpose(0, 2, 1, 3).reshape(128, 128)
    natural = np.eye(128, dtype=np.float32).reshape(2, CHUNKS, PART, 128)
    natural = natural.swapaxes(0, 1).reshape(128, 128)
    both = np.zeros((2, 2, 2, RADIX, 2, 128), np.float32)
    for lane in range(128):
        far, j = divmod(lane, RADIX)
        both[1, :, far, :, :, lane] = back[:, :, :, RADIX - 1 - j if far else j].transpose(0, 2, 1)
        if j >= RADIX // 2:
            half, j = 1, (95 - j if far else j - 32)
        else:
            half, j = 0, ((RADIX - j if j else 32) if far else j)
        both[0, :, half, :, :, lane] = back[:, :, :, j].transpose(0, 2, 1)
    tables = (
        flat(ahead),
        flat(back),
        both.reshape(2, 256, 256),
        np.eye(128, dtype=np.float32),
        natural,
    )
    return [jnp.asarray(ahead[:, 0].reshape(128, RADIX), F32)] + [
        jnp.asarray(table, BF16) for table in tables
    ]


def row_pass(x, hologram, background, open_exact, ahead, eye, wide, middle, sections):
    for t in range(32):
        here = slice(t * 128, (t + 1) * 128)
        ratio = hologram[:, here].astype(F32) / background[:, here].astype(F32)
        contrast = (ratio - 1.0).astype(BF16)
        made = lax.dot_general(eye[...], contrast, NT, preferred_element_type=F32)
        wide[2 * t * WIDE : 2 * t * WIDE + RADIX, :] = made[:RADIX]
        wide[(2 * t + 1) * WIDE : (2 * t + 1) * WIDE + RADIX, :] = made[RADIX:]
    own = pl.multiple_of(x * 8, 8)
    chosen = [open_exact[pl.ds(own, 8), :], open_exact[32:40, :]]
    chosen += [open_exact[pl.ds(RADIX + own, 8), :], open_exact[RADIX + 32 : RADIX + 40, :]]
    matrix = jnp.concatenate(chosen).astype(BF16)
    row = lax.broadcasted_iota(jnp.int32, (16, 128), 0)
    k = jnp.where(row < 8, x * 8 + row, row + 24).astype(F32)

    def opening(b, carry):
        data = wide[pl.ds(b, RADIX, stride=WIDE), :].astype(BF16)
        made = jnp.dot(matrix, data, preferred_element_type=F32)
        real, imag = made[:16], made[16:]
        sine, cosine = sine_cosine(k * (b.astype(F32) / N))
        middle[pl.ds(b, 16, stride=DEEP), :] = real * cosine + imag * sine
        middle[pl.ds(RADIX + b, 16, stride=DEEP), :] = imag * cosine - real * sine
        return carry

    lax.fori_loop(0, RADIX, opening, 0, unroll=16)

    def section(index):
        made = matmul(ahead, middle[index * DEEP : index * DEEP + 128, :].astype(BF16))
        return lax.dot_general(eye[...], made.astype(BF16), NT, preferred_element_type=F32)

    lane = lax.broadcasted_iota(jnp.int32, (128, 128), 1)
    zero, half = section(0), section(8)
    turned = pltpu.roll(zero, 32, 1)
    packed = jnp.where(lax.rem(lane, RADIX) >= 32, pltpu.roll(half, 32, 1), zero)
    packed = jnp.where(lane == RADIX, turned, packed)
    sections[0] = jnp.where(x == 0, packed, zero).astype(BF16)
    for index in range(1, 8):
        sections[index] = section(index).astype(BF16)


def remote(source, target, send_sem, recv_sem, device):
    return pltpu.make_async_remote_copy(
        src_ref=source,
        dst_ref=target,
        send_sem=send_sem,
        recv_sem=recv_sem,
        device_id=device,
        device_id_type=MESH,
    )


def sine_cosine(turns):
    half = (turns - jnp.floor(turns + 0.5)) * math.pi
    square = half * half
    sine, cosine = jnp.zeros_like(half), jnp.zeros_like(half)
    for power in range(6, -1, -1):
        cosine = cosine * square + (-1) ** power / math.factorial(2 * power)
        if power < 6:
            sine = sine * square + (-1) ** power / math.factorial(2 * power + 1)
    sine = sine * half
    return 2.0 * sine * cosine, 1.0 - 2.0 * sine * sine


def make_tables(me, z, cosines, sines, k_real, k_imag):
    distance = depth_start + depth_step * z.astype(F32)
    lane = lax.broadcasted_iota(jnp.int32, (RADIX, 128), 1)
    row = lax.broadcasted_iota(jnp.int32, (RADIX, 128), 0)
    j = lax.rem(lane, RADIX)
    general = me + RADIX * j
    lone = jnp.where(j == 0, jnp.where(lane >= RADIX, N // 2, 0), RADIX * j)
    lone = jnp.where(j >= RADIX // 2, 32 + RADIX * (j - RADIX // 2), lone)
    natural = jnp.where(me == 0, lone, general)
    freq = jnp.where(natural >= N // 2, natural - N, natural).astype(F32) / N
    column_part = freq * freq
    base = jnp.where(row >= RADIX // 2, RADIX * row - N, RADIX * row)
    limit = wave_number * wave_number

    def tile(k, carry):
        here = pl.ds(k * RADIX, RADIX)
        sine, cosine = sine_cosine((row * k).astype(F32) / N)
        cosines[k], sines[k] = cosine, sine
        freq = (base + k).astype(F32) / N
        radial = freq * freq + column_part
        amplitude = jnp.exp(
            (-2.0 * math.pi * distance) * jnp.sqrt(jnp.maximum(radial - limit, 0.0))
        )
        turns = distance * (jnp.sqrt(jnp.maximum(limit - radial, 0.0)) - wave_number)
        sine, cosine = sine_cosine(turns)
        k_real[here, :] = amplitude * cosine
        k_imag[here, :] = amplitude * sine
        return carry

    lax.fori_loop(0, RADIX, tile, 0)


def widen(slab, columns, wide):
    for half in range(2):
        rows = columns[slab, pl.ds(half * RADIX, RADIX), :]
        wide[pl.ds((2 * slab + half) * WIDE, RADIX), :] = rows.astype(F32)


def matmul(matrix, data):
    return jnp.dot(matrix[...], data, preferred_element_type=F32)


def matmul_right(data, matrix):
    return jnp.dot(data, matrix[...], preferred_element_type=F32)


def column_pass(me, tables, wide, middle, other, k_real, k_imag, cosines, sines):
    open_exact, ahead, back = tables
    lane = lax.broadcasted_iota(jnp.int32, (RADIX, 128), 1)
    low = lane < RADIX
    alone = (me == 0) & (lax.rem(lane, RADIX) == 0)

    open_ahead = open_exact[...].astype(BF16)

    def first(b, carry):
        made = matmul(open_ahead, wide[pl.ds(b, RADIX, stride=WIDE), :].astype(BF16))
        real, imag = made[:RADIX], made[RADIX:]
        cosine, sine = cosines[b], sines[b]
        middle[pl.ds(b, RADIX, stride=DEEP), :] = real * cosine + imag * sine
        middle[pl.ds(RADIX + b, RADIX, stride=DEEP), :] = imag * cosine - real * sine
        return carry

    lax.fori_loop(0, RADIX, first, 0, unroll=16)

    def second(k, carry):
        made = matmul(ahead, middle[pl.ds(k * DEEP, 128), :].astype(BF16))
        real, imag = made[:RADIX], made[RADIX:]
        real_turn, imag_turn = pltpu.roll(real, RADIX, 1), pltpu.roll(imag, RADIX, 1)
        spectrum_real = jnp.where(low, real - imag_turn, real_turn + imag)
        spectrum_imag = jnp.where(low, imag + real_turn, imag_turn - real)
        spectrum_real = jnp.where(alone, real, spectrum_real).astype(BF16).astype(F32)
        spectrum_imag = jnp.where(alone, imag, spectrum_imag).astype(BF16).astype(F32)
        here = pl.ds(k * RADIX, RADIX)
        kernel_real, kernel_imag = k_real[here, :], k_imag[here, :]
        propagated = jnp.concatenate(
            [
                spectrum_real * kernel_real - spectrum_imag * kernel_imag,
                spectrum_real * kernel_imag + spectrum_imag * kernel_real,
            ]
        )
        made = matmul(back, propagated.astype(BF16))
        real, imag = made[:RADIX], made[RADIX:]
        cosine, sine = cosines[k], sines[k]
        other[pl.ds(k, RADIX, stride=DEEP), :] = real * cosine - imag * sine
        other[pl.ds(RADIX + k, RADIX, stride=DEEP), :] = real * sine + imag * cosine
        return carry

    lax.fori_loop(0, RADIX, second, 0, unroll=16)

    def third(b, carry):
        made = matmul(back, other[pl.ds(b * DEEP, 128), :].astype(BF16))
        middle[pl.ds(b, RADIX, stride=WIDE), :] = made[:RADIX]
        middle[pl.ds(RADIX * WIDE + b, RADIX, stride=WIDE), :] = made[RADIX:]
        return carry

    lax.fori_loop(0, RADIX, third, 0, unroll=16)


def block_rows(middle, part, x, yc):
    rows = []
    for low_z in range(4):
        start = (part * RADIX + low_z * 16 + yc * 2) * WIDE + lax.rem(x - low_z + 4, 4) * 8
        for zh in range(4):
            offset = pl.multiple_of(start + zh // 2 * WIDE + zh % 2 * 32, 8)
            rows.append(middle[pl.ds(offset, 8), :])
    return jnp.concatenate(rows).astype(BF16)


def partner(k):
    return jnp.where(k == 0, 32, RADIX - k)


def make_block(me, target, both, middle, cosines, sines, blocks):
    x, yc = target // 8, lax.rem(target, 8)
    data = jnp.concatenate([block_rows(middle, part, x, yc) for part in range(2)], axis=1)
    made = lax.dot_general(both[jnp.minimum(me, 1)], data, NT, preferred_element_type=F32)
    for half in range(2):
        k = partner(me) if half else me
        real = made[half * RADIX : (half + 1) * RADIX]
        imag = made[128 + half * RADIX : 128 + (half + 1) * RADIX]
        cosine, sine = cosines[k], sines[k]
        turned = (real * cosine - imag * sine, real * sine + imag * cosine)
        for part in range(2):
            for chunk in range(CHUNKS):
                rows = turned[part][chunk * PART : (chunk + 1) * PART]
                blocks[target, chunk, part * 2 + half] = rows.astype(BF16)


def place_block(source, chunk, gathered, other):
    for part in range(2):
        for half in range(2):
            k = partner(source) if half else source
            rows = gathered[source, chunk, part * 2 + half].astype(F32)
            start = chunk * PART * DEEP + part * RADIX + k
            other[pl.ds(start, PART, stride=DEEP), :] = rows


def close_rows(chunk, back, eye, other, wide, planes):
    def closing(index, carry):
        b = chunk * PART + index
        made = matmul(back, other[pl.ds(b * DEEP, 128), :].astype(BF16))
        real, imag = made[:RADIX], made[RADIX:]
        wide[pl.ds(b, RADIX, stride=WIDE), :] = real * real + imag * imag
        return carry

    lax.fori_loop(0, PART, closing, 0, unroll=16)
    span = 128 // PART
    for t in range(LANES // 128):
        rows = [
            wide[a * WIDE + chunk * PART : a * WIDE + (chunk + 1) * PART, :]
            for a in range(span * t, span * (t + 1))
        ]
        block = jnp.concatenate(rows).astype(BF16)
        made = lax.dot_general(eye[...], block, NT, preferred_element_type=F32)
        here = slice(t * 128, (t + 1) * 128)
        planes[chunk, :, :, here] = made.reshape(16, 8, 128).astype(BF16)


def edge_rows(chunk, stack, low, high):
    rows = lax.broadcasted_iota(jnp.int32, (PLANES, LANES), 0)
    bottom, top = jnp.zeros((PLANES, LANES), F32), jnp.zeros((PLANES, LANES), F32)
    for g in range(PLANES):
        plane = stack[chunk, g].astype(F32)
        bottom = jnp.where(rows == g, plane[0:1], bottom)
        top = jnp.where(rows == g, plane[7:8], top)
    low[chunk] = bottom.astype(BF16)
    high[chunk] = top.astype(BF16)


def depth_scores(chunk, stack, scores):
    def one(g, carry):
        lower = stack[chunk, jnp.maximum(g - 1, 0)].astype(F32)
        upper = stack[chunk, jnp.minimum(g + 1, PLANES - 1)].astype(F32)
        scores[chunk, g] = (upper - lower) * (upper - lower)
        return carry

    lax.fori_loop(0, PLANES, one, 0, unroll=2)


def row_scores(chunk, stack, scores, north, south, first, last):
    row = lax.broadcasted_iota(jnp.int32, (8, LANES), 0)
    norths, souths = north[chunk].astype(F32), south[chunk].astype(F32)
    for g in range(PLANES):
        centre = stack[chunk, g].astype(F32)
        before = jnp.where(first, centre[0:1], norths[g : g + 1])
        after = jnp.where(last, centre[7:8], souths[g : g + 1])
        above = jnp.where(row == 0, before, pltpu.roll(centre, 1, 0))
        below = jnp.where(row == 7, after, pltpu.roll(centre, 7, 0))
        scores[chunk, g] = scores[chunk, g] + (below - above) * (below - above)


def side_scores(chunk, stack, scores):
    lane = lax.broadcasted_iota(jnp.int32, (8, LANES), 1)
    start, end = lax.rem(lane, PART) == 0, lax.rem(lane, PART) == PART - 1

    def one(g, carry):
        centre = stack[chunk, g].astype(F32)
        before = stack[(chunk - 1) % CHUNKS, g].astype(F32)
        after = stack[(chunk + 1) % CHUNKS, g].astype(F32)
        if chunk:
            before = pltpu.roll(before, LANES - PART + 1, 1)
        else:
            before = jnp.where(lane == 0, centre, pltpu.roll(before, 1, 1))
        if chunk < CHUNKS - 1:
            after = pltpu.roll(after, PART - 1, 1)
        else:
            after = jnp.where(lane == LANES - 1, centre, pltpu.roll(after, LANES - 1, 1))
        west = jnp.where(start, before, pltpu.roll(centre, 1, 1))
        east = jnp.where(end, after, pltpu.roll(centre, LANES - 1, 1))
        scores[chunk, g] = scores[chunk, g] + (east - west) * (east - west)
        return carry

    lax.fori_loop(0, PLANES, one, 0, unroll=2)


def sharpest(scores, natural, piece):
    best = [jnp.max(scores[chunk], axis=0) / 8.0 for chunk in range(CHUNKS)]
    width = 128 // CHUNKS
    lane = lax.broadcasted_iota(jnp.int32, (8, 128), 1)
    tiles = []
    for t in range(32):
        here = slice(t // CHUNKS * 128, (t // CHUNKS + 1) * 128)
        made = jnp.zeros((8, 128), F32)
        for chunk in range(CHUNKS):
            shift = (chunk - t) % CHUNKS * width
            moved = best[chunk][:, here]
            moved = pltpu.roll(moved, shift, 1) if shift else moved
            made = jnp.where(lane // width == chunk, moved, made)
        tiles.append(made)
    made = matmul_right(jnp.concatenate(tiles).astype(BF16), natural)
    for t in range(32):
        piece[:, t * 128 : (t + 1) * 128] = made[t * 8 : (t + 1) * 8].astype(BF16)


def whole_kernel(
    hologram_in, background_in, exact_in, ahead_in, back_in, both_in, eye_in, natural_in, out,
    hologram, background, open_exact, ahead, back, both, eye, natural, load_sem,
    sections, columns, passing, wide, middle, other, cosines, sines, k_real, k_imag,
    blocks, staged, gathered, planes, opposite, stack, scores, low, high, north, south, piece,
    send1, recv1, relay1_send, relay1_recv, send2, recv2, relay_send, relay_recv,
    send3, recv3, far_send, far_recv, send4, recv4, send5, recv5, own_sem,
):
    at = {name: lax.axis_index(name) for name in AXES}
    x, y, c, zh, zl = at["x"], at["y"], at["c"], at["zh"], at["zl"]
    yc, z = y * 2 + c, zh * 4 + zl
    me, slab = x * 8 + yc, zl * 8 + yc
    xs = lax.rem(x - zl + 4, 4)
    q = (slab * 4 + zh) * 4 + xs

    def near(dy, dc, turn):
        layer = lax.rem(z + turn + 16, 16)
        return {
            "zh": layer // 4,
            "x": x,
            "zl": lax.rem(layer, 4),
            "y": lax.rem(y + dy + 4, 4),
            "c": lax.rem(c + dc, 2),
        }

    def level(dx, dy, dc):
        return {
            "zh": zh,
            "x": lax.rem(x + dx + 4, 4),
            "zl": zl,
            "y": lax.rem(y + dy + 4, 4),
            "c": lax.rem(c + dc, 2),
        }

    def number(device):
        return device["x"] * 8 + device["y"] * 2 + device["c"]

    def slab_of(device):
        return device["zl"] * 8 + device["y"] * 2 + device["c"]

    def above(layer):
        return {**at, "zh": layer // 4, "zl": lax.rem(layer, 4)}

    def up(turn):
        return lax.rem(z + turn + 16, 16)

    def block_owner(index):
        owner = index // 16
        low_z = owner // 8
        return {
            "zh": lax.rem(index // 4, 4),
            "x": lax.rem(lax.rem(index, 4) + low_z, 4),
            "zl": low_z,
            "y": lax.rem(owner // 2, 4),
            "c": lax.rem(owner, 2),
        }

    moves, hops = [], []
    for turn in (2, 1, -1, 0):
        for dc in (1, 0):
            toward = -2 if turn == 2 and dc else turn
            hops.append((-1 if dc else 1, dc, toward))
            for dy in (1, -1, 0):
                if (dy, dc, turn) != (0, 0, 0):
                    moves.append((dy, dc, toward))
    relayed, direct = [], []
    for dx in (2, 1, 3, 0):
        for dy in (2, 1, 3, 0):
            for dc in (1, 0):
                if 2 in (dx, dy):
                    side = -1 if dc else 1
                    hop = [side if d == 2 else (-1 if d == 3 else d) for d in (dx, dy)]
                    rest = [side if d == 2 else 0 for d in (dx, dy)]
                    relayed.append((hop[0], hop[1], dc, rest[0], rest[1]))
                elif (dx, dy, dc) != (0, 0, 0):
                    direct.append((-1 if dx == 3 else dx, -1 if dy == 3 else dy, dc))
    turns = (7, -7, 6, -6, 5, -5, 4, -4, 3, -3, 2, -2, 1, -1)
    ahead_q, behind_q = block_owner(lax.rem(q + 1, 512)), block_owner(lax.rem(q + 511, 512))

    pairs = (
        (hologram_in, hologram), (background_in, background), (eye_in, eye),
        (exact_in, open_exact), (ahead_in, ahead), (back_in, back), (both_in, both),
        (natural_in, natural),
    )
    loads = [
        pltpu.make_async_copy(source, target, load_sem.at[index])
        for index, (source, target) in enumerate(pairs)
    ]
    for copy in loads:
        copy.start()
    barrier = pltpu.get_barrier_semaphore()
    everyone = [near(-dy, dc, -turn) for dy, dc, turn in moves + hops]
    everyone += [level(dx, dy, dc) for dx in range(4) for dy in range(4) for dc in range(2)][1:]
    everyone += [above(up(turn)) for turn in turns]
    everyone += [ahead_q, behind_q]
    for device in everyone:
        pl.semaphore_signal(barrier, inc=1, device_id=device, device_id_type=MESH)
    for copy in loads:
        copy.wait()
    row_pass(x, hologram, background, open_exact, ahead, eye, wide, middle, sections)
    pl.semaphore_wait(barrier, len(everyone))

    sent = []
    for index, (side, dc, turn) in enumerate(hops):
        target = near(2, dc, turn)
        sent.append(
            remote(
                sections.at[target["y"] * 2 + target["c"]],
                passing.at[index],
                relay1_send.at[index],
                relay1_recv.at[index],
                near(side, dc, turn),
            )
        )
        sent[-1].start()
    for index, (dy, dc, turn) in enumerate(moves):
        target = near(dy, dc, turn)
        sent.append(
            remote(
                sections.at[target["y"] * 2 + target["c"]],
                columns.at[slab],
                send1.at[index],
                recv1.at[slab],
                target,
            )
        )
        sent[-1].start()
    own = pltpu.make_async_copy(sections.at[yc], columns.at[slab], own_sem)
    own.start()
    make_tables(me, z, cosines, sines, k_real, k_imag)
    own.wait()
    widen(slab, columns, wide)
    for index, (side, dc, turn) in enumerate(hops):
        source = near(-side, dc, -turn)
        slot = passing.at[index]
        remote(slot, slot, own_sem, relay1_recv.at[index], source).wait_recv()
        sent.append(
            remote(
                slot,
                columns.at[slab_of(source)],
                send1.at[len(moves) + index],
                recv1.at[slab_of(source)],
                level(0, side, 0),
            )
        )
        sent[-1].start()
    arrivals = [(-dy, dc, -turn) for dy, dc, turn in reversed(moves)]
    arrivals += [(2, dc, -turn) for side, dc, turn in hops]
    for dy, dc, turn in arrivals:
        source = near(dy, dc, turn)
        origin = slab_of(source)
        slot = columns.at[origin]
        remote(slot, slot, own_sem, recv1.at[origin], source).wait_recv()
        widen(origin, columns, wide)
    for copy in sent:
        copy.wait_send()

    tables = (open_exact, ahead, back)
    column_pass(me, tables, wide, middle, other, k_real, k_imag, cosines, sines)

    sent = []

    def send_relayed(chunk, index):
        hx, hy, dc, rx, ry = relayed[index]
        sent.append(
            remote(
                blocks.at[number(level(hx + rx, hy + ry, dc)), chunk],
                staged.at[chunk, index],
                relay_send.at[chunk, index],
                relay_recv.at[chunk, index],
                level(hx, hy, dc),
            )
        )
        sent[-1].start()

    def send_direct(chunk, index):
        device = level(*direct[index])
        sent.append(
            remote(
                blocks.at[number(device), chunk],
                gathered.at[me, chunk],
                send2.at[chunk, index],
                recv2.at[me, chunk],
                device,
            )
        )
        sent[-1].start()

    def make(device):
        make_block(me, number(device), both, middle, cosines, sines, blocks)

    for index, (hx, hy, dc, rx, ry) in enumerate(relayed):
        make(level(hx + rx, hy + ry, dc))
        if index % 2:
            send_relayed(0, index - 1)
            send_relayed(0, index)
    for index, offset in enumerate(direct):
        make(level(*offset))
        if index % 2:
            send_direct(0, index - 1)
            send_direct(0, index)
    send_direct(0, len(direct) - 1)
    make(level(0, 0, 0))
    own = pltpu.make_async_copy(blocks.at[me], gathered.at[me], own_sem)
    own.start()
    own.wait()

    def part(chunk, layer):
        return planes.at[chunk, lax.rem(layer, 4) * 4 + layer // 4]

    lanes = (pl.ds(0, LANES // 2), pl.ds(LANES // 2, LANES // 2))

    def forward_far(chunk):
        for side, turn in enumerate((4, -4)):
            slot = opposite.at[chunk, side]
            remote(slot, slot, own_sem, far_recv.at[chunk, side], above(up(-turn))).wait_recv()
            sent.append(
                remote(
                    slot,
                    stack.at[chunk, up(-turn), :, lanes[side]],
                    far_send.at[chunk, 2 + side],
                    recv3.at[chunk, up(-turn), side],
                    above(up(turn)),
                )
            )
            sent[-1].start()

    for chunk in range(CHUNKS):
        for index, (hx, hy, dc, rx, ry) in enumerate(relayed):
            source = level(-hx, -hy, dc)
            slot = staged.at[chunk, index]
            remote(slot, slot, own_sem, relay_recv.at[chunk, index], source).wait_recv()
            sent.append(
                remote(
                    slot,
                    gathered.at[number(source), chunk],
                    send2.at[chunk, len(direct) + index],
                    recv2.at[number(source), chunk],
                    level(rx, ry, 0),
                )
            )
            sent[-1].start()
        if chunk + 1 < CHUNKS:
            for index in range(len(relayed)):
                send_relayed(chunk + 1, index)
            for index in range(len(direct)):
                send_direct(chunk + 1, index)
        place_block(me, chunk, gathered, other)
        arrivals = [(-dx, -dy, dc) for dx, dy, dc in direct]
        arrivals += [(-hx - rx, -hy - ry, dc) for hx, hy, dc, rx, ry in relayed]
        for dx, dy, dc in arrivals:
            device = level(dx, dy, dc)
            source = number(device)
            slot = gathered.at[source, chunk]
            remote(slot, slot, own_sem, recv2.at[source, chunk], device).wait_recv()
            place_block(source, chunk, gathered, other)
        close_rows(chunk, back, eye, other, wide, planes)
        if chunk:
            forward_far(chunk - 1)
        far = up(8)
        for side, turn in enumerate((4, -4)):
            sent.append(
                remote(
                    part(chunk, far).at[:, lanes[side]],
                    opposite.at[chunk, side],
                    far_send.at[chunk, side],
                    far_recv.at[chunk, side],
                    above(up(turn)),
                )
            )
            sent[-1].start()
        for index, turn in enumerate(turns):
            layer = up(turn)
            sent.append(
                remote(
                    part(chunk, layer),
                    stack.at[chunk, z],
                    send3.at[chunk, index],
                    recv3.at[chunk, z, 0],
                    above(layer),
                )
            )
            sent[-1].start()
        own = pltpu.make_async_copy(part(chunk, z), stack.at[chunk, z], own_sem)
        own.start()
        own.wait()
    forward_far(CHUNKS - 1)

    def edges(chunk):
        edge_rows(chunk, stack, low, high)
        pair = [
            remote(
                high.at[chunk], north.at[chunk],
                send4.at[chunk, 0], recv4.at[chunk, 0], ahead_q,
            ),
            remote(
                low.at[chunk], south.at[chunk],
                send4.at[chunk, 1], recv4.at[chunk, 1], behind_q,
            ),
        ]
        for copy in pair:
            copy.start()
        return pair

    for chunk in range(CHUNKS):
        for turn in reversed(turns):
            slot = stack.at[chunk, up(turn)]
            remote(slot, slot, own_sem, recv3.at[chunk, up(turn), 0], above(up(turn))).wait_recv()
        for side, turn in enumerate((-4, 4)):
            slot = stack.at[chunk, up(8), :, lanes[side]]
            remote(slot, slot, own_sem, recv3.at[chunk, up(8), side], above(up(turn))).wait_recv()
        pair = edges(chunk)
        depth_scores(chunk, stack, scores)
        if chunk > 1:
            side_scores(chunk - 1, stack, scores)
        if chunk == CHUNKS - 1:
            side_scores(0, stack, scores)
            side_scores(chunk, stack, scores)
        for copy in pair:
            copy.wait()
        row_scores(chunk, stack, scores, north, south, q == 0, q == 511)
    for copy in sent:
        copy.wait_send()
    sharpest(scores, natural, piece)

    left, right = pl.ds(0, N // 2), pl.ds(N // 2, N // 2)
    halves = (left, right)
    sent = []

    def across(step):
        return {**at, "x": lax.rem(x + step + 4, 4)}

    def along(step):
        return {**at, "zh": lax.rem(zh + step + 4, 4)}

    def row_of(place):
        return lax.rem(place - zl + 4, 4)

    def send(source, target, sem, device):
        sent.append(remote(source, target, send5.at[len(sent)], sem, device))
        sent[-1].start()

    def arrive(place, high_z, half, device):
        slot = out.at[high_z, row_of(place)]
        slot = slot if half is None else slot.at[:, halves[half]]
        sem = recv5.at[place, high_z, half or 0]
        remote(slot, slot, own_sem, sem, device).wait_recv()

    for step in (1, -1):
        send(piece, out.at[zh, xs], recv5.at[x, zh, 0], along(step))
    for step in (1, -1):
        send(piece, out.at[zh, xs], recv5.at[x, zh, 0], across(step))
    own = pltpu.make_async_copy(piece, out.at[zh, xs], own_sem)
    own.start()
    for half, step in enumerate((1, -1)):
        from_z = lax.rem(zh - step + 4, 4)
        arrive(x, from_z, None, along(-step))
        slot = out.at[from_z, xs, :, halves[half]]
        send(slot, slot, recv5.at[x, from_z, half], along(step))
        for turn in (1, -1):
            slot = out.at[from_z, xs]
            send(slot, slot, recv5.at[x, from_z, 0], across(turn))
    far_z = lax.rem(zh + 2, 4)
    for high_z in (zh, lax.rem(zh + 3, 4), lax.rem(zh + 1, 4), far_z):
        if high_z is far_z:
            for half, step in enumerate((1, -1)):
                arrive(x, far_z, half, along(-step))
            for turn in (1, -1):
                slot = out.at[far_z, xs]
                send(slot, slot, recv5.at[x, far_z, 0], across(turn))
        for half, step in enumerate((1, -1)):
            place = lax.rem(x - step + 4, 4)
            arrive(place, high_z, None, across(-step))
            slot = out.at[high_z, row_of(place), :, halves[half]]
            send(slot, slot, recv5.at[place, high_z, half], across(step))
    for high_z in (zh, lax.rem(zh + 3, 4), lax.rem(zh + 1, 4), far_z):
        for half, step in enumerate((1, -1)):
            arrive(lax.rem(x + 2, 4), high_z, half, across(-step))
    own.wait()
    for copy in sent:
        copy.wait_send()


def shards(hologram, background):
    vmem, dma = pltpu.VMEM, pltpu.SemaphoreType.DMA
    table = vmem((RADIX, RADIX, 128), F32)
    merged = pl.pallas_call(
        whole_kernel,
        name="whole",
        out_shape=jax.ShapeDtypeStruct((4, 4, 8, N), BF16),
        in_specs=[pl.BlockSpec(memory_space=pltpu.HBM)] * 8,
        out_specs=pl.BlockSpec(memory_space=vmem),
        scratch_shapes=[
            vmem((128, N), BF16),
            vmem((128, N), BF16),
            vmem((128, RADIX), F32),
            vmem((128, 128), BF16),
            vmem((128, 128), BF16),
            vmem((2, 256, 256), BF16),
            vmem((128, 128), BF16),
            vmem((128, 128), BF16),
            dma((8,)),
            vmem((8, 128, 128), BF16),
            vmem((32, 128, 128), BF16),
            vmem((8, 128, 128), BF16),
            vmem((RADIX * WIDE, 128), F32),
            vmem((2 * RADIX * WIDE, 128), F32),
            vmem((2 * RADIX * WIDE, 128), F32),
            table,
            table,
            vmem((N, 128), F32),
            vmem((N, 128), F32),
            vmem((32, CHUNKS, 4, PART, 128), BF16),
            vmem((CHUNKS, 14, 4, PART, 128), BF16),
            vmem((32, CHUNKS, 4, PART, 128), BF16),
            vmem((CHUNKS, 16, 8, LANES), BF16),
            vmem((CHUNKS, 2, 8, LANES // 2), BF16),
            vmem((CHUNKS, PLANES, 8, LANES), BF16),
            vmem((CHUNKS, PLANES, 8, LANES), F32),
            *[vmem((CHUNKS, PLANES, LANES), BF16)] * 4,
            vmem((8, N), BF16),
            dma((31,)),
            dma((32,)),
            dma((8,)),
            dma((8,)),
            dma((CHUNKS, 31)),
            dma((32, CHUNKS)),
            dma((CHUNKS, 14)),
            dma((CHUNKS, 14)),
            dma((CHUNKS, 14)),
            dma((CHUNKS, 16, 2)),
            dma((CHUNKS, 4)),
            dma((CHUNKS, 2)),
            dma((CHUNKS, 2)),
            dma((CHUNKS, 2)),
            dma((20,)),
            dma((4, 4, 2)),
            dma,
        ],
        compiler_params=pltpu.CompilerParams(
            collective_id=0, has_side_effects=True, vmem_limit_bytes=65400000
        ),
    )(hologram, background, *pass_tables())
    return merged.reshape(128, N).astype(F32)


def solution(mesh):
    fine = Mesh(mesh.devices.reshape(SIZES), AXES)
    spec = P(("zl", "y", "c"), None)
    return jax.shard_map(
        shards, mesh=fine, in_specs=(spec, spec), out_specs=spec, check_vma=False
    )
```

```python
import math

import jax
import jax.numpy as jnp
import numpy as np
from jax import lax
from jax.experimental import pallas as pl
from jax.experimental.pallas import tpu as pltpu
from jax.sharding import Mesh
from jax.sharding import PartitionSpec as P

N = 4096
RADIX = 64
PLANES = 16
WIDE = 72
DEEP = 136
CHUNKS = 4
PART = RADIX // CHUNKS
LANES = N // CHUNKS
AXES = ("zh", "x", "zl", "y", "c")
SIZES = (4, 4, 4, 4, 2)
MESH = pl.DeviceIdType.MESH
NT = (((1,), (1,)), ((), ()))
F32 = jnp.float32
BF16 = jnp.bfloat16

wave_number = 0.6
depth_start = 8.0
depth_step = 2.0


def fourier_tables(sign_value):
    indices = np.arange(RADIX)
    angles = (indices[:, None] * indices[None, :] % RADIX) * (sign_value * 2.0 * math.pi / RADIX)
    real, imag = np.cos(angles) / math.sqrt(RADIX), np.sin(angles) / math.sqrt(RADIX)
    matrix = np.stack([np.stack([real, -imag]), np.stack([imag, real])])
    return matrix.astype(np.float32)


def twiddle_table(sign_value):
    indices = np.arange(RADIX)
    angles = (indices[:, None] * indices[None, :]) * (sign_value * 2.0 * math.pi / N)
    return np.cos(angles).astype(np.float32), np.sin(angles).astype(np.float32)


def pass_tables():
    ahead, back = fourier_tables(-1.0), fourier_tables(1.0)
    flat = lambda table: table.transpose(0, 2, 1, 3).reshape(128, 128)
    natural = np.eye(128, dtype=np.float32).reshape(2, CHUNKS, PART, 128)
    natural = natural.swapaxes(0, 1).reshape(128, 128)
    both = np.zeros((2, 2, 2, RADIX, 2, 128), np.float32)
    for lane in range(128):
        far, j = divmod(lane, RADIX)
        both[1, :, far, :, :, lane] = back[:, :, :, RADIX - 1 - j if far else j].transpose(0, 2, 1)
        if j >= RADIX // 2:
            half, j = 1, (95 - j if far else j - 32)
        else:
            half, j = 0, ((RADIX - j if j else 32) if far else j)
        both[0, :, half, :, :, lane] = back[:, :, :, j].transpose(0, 2, 1)
    tables = (
        flat(ahead),
        flat(back),
        both.reshape(2, 256, 256),
        np.eye(128, dtype=np.float32),
        natural,
    )
    return [jnp.asarray(ahead[:, 0].reshape(128, RADIX), F32)] + [
        jnp.asarray(table, BF16) for table in tables
    ]


def row_pass(x, hologram, background, open_exact, ahead, eye, wide, middle, sections):
    for t in range(32):
        here = slice(t * 128, (t + 1) * 128)
        ratio = hologram[:, here].astype(F32) / background[:, here].astype(F32)
        contrast = (ratio - 1.0).astype(BF16)
        made = lax.dot_general(eye[...], contrast, NT, preferred_element_type=F32)
        wide[2 * t * WIDE : 2 * t * WIDE + RADIX, :] = made[:RADIX]
        wide[(2 * t + 1) * WIDE : (2 * t + 1) * WIDE + RADIX, :] = made[RADIX:]
    own = pl.multiple_of(x * 8, 8)
    chosen = [open_exact[pl.ds(own, 8), :], open_exact[32:40, :]]
    chosen += [open_exact[pl.ds(RADIX + own, 8), :], open_exact[RADIX + 32 : RADIX + 40, :]]
    matrix = jnp.concatenate(chosen).astype(BF16)
    row = lax.broadcasted_iota(jnp.int32, (16, 128), 0)
    k = jnp.where(row < 8, x * 8 + row, row + 24).astype(F32)

    def opening(b, carry):
        data = wide[pl.ds(b, RADIX, stride=WIDE), :].astype(BF16)
        made = jnp.dot(matrix, data, preferred_element_type=F32)
        real, imag = made[:16], made[16:]
        sine, cosine = sine_cosine(k * (b.astype(F32) / N))
        middle[pl.ds(b, 16, stride=DEEP), :] = real * cosine + imag * sine
        middle[pl.ds(RADIX + b, 16, stride=DEEP), :] = imag * cosine - real * sine
        return carry

    lax.fori_loop(0, RADIX, opening, 0, unroll=16)

    def section(index):
        made = matmul(ahead, middle[index * DEEP : index * DEEP + 128, :].astype(BF16))
        return lax.dot_general(eye[...], made.astype(BF16), NT, preferred_element_type=F32)

    lane = lax.broadcasted_iota(jnp.int32, (128, 128), 1)
    zero, half = section(0), section(8)
    turned = pltpu.roll(zero, 32, 1)
    packed = jnp.where(lax.rem(lane, RADIX) >= 32, pltpu.roll(half, 32, 1), zero)
    packed = jnp.where(lane == RADIX, turned, packed)
    sections[0] = jnp.where(x == 0, packed, zero).astype(BF16)
    for index in range(1, 8):
        sections[index] = section(index).astype(BF16)


def remote(source, target, send_sem, recv_sem, device):
    return pltpu.make_async_remote_copy(
        src_ref=source,
        dst_ref=target,
        send_sem=send_sem,
        recv_sem=recv_sem,
        device_id=device,
        device_id_type=MESH,
    )


def sine_cosine(turns):
    half = (turns - jnp.floor(turns + 0.5)) * math.pi
    square = half * half
    sine, cosine = jnp.zeros_like(half), jnp.zeros_like(half)
    for power in range(6, -1, -1):
        cosine = cosine * square + (-1) ** power / math.factorial(2 * power)
        if power < 6:
            sine = sine * square + (-1) ** power / math.factorial(2 * power + 1)
    sine = sine * half
    return 2.0 * sine * cosine, 1.0 - 2.0 * sine * sine


def make_tables(me, z, cosines, sines, k_real, k_imag):
    distance = depth_start + depth_step * z.astype(F32)
    lane = lax.broadcasted_iota(jnp.int32, (RADIX, 128), 1)
    row = lax.broadcasted_iota(jnp.int32, (RADIX, 128), 0)
    j = lax.rem(lane, RADIX)
    general = me + RADIX * j
    lone = jnp.where(j == 0, jnp.where(lane >= RADIX, N // 2, 0), RADIX * j)
    lone = jnp.where(j >= RADIX // 2, 32 + RADIX * (j - RADIX // 2), lone)
    natural = jnp.where(me == 0, lone, general)
    freq = jnp.where(natural >= N // 2, natural - N, natural).astype(F32) / N
    column_part = freq * freq
    base = jnp.where(row >= RADIX // 2, RADIX * row - N, RADIX * row)
    limit = wave_number * wave_number

    def tile(k, carry):
        here = pl.ds(k * RADIX, RADIX)
        sine, cosine = sine_cosine((row * k).astype(F32) / N)
        cosines[k], sines[k] = cosine, sine
        freq = (base + k).astype(F32) / N
        radial = freq * freq + column_part
        amplitude = jnp.exp(
            (-2.0 * math.pi * distance) * jnp.sqrt(jnp.maximum(radial - limit, 0.0))
        )
        turns = distance * (jnp.sqrt(jnp.maximum(limit - radial, 0.0)) - wave_number)
        sine, cosine = sine_cosine(turns)
        k_real[here, :] = amplitude * cosine
        k_imag[here, :] = amplitude * sine
        return carry

    lax.fori_loop(0, RADIX, tile, 0)


def widen(slab, columns, wide):
    for half in range(2):
        rows = columns[slab, pl.ds(half * RADIX, RADIX), :]
        wide[pl.ds((2 * slab + half) * WIDE, RADIX), :] = rows.astype(F32)


def matmul(matrix, data):
    return jnp.dot(matrix[...], data, preferred_element_type=F32)


def matmul_right(data, matrix):
    return jnp.dot(data, matrix[...], preferred_element_type=F32)


def column_pass(me, tables, wide, middle, other, k_real, k_imag, cosines, sines):
    open_exact, ahead, back = tables
    lane = lax.broadcasted_iota(jnp.int32, (RADIX, 128), 1)
    low = lane < RADIX
    alone = (me == 0) & (lax.rem(lane, RADIX) == 0)

    open_ahead = open_exact[...].astype(BF16)

    def first(b, carry):
        made = matmul(open_ahead, wide[pl.ds(b, RADIX, stride=WIDE), :].astype(BF16))
        real, imag = made[:RADIX], made[RADIX:]
        cosine, sine = cosines[b], sines[b]
        middle[pl.ds(b, RADIX, stride=DEEP), :] = real * cosine + imag * sine
        middle[pl.ds(RADIX + b, RADIX, stride=DEEP), :] = imag * cosine - real * sine
        return carry

    lax.fori_loop(0, RADIX, first, 0, unroll=16)

    def second(k, carry):
        made = matmul(ahead, middle[pl.ds(k * DEEP, 128), :].astype(BF16))
        real, imag = made[:RADIX], made[RADIX:]
        real_turn, imag_turn = pltpu.roll(real, RADIX, 1), pltpu.roll(imag, RADIX, 1)
        spectrum_real = jnp.where(low, real - imag_turn, real_turn + imag)
        spectrum_imag = jnp.where(low, imag + real_turn, imag_turn - real)
        spectrum_real = jnp.where(alone, real, spectrum_real).astype(BF16).astype(F32)
        spectrum_imag = jnp.where(alone, imag, spectrum_imag).astype(BF16).astype(F32)
        here = pl.ds(k * RADIX, RADIX)
        kernel_real, kernel_imag = k_real[here, :], k_imag[here, :]
        propagated = jnp.concatenate(
            [
                spectrum_real * kernel_real - spectrum_imag * kernel_imag,
                spectrum_real * kernel_imag + spectrum_imag * kernel_real,
            ]
        )
        made = matmul(back, propagated.astype(BF16))
        real, imag = made[:RADIX], made[RADIX:]
        cosine, sine = cosines[k], sines[k]
        other[pl.ds(k, RADIX, stride=DEEP), :] = real * cosine - imag * sine
        other[pl.ds(RADIX + k, RADIX, stride=DEEP), :] = real * sine + imag * cosine
        return carry

    lax.fori_loop(0, RADIX, second, 0, unroll=16)

    def third(b, carry):
        made = matmul(back, other[pl.ds(b * DEEP, 128), :].astype(BF16))
        middle[pl.ds(b, RADIX, stride=WIDE), :] = made[:RADIX]
        middle[pl.ds(RADIX * WIDE + b, RADIX, stride=WIDE), :] = made[RADIX:]
        return carry

    lax.fori_loop(0, RADIX, third, 0, unroll=16)


def block_rows(middle, part, x, yc):
    rows = []
    for low_z in range(4):
        start = (part * RADIX + low_z * 16 + yc * 2) * WIDE + lax.rem(x - low_z + 4, 4) * 8
        for zh in range(4):
            offset = pl.multiple_of(start + zh // 2 * WIDE + zh % 2 * 32, 8)
            rows.append(middle[pl.ds(offset, 8), :])
    return jnp.concatenate(rows).astype(BF16)


def partner(k):
    return jnp.where(k == 0, 32, RADIX - k)


def make_block(me, target, both, middle, cosines, sines, blocks):
    x, yc = target // 8, lax.rem(target, 8)
    data = jnp.concatenate([block_rows(middle, part, x, yc) for part in range(2)], axis=1)
    made = lax.dot_general(both[jnp.minimum(me, 1)], data, NT, preferred_element_type=F32)
    for half in range(2):
        k = partner(me) if half else me
        real = made[half * RADIX : (half + 1) * RADIX]
        imag = made[128 + half * RADIX : 128 + (half + 1) * RADIX]
        cosine, sine = cosines[k], sines[k]
        turned = (real * cosine - imag * sine, real * sine + imag * cosine)
        for part in range(2):
            for chunk in range(CHUNKS):
                rows = turned[part][chunk * PART : (chunk + 1) * PART]
                blocks[target, chunk, part * 2 + half] = rows.astype(BF16)


def place_block(source, chunk, gathered, other):
    for part in range(2):
        for half in range(2):
            k = partner(source) if half else source
            rows = gathered[source, chunk, part * 2 + half].astype(F32)
            start = chunk * PART * DEEP + part * RADIX + k
            other[pl.ds(start, PART, stride=DEEP), :] = rows


def close_rows(chunk, back, eye, other, wide, planes):
    def closing(index, carry):
        b = chunk * PART + index
        made = matmul(back, other[pl.ds(b * DEEP, 128), :].astype(BF16))
        real, imag = made[:RADIX], made[RADIX:]
        wide[pl.ds(b, RADIX, stride=WIDE), :] = real * real + imag * imag
        return carry

    lax.fori_loop(0, PART, closing, 0, unroll=16)
    span = 128 // PART
    for t in range(LANES // 128):
        rows = [
            wide[a * WIDE + chunk * PART : a * WIDE + (chunk + 1) * PART, :]
            for a in range(span * t, span * (t + 1))
        ]
        block = jnp.concatenate(rows).astype(BF16)
        made = lax.dot_general(eye[...], block, NT, preferred_element_type=F32)
        here = slice(t * 128, (t + 1) * 128)
        planes[chunk, :, :, here] = made.reshape(16, 8, 128).astype(BF16)


def edge_rows(chunk, stack, low, high):
    rows = lax.broadcasted_iota(jnp.int32, (PLANES, LANES), 0)
    bottom, top = jnp.zeros((PLANES, LANES), F32), jnp.zeros((PLANES, LANES), F32)
    for g in range(PLANES):
        plane = stack[chunk, g].astype(F32)
        bottom = jnp.where(rows == g, plane[0:1], bottom)
        top = jnp.where(rows == g, plane[7:8], top)
    low[chunk] = bottom.astype(BF16)
    high[chunk] = top.astype(BF16)


def depth_scores(chunk, stack, scores):
    def one(g, carry):
        lower = stack[chunk, jnp.maximum(g - 1, 0)].astype(F32)
        upper = stack[chunk, jnp.minimum(g + 1, PLANES - 1)].astype(F32)
        scores[chunk, g] = (upper - lower) * (upper - lower)
        return carry

    lax.fori_loop(0, PLANES, one, 0, unroll=2)


def row_scores(chunk, stack, scores, north, south, first, last):
    row = lax.broadcasted_iota(jnp.int32, (8, LANES), 0)
    norths, souths = north[chunk].astype(F32), south[chunk].astype(F32)
    for g in range(PLANES):
        centre = stack[chunk, g].astype(F32)
        before = jnp.where(first, centre[0:1], norths[g : g + 1])
        after = jnp.where(last, centre[7:8], souths[g : g + 1])
        above = jnp.where(row == 0, before, pltpu.roll(centre, 1, 0))
        below = jnp.where(row == 7, after, pltpu.roll(centre, 7, 0))
        scores[chunk, g] = scores[chunk, g] + (below - above) * (below - above)


def side_scores(chunk, stack, scores):
    lane = lax.broadcasted_iota(jnp.int32, (8, LANES), 1)
    start, end = lax.rem(lane, PART) == 0, lax.rem(lane, PART) == PART - 1

    def one(g, carry):
        centre = stack[chunk, g].astype(F32)
        before = stack[(chunk - 1) % CHUNKS, g].astype(F32)
        after = stack[(chunk + 1) % CHUNKS, g].astype(F32)
        if chunk:
            before = pltpu.roll(before, LANES - PART + 1, 1)
        else:
            before = jnp.where(lane == 0, centre, pltpu.roll(before, 1, 1))
        if chunk < CHUNKS - 1:
            after = pltpu.roll(after, PART - 1, 1)
        else:
            after = jnp.where(lane == LANES - 1, centre, pltpu.roll(after, LANES - 1, 1))
        west = jnp.where(start, before, pltpu.roll(centre, 1, 1))
        east = jnp.where(end, after, pltpu.roll(centre, LANES - 1, 1))
        scores[chunk, g] = scores[chunk, g] + (east - west) * (east - west)
        return carry

    lax.fori_loop(0, PLANES, one, 0, unroll=2)


def sharpest(scores, natural, piece):
    best = [jnp.max(scores[chunk], axis=0) / 8.0 for chunk in range(CHUNKS)]
    width = 128 // CHUNKS
    lane = lax.broadcasted_iota(jnp.int32, (8, 128), 1)
    tiles = []
    for t in range(32):
        here = slice(t // CHUNKS * 128, (t // CHUNKS + 1) * 128)
        made = jnp.zeros((8, 128), F32)
        for chunk in range(CHUNKS):
            shift = (chunk - t) % CHUNKS * width
            moved = best[chunk][:, here]
            moved = pltpu.roll(moved, shift, 1) if shift else moved
            made = jnp.where(lane // width == chunk, moved, made)
        tiles.append(made)
    made = matmul_right(jnp.concatenate(tiles).astype(BF16), natural)
    for t in range(32):
        piece[:, t * 128 : (t + 1) * 128] = made[t * 8 : (t + 1) * 8].astype(BF16)


def whole_kernel(
    hologram_in, background_in, exact_in, ahead_in, back_in, both_in, eye_in, natural_in, out,
    hologram, background, open_exact, ahead, back, both, eye, natural, load_sem,
    sections, columns, passing, wide, middle, other, cosines, sines, k_real, k_imag,
    blocks, staged, gathered, planes, opposite, stack, scores, low, high, north, south, piece,
    send1, recv1, relay1_send, relay1_recv, send2, recv2, relay_send, relay_recv,
    send3, recv3, far_send, far_recv, send4, recv4, send5, recv5, own_sem,
):
    at = {name: lax.axis_index(name) for name in AXES}
    x, y, c, zh, zl = at["x"], at["y"], at["c"], at["zh"], at["zl"]
    yc, z = y * 2 + c, zh * 4 + zl
    me, slab = x * 8 + yc, zl * 8 + yc
    xs = lax.rem(x - zl + 4, 4)
    q = (slab * 4 + zh) * 4 + xs

    def near(dy, dc, turn):
        layer = lax.rem(z + turn + 16, 16)
        return {
            "zh": layer // 4,
            "x": x,
            "zl": lax.rem(layer, 4),
            "y": lax.rem(y + dy + 4, 4),
            "c": lax.rem(c + dc, 2),
        }

    def level(dx, dy, dc):
        return {
            "zh": zh,
            "x": lax.rem(x + dx + 4, 4),
            "zl": zl,
            "y": lax.rem(y + dy + 4, 4),
            "c": lax.rem(c + dc, 2),
        }

    def number(device):
        return device["x"] * 8 + device["y"] * 2 + device["c"]

    def slab_of(device):
        return device["zl"] * 8 + device["y"] * 2 + device["c"]

    def above(layer):
        return {**at, "zh": layer // 4, "zl": lax.rem(layer, 4)}

    def up(turn):
        return lax.rem(z + turn + 16, 16)

    def block_owner(index):
        owner = index // 16
        low_z = owner // 8
        return {
            "zh": lax.rem(index // 4, 4),
            "x": lax.rem(lax.rem(index, 4) + low_z, 4),
            "zl": low_z,
            "y": lax.rem(owner // 2, 4),
            "c": lax.rem(owner, 2),
        }

    moves, hops = [], []
    for turn in (2, 1, -1, 0):
        for dc in (1, 0):
            toward = -2 if turn == 2 and dc else turn
            hops.append((-1 if dc else 1, dc, toward))
            for dy in (1, -1, 0):
                if (dy, dc, turn) != (0, 0, 0):
                    moves.append((dy, dc, toward))
    relayed, direct = [], []
    for dx in (2, 1, 3, 0):
        for dy in (2, 1, 3, 0):
            for dc in (1, 0):
                if 2 in (dx, dy):
                    side = -1 if dc else 1
                    hop = [side if d == 2 else (-1 if d == 3 else d) for d in (dx, dy)]
                    rest = [side if d == 2 else 0 for d in (dx, dy)]
                    relayed.append((hop[0], hop[1], dc, rest[0], rest[1]))
                elif (dx, dy, dc) != (0, 0, 0):
                    direct.append((-1 if dx == 3 else dx, -1 if dy == 3 else dy, dc))
    turns = (7, -7, 6, -6, 5, -5, 4, -4, 3, -3, 2, -2, 1, -1)
    ahead_q, behind_q = block_owner(lax.rem(q + 1, 512)), block_owner(lax.rem(q + 511, 512))

    pairs = (
        (hologram_in, hologram), (background_in, background), (eye_in, eye),
        (exact_in, open_exact), (ahead_in, ahead), (back_in, back), (both_in, both),
        (natural_in, natural),
    )
    loads = [
        pltpu.make_async_copy(source, target, load_sem.at[index])
        for index, (source, target) in enumerate(pairs)
    ]
    for copy in loads:
        copy.start()
    barrier = pltpu.get_barrier_semaphore()
    everyone = [near(-dy, dc, -turn) for dy, dc, turn in moves + hops]
    everyone += [level(dx, dy, dc) for dx in range(4) for dy in range(4) for dc in range(2)][1:]
    everyone += [above(up(turn)) for turn in turns]
    everyone += [ahead_q, behind_q]
    for device in everyone:
        pl.semaphore_signal(barrier, inc=1, device_id=device, device_id_type=MESH)
    for copy in loads:
        copy.wait()
    row_pass(x, hologram, background, open_exact, ahead, eye, wide, middle, sections)
    pl.semaphore_wait(barrier, len(everyone))

    sent = []
    for index, (side, dc, turn) in enumerate(hops):
        target = near(2, dc, turn)
        sent.append(
            remote(
                sections.at[target["y"] * 2 + target["c"]],
                passing.at[index],
                relay1_send.at[index],
                relay1_recv.at[index],
                near(side, dc, turn),
            )
        )
        sent[-1].start()
    for index, (dy, dc, turn) in enumerate(moves):
        target = near(dy, dc, turn)
        sent.append(
            remote(
                sections.at[target["y"] * 2 + target["c"]],
                columns.at[slab],
                send1.at[index],
                recv1.at[slab],
                target,
            )
        )
        sent[-1].start()
    own = pltpu.make_async_copy(sections.at[yc], columns.at[slab], own_sem)
    own.start()
    make_tables(me, z, cosines, sines, k_real, k_imag)
    own.wait()
    widen(slab, columns, wide)
    for index, (side, dc, turn) in enumerate(hops):
        source = near(-side, dc, -turn)
        slot = passing.at[index]
        remote(slot, slot, own_sem, relay1_recv.at[index], source).wait_recv()
        sent.append(
            remote(
                slot,
                columns.at[slab_of(source)],
                send1.at[len(moves) + index],
                recv1.at[slab_of(source)],
                level(0, side, 0),
            )
        )
        sent[-1].start()
    arrivals = [(-dy, dc, -turn) for dy, dc, turn in reversed(moves)]
    arrivals += [(2, dc, -turn) for side, dc, turn in hops]
    for dy, dc, turn in arrivals:
        source = near(dy, dc, turn)
        origin = slab_of(source)
        slot = columns.at[origin]
        remote(slot, slot, own_sem, recv1.at[origin], source).wait_recv()
        widen(origin, columns, wide)
    for copy in sent:
        copy.wait_send()

    tables = (open_exact, ahead, back)
    column_pass(me, tables, wide, middle, other, k_real, k_imag, cosines, sines)

    sent = []

    def send_relayed(chunk, index):
        hx, hy, dc, rx, ry = relayed[index]
        sent.append(
            remote(
                blocks.at[number(level(hx + rx, hy + ry, dc)), chunk],
                staged.at[chunk, index],
                relay_send.at[chunk, index],
                relay_recv.at[chunk, index],
                level(hx, hy, dc),
            )
        )
        sent[-1].start()

    def send_direct(chunk, index):
        device = level(*direct[index])
        sent.append(
            remote(
                blocks.at[number(device), chunk],
                gathered.at[me, chunk],
                send2.at[chunk, index],
                recv2.at[me, chunk],
                device,
            )
        )
        sent[-1].start()

    def make(device):
        make_block(me, number(device), both, middle, cosines, sines, blocks)

    for index, (hx, hy, dc, rx, ry) in enumerate(relayed):
        make(level(hx + rx, hy + ry, dc))
        if index % 2:
            send_relayed(0, index - 1)
            send_relayed(0, index)
    for index, offset in enumerate(direct):
        make(level(*offset))
        if index % 2:
            send_direct(0, index - 1)
            send_direct(0, index)
    send_direct(0, len(direct) - 1)
    make(level(0, 0, 0))
    own = pltpu.make_async_copy(blocks.at[me], gathered.at[me], own_sem)
    own.start()
    own.wait()

    def part(chunk, layer):
        return planes.at[chunk, lax.rem(layer, 4) * 4 + layer // 4]

    lanes = (pl.ds(0, LANES // 2), pl.ds(LANES // 2, LANES // 2))

    def forward_far(chunk):
        for side, turn in enumerate((4, -4)):
            slot = opposite.at[chunk, side]
            remote(slot, slot, own_sem, far_recv.at[chunk, side], above(up(-turn))).wait_recv()
            sent.append(
                remote(
                    slot,
                    stack.at[chunk, up(-turn), :, lanes[side]],
                    far_send.at[chunk, 2 + side],
                    recv3.at[chunk, up(-turn), side],
                    above(up(turn)),
                )
            )
            sent[-1].start()

    for chunk in range(CHUNKS):
        for index, (hx, hy, dc, rx, ry) in enumerate(relayed):
            source = level(-hx, -hy, dc)
            slot = staged.at[chunk, index]
            remote(slot, slot, own_sem, relay_recv.at[chunk, index], source).wait_recv()
            sent.append(
                remote(
                    slot,
                    gathered.at[number(source), chunk],
                    send2.at[chunk, len(direct) + index],
                    recv2.at[number(source), chunk],
                    level(rx, ry, 0),
                )
            )
            sent[-1].start()
        if chunk + 1 < CHUNKS:
            for index in range(len(relayed)):
                send_relayed(chunk + 1, index)
            for index in range(len(direct)):
                send_direct(chunk + 1, index)
        place_block(me, chunk, gathered, other)
        arrivals = [(-dx, -dy, dc) for dx, dy, dc in direct]
        arrivals += [(-hx - rx, -hy - ry, dc) for hx, hy, dc, rx, ry in relayed]
        for dx, dy, dc in arrivals:
            device = level(dx, dy, dc)
            source = number(device)
            slot = gathered.at[source, chunk]
            remote(slot, slot, own_sem, recv2.at[source, chunk], device).wait_recv()
            place_block(source, chunk, gathered, other)
        close_rows(chunk, back, eye, other, wide, planes)
        if chunk:
            forward_far(chunk - 1)
        far = up(8)
        for side, turn in enumerate((4, -4)):
            sent.append(
                remote(
                    part(chunk, far).at[:, lanes[side]],
                    opposite.at[chunk, side],
                    far_send.at[chunk, side],
                    far_recv.at[chunk, side],
                    above(up(turn)),
                )
            )
            sent[-1].start()
        for index, turn in enumerate(turns):
            layer = up(turn)
            sent.append(
                remote(
                    part(chunk, layer),
                    stack.at[chunk, z],
                    send3.at[chunk, index],
                    recv3.at[chunk, z, 0],
                    above(layer),
                )
            )
            sent[-1].start()
        own = pltpu.make_async_copy(part(chunk, z), stack.at[chunk, z], own_sem)
        own.start()
        own.wait()
    forward_far(CHUNKS - 1)

    def edges(chunk):
        edge_rows(chunk, stack, low, high)
        pair = [
            remote(
                high.at[chunk], north.at[chunk],
                send4.at[chunk, 0], recv4.at[chunk, 0], ahead_q,
            ),
            remote(
                low.at[chunk], south.at[chunk],
                send4.at[chunk, 1], recv4.at[chunk, 1], behind_q,
            ),
        ]
        for copy in pair:
            copy.start()
        return pair

    for chunk in range(CHUNKS):
        for turn in reversed(turns):
            slot = stack.at[chunk, up(turn)]
            remote(slot, slot, own_sem, recv3.at[chunk, up(turn), 0], above(up(turn))).wait_recv()
        for side, turn in enumerate((-4, 4)):
            slot = stack.at[chunk, up(8), :, lanes[side]]
            remote(slot, slot, own_sem, recv3.at[chunk, up(8), side], above(up(turn))).wait_recv()
        pair = edges(chunk)
        depth_scores(chunk, stack, scores)
        if chunk > 1:
            side_scores(chunk - 1, stack, scores)
        if chunk == CHUNKS - 1:
            side_scores(0, stack, scores)
            side_scores(chunk, stack, scores)
        for copy in pair:
            copy.wait()
        row_scores(chunk, stack, scores, north, south, q == 0, q == 511)
    for copy in sent:
        copy.wait_send()
    sharpest(scores, natural, piece)

    left, right = pl.ds(0, N // 2), pl.ds(N // 2, N // 2)
    halves = (left, right)
    sent = []

    def across(step):
        return {**at, "x": lax.rem(x + step + 4, 4)}

    def along(step):
        return {**at, "zh": lax.rem(zh + step + 4, 4)}

    def row_of(place):
        return lax.rem(place - zl + 4, 4)

    def send(source, target, sem, device):
        sent.append(remote(source, target, send5.at[len(sent)], sem, device))
        sent[-1].start()

    def arrive(place, high_z, half, device):
        slot = out.at[high_z, row_of(place)]
        slot = slot if half is None else slot.at[:, halves[half]]
        sem = recv5.at[place, high_z, half or 0]
        remote(slot, slot, own_sem, sem, device).wait_recv()

    for step in (1, -1):
        send(piece, out.at[zh, xs], recv5.at[x, zh, 0], along(step))
    for step in (1, -1):
        send(piece, out.at[zh, xs], recv5.at[x, zh, 0], across(step))
    own = pltpu.make_async_copy(piece, out.at[zh, xs], own_sem)
    own.start()
    for half, step in enumerate((1, -1)):
        from_z = lax.rem(zh - step + 4, 4)
        arrive(x, from_z, None, along(-step))
        slot = out.at[from_z, xs, :, halves[half]]
        send(slot, slot, recv5.at[x, from_z, half], along(step))
        for turn in (1, -1):
            slot = out.at[from_z, xs]
            send(slot, slot, recv5.at[x, from_z, 0], across(turn))
    far_z = lax.rem(zh + 2, 4)
    for high_z in (zh, lax.rem(zh + 3, 4), lax.rem(zh + 1, 4), far_z):
        if high_z is far_z:
            for half, step in enumerate((1, -1)):
                arrive(x, far_z, half, along(-step))
            for turn in (1, -1):
                slot = out.at[far_z, xs]
                send(slot, slot, recv5.at[x, far_z, 0], across(turn))
        for half, step in enumerate((1, -1)):
            place = lax.rem(x - step + 4, 4)
            arrive(place, high_z, None, across(-step))
            slot = out.at[high_z, row_of(place), :, halves[half]]
            send(slot, slot, recv5.at[place, high_z, half], across(step))
    for high_z in (zh, lax.rem(zh + 3, 4), lax.rem(zh + 1, 4), far_z):
        for half, step in enumerate((1, -1)):
            arrive(lax.rem(x + 2, 4), high_z, half, across(-step))
    own.wait()
    for copy in sent:
        copy.wait_send()


def shards(hologram, background):
    vmem, dma = pltpu.VMEM, pltpu.SemaphoreType.DMA
    table = vmem((RADIX, RADIX, 128), F32)
    merged = pl.pallas_call(
        whole_kernel,
        name="whole",
        out_shape=jax.ShapeDtypeStruct((4, 4, 8, N), BF16),
        in_specs=[pl.BlockSpec(memory_space=pltpu.HBM)] * 8,
        out_specs=pl.BlockSpec(memory_space=vmem),
        scratch_shapes=[
            vmem((128, N), BF16),
            vmem((128, N), BF16),
            vmem((128, RADIX), F32),
            vmem((128, 128), BF16),
            vmem((128, 128), BF16),
            vmem((2, 256, 256), BF16),
            vmem((128, 128), BF16),
            vmem((128, 128), BF16),
            dma((8,)),
            vmem((8, 128, 128), BF16),
            vmem((32, 128, 128), BF16),
            vmem((8, 128, 128), BF16),
            vmem((RADIX * WIDE, 128), F32),
            vmem((2 * RADIX * WIDE, 128), F32),
            vmem((2 * RADIX * WIDE, 128), F32),
            table,
            table,
            vmem((N, 128), F32),
            vmem((N, 128), F32),
            vmem((32, CHUNKS, 4, PART, 128), BF16),
            vmem((CHUNKS, 14, 4, PART, 128), BF16),
            vmem((32, CHUNKS, 4, PART, 128), BF16),
            vmem((CHUNKS, 16, 8, LANES), BF16),
            vmem((CHUNKS, 2, 8, LANES // 2), BF16),
            vmem((CHUNKS, PLANES, 8, LANES), BF16),
            vmem((CHUNKS, PLANES, 8, LANES), F32),
            *[vmem((CHUNKS, PLANES, LANES), BF16)] * 4,
            vmem((8, N), BF16),
            dma((31,)),
            dma((32,)),
            dma((8,)),
            dma((8,)),
            dma((CHUNKS, 31)),
            dma((32, CHUNKS)),
            dma((CHUNKS, 14)),
            dma((CHUNKS, 14)),
            dma((CHUNKS, 14)),
            dma((CHUNKS, 16, 2)),
            dma((CHUNKS, 4)),
            dma((CHUNKS, 2)),
            dma((CHUNKS, 2)),
            dma((CHUNKS, 2)),
            dma((20,)),
            dma((4, 4, 2)),
            dma,
        ],
        compiler_params=pltpu.CompilerParams(
            collective_id=0, has_side_effects=True, vmem_limit_bytes=65400000
        ),
    )(hologram, background, *pass_tables())
    return merged.reshape(128, N).astype(F32)


def solution(mesh):
    fine = Mesh(mesh.devices.reshape(SIZES), AXES)
    spec = P(("zl", "y", "c"), None)
    return jax.shard_map(
        shards, mesh=fine, in_specs=(spec, spec), out_specs=spec, check_vma=False
    )
```

```python
import math

import jax
import jax.numpy as jnp
import numpy as np
from jax import lax
from jax.experimental import pallas as pl
from jax.experimental.pallas import tpu as pltpu
from jax.sharding import Mesh
from jax.sharding import PartitionSpec as P

N = 4096
RADIX = 64
PLANES = 16
WIDE = 72
DEEP = 136
CHUNKS = 2
PART = RADIX // CHUNKS
LANES = N // CHUNKS
AXES = ("zh", "x", "zl", "y", "c")
SIZES = (4, 4, 4, 4, 2)
MESH = pl.DeviceIdType.MESH
NT = (((1,), (1,)), ((), ()))
F32 = jnp.float32
BF16 = jnp.bfloat16

wave_number = 0.6
depth_start = 8.0
depth_step = 2.0


def fourier_tables(sign_value):
    indices = np.arange(RADIX)
    angles = (indices[:, None] * indices[None, :] % RADIX) * (sign_value * 2.0 * math.pi / RADIX)
    real, imag = np.cos(angles) / math.sqrt(RADIX), np.sin(angles) / math.sqrt(RADIX)
    matrix = np.stack([np.stack([real, -imag]), np.stack([imag, real])])
    return matrix.astype(np.float32)


def twiddle_table(sign_value):
    indices = np.arange(RADIX)
    angles = (indices[:, None] * indices[None, :]) * (sign_value * 2.0 * math.pi / N)
    return np.cos(angles).astype(np.float32), np.sin(angles).astype(np.float32)


def pass_tables():
    ahead, back = fourier_tables(-1.0), fourier_tables(1.0)
    flat = lambda table: table.transpose(0, 2, 1, 3).reshape(128, 128)
    natural = np.eye(128, dtype=np.float32).reshape(2, CHUNKS, PART, 128)
    natural = natural.swapaxes(0, 1).reshape(128, 128)
    both = np.zeros((2, 2, 2, RADIX, 2, 128), np.float32)
    for lane in range(128):
        far, j = divmod(lane, RADIX)
        both[1, :, far, :, :, lane] = back[:, :, :, RADIX - 1 - j if far else j].transpose(0, 2, 1)
        if j >= RADIX // 2:
            half, j = 1, (95 - j if far else j - 32)
        else:
            half, j = 0, ((RADIX - j if j else 32) if far else j)
        both[0, :, half, :, :, lane] = back[:, :, :, j].transpose(0, 2, 1)
    tables = (
        flat(ahead),
        flat(back),
        both.reshape(2, 256, 256),
        np.eye(128, dtype=np.float32),
        natural,
    )
    return [jnp.asarray(ahead[:, 0].reshape(128, RADIX), F32)] + [
        jnp.asarray(table, BF16) for table in tables
    ]


def row_pass(x, hologram, background, open_exact, ahead, eye, wide, middle, sections):
    for t in range(32):
        here = slice(t * 128, (t + 1) * 128)
        ratio = hologram[:, here].astype(F32) / background[:, here].astype(F32)
        contrast = (ratio - 1.0).astype(BF16)
        made = lax.dot_general(eye[...], contrast, NT, preferred_element_type=F32)
        wide[2 * t * WIDE : 2 * t * WIDE + RADIX, :] = made[:RADIX]
        wide[(2 * t + 1) * WIDE : (2 * t + 1) * WIDE + RADIX, :] = made[RADIX:]
    own = pl.multiple_of(x * 8, 8)
    chosen = [open_exact[pl.ds(own, 8), :], open_exact[32:40, :]]
    chosen += [open_exact[pl.ds(RADIX + own, 8), :], open_exact[RADIX + 32 : RADIX + 40, :]]
    matrix = jnp.concatenate(chosen).astype(BF16)
    row = lax.broadcasted_iota(jnp.int32, (16, 128), 0)
    k = jnp.where(row < 8, x * 8 + row, row + 24).astype(F32)

    def opening(b, carry):
        data = wide[pl.ds(b, RADIX, stride=WIDE), :].astype(BF16)
        made = jnp.dot(matrix, data, preferred_element_type=F32)
        real, imag = made[:16], made[16:]
        sine, cosine = sine_cosine(k * (b.astype(F32) / N))
        middle[pl.ds(b, 16, stride=DEEP), :] = real * cosine + imag * sine
        middle[pl.ds(RADIX + b, 16, stride=DEEP), :] = imag * cosine - real * sine
        return carry

    lax.fori_loop(0, RADIX, opening, 0, unroll=16)

    def section(index):
        made = matmul(ahead, middle[index * DEEP : index * DEEP + 128, :].astype(BF16))
        return lax.dot_general(eye[...], made.astype(BF16), NT, preferred_element_type=F32)

    lane = lax.broadcasted_iota(jnp.int32, (128, 128), 1)
    zero, half = section(0), section(8)
    turned = pltpu.roll(zero, 32, 1)
    packed = jnp.where(lax.rem(lane, RADIX) >= 32, pltpu.roll(half, 32, 1), zero)
    packed = jnp.where(lane == RADIX, turned, packed)
    sections[0] = jnp.where(x == 0, packed, zero).astype(BF16)
    for index in range(1, 8):
        sections[index] = section(index).astype(BF16)


def remote(source, target, send_sem, recv_sem, device):
    return pltpu.make_async_remote_copy(
        src_ref=source,
        dst_ref=target,
        send_sem=send_sem,
        recv_sem=recv_sem,
        device_id=device,
        device_id_type=MESH,
    )


def sine_cosine(turns):
    half = (turns - jnp.floor(turns + 0.5)) * math.pi
    square = half * half
    sine, cosine = jnp.zeros_like(half), jnp.zeros_like(half)
    for power in range(6, -1, -1):
        cosine = cosine * square + (-1) ** power / math.factorial(2 * power)
        if power < 6:
            sine = sine * square + (-1) ** power / math.factorial(2 * power + 1)
    sine = sine * half
    return 2.0 * sine * cosine, 1.0 - 2.0 * sine * sine


def make_tables(me, z, cosines, sines, k_real, k_imag):
    distance = depth_start + depth_step * z.astype(F32)
    lane = lax.broadcasted_iota(jnp.int32, (RADIX, 128), 1)
    row = lax.broadcasted_iota(jnp.int32, (RADIX, 128), 0)
    j = lax.rem(lane, RADIX)
    general = me + RADIX * j
    lone = jnp.where(j == 0, jnp.where(lane >= RADIX, N // 2, 0), RADIX * j)
    lone = jnp.where(j >= RADIX // 2, 32 + RADIX * (j - RADIX // 2), lone)
    natural = jnp.where(me == 0, lone, general)
    freq = jnp.where(natural >= N // 2, natural - N, natural).astype(F32) / N
    column_part = freq * freq
    base = jnp.where(row >= RADIX // 2, RADIX * row - N, RADIX * row)
    limit = wave_number * wave_number

    def tile(k, carry):
        here = pl.ds(k * RADIX, RADIX)
        sine, cosine = sine_cosine((row * k).astype(F32) / N)
        cosines[k], sines[k] = cosine, sine
        freq = (base + k).astype(F32) / N
        radial = freq * freq + column_part
        amplitude = jnp.exp(
            (-2.0 * math.pi * distance) * jnp.sqrt(jnp.maximum(radial - limit, 0.0))
        )
        turns = distance * (jnp.sqrt(jnp.maximum(limit - radial, 0.0)) - wave_number)
        sine, cosine = sine_cosine(turns)
        k_real[here, :] = amplitude * cosine
        k_imag[here, :] = amplitude * sine
        return carry

    lax.fori_loop(0, RADIX, tile, 0)


def widen(slab, columns, wide):
    for half in range(2):
        rows = columns[slab, pl.ds(half * RADIX, RADIX), :]
        wide[pl.ds((2 * slab + half) * WIDE, RADIX), :] = rows.astype(F32)


def matmul(matrix, data):
    return jnp.dot(matrix[...], data, preferred_element_type=F32)


def matmul_right(data, matrix):
    return jnp.dot(data, matrix[...], preferred_element_type=F32)


def column_pass(me, tables, wide, middle, other, k_real, k_imag, cosines, sines):
    open_exact, ahead, back = tables
    lane = lax.broadcasted_iota(jnp.int32, (RADIX, 128), 1)
    low = lane < RADIX
    alone = (me == 0) & (lax.rem(lane, RADIX) == 0)

    open_ahead = open_exact[...].astype(BF16)

    def first(b, carry):
        made = matmul(open_ahead, wide[pl.ds(b, RADIX, stride=WIDE), :].astype(BF16))
        real, imag = made[:RADIX], made[RADIX:]
        cosine, sine = cosines[b], sines[b]
        middle[pl.ds(b, RADIX, stride=DEEP), :] = real * cosine + imag * sine
        middle[pl.ds(RADIX + b, RADIX, stride=DEEP), :] = imag * cosine - real * sine
        return carry

    lax.fori_loop(0, RADIX, first, 0, unroll=16)

    def second(k, carry):
        made = matmul(ahead, middle[pl.ds(k * DEEP, 128), :].astype(BF16))
        real, imag = made[:RADIX], made[RADIX:]
        real_turn, imag_turn = pltpu.roll(real, RADIX, 1), pltpu.roll(imag, RADIX, 1)
        spectrum_real = jnp.where(low, real - imag_turn, real_turn + imag)
        spectrum_imag = jnp.where(low, imag + real_turn, imag_turn - real)
        spectrum_real = jnp.where(alone, real, spectrum_real).astype(BF16).astype(F32)
        spectrum_imag = jnp.where(alone, imag, spectrum_imag).astype(BF16).astype(F32)
        here = pl.ds(k * RADIX, RADIX)
        kernel_real, kernel_imag = k_real[here, :], k_imag[here, :]
        propagated = jnp.concatenate(
            [
                spectrum_real * kernel_real - spectrum_imag * kernel_imag,
                spectrum_real * kernel_imag + spectrum_imag * kernel_real,
            ]
        )
        made = matmul(back, propagated.astype(BF16))
        real, imag = made[:RADIX], made[RADIX:]
        cosine, sine = cosines[k], sines[k]
        other[pl.ds(k, RADIX, stride=DEEP), :] = real * cosine - imag * sine
        other[pl.ds(RADIX + k, RADIX, stride=DEEP), :] = real * sine + imag * cosine
        return carry

    lax.fori_loop(0, RADIX, second, 0, unroll=16)

    def third(b, carry):
        made = matmul(back, other[pl.ds(b * DEEP, 128), :].astype(BF16))
        middle[pl.ds(b, RADIX, stride=WIDE), :] = made[:RADIX]
        middle[pl.ds(RADIX * WIDE + b, RADIX, stride=WIDE), :] = made[RADIX:]
        return carry

    lax.fori_loop(0, RADIX, third, 0, unroll=16)


def block_rows(middle, part, x, yc):
    rows = []
    for low_z in range(4):
        start = (part * RADIX + low_z * 16 + yc * 2) * WIDE + lax.rem(x - low_z + 4, 4) * 8
        for zh in range(4):
            offset = pl.multiple_of(start + zh // 2 * WIDE + zh % 2 * 32, 8)
            rows.append(middle[pl.ds(offset, 8), :])
    return jnp.concatenate(rows).astype(BF16)


def partner(k):
    return jnp.where(k == 0, 32, RADIX - k)


def make_block(me, target, both, middle, cosines, sines, blocks):
    x, yc = target // 8, lax.rem(target, 8)
    data = jnp.concatenate([block_rows(middle, part, x, yc) for part in range(2)], axis=1)
    made = lax.dot_general(both[jnp.minimum(me, 1)], data, NT, preferred_element_type=F32)
    for half in range(2):
        k = partner(me) if half else me
        real = made[half * RADIX : (half + 1) * RADIX]
        imag = made[128 + half * RADIX : 128 + (half + 1) * RADIX]
        cosine, sine = cosines[k], sines[k]
        turned = (real * cosine - imag * sine, real * sine + imag * cosine)
        for part in range(2):
            for chunk in range(CHUNKS):
                rows = turned[part][chunk * PART : (chunk + 1) * PART]
                blocks[target, chunk, part * 2 + half] = rows.astype(BF16)


def place_block(source, chunk, gathered, other):
    for part in range(2):
        for half in range(2):
            k = partner(source) if half else source
            rows = gathered[source, chunk, part * 2 + half].astype(F32)
            start = chunk * PART * DEEP + part * RADIX + k
            other[pl.ds(start, PART, stride=DEEP), :] = rows


def close_rows(chunk, back, eye, other, wide, planes):
    def closing(index, carry):
        b = chunk * PART + index
        made = matmul(back, other[pl.ds(b * DEEP, 128), :].astype(BF16))
        real, imag = made[:RADIX], made[RADIX:]
        wide[pl.ds(b, RADIX, stride=WIDE), :] = real * real + imag * imag
        return carry

    lax.fori_loop(0, PART, closing, 0, unroll=16)
    span = 128 // PART
    for t in range(LANES // 128):
        rows = [
            wide[a * WIDE + chunk * PART : a * WIDE + (chunk + 1) * PART, :]
            for a in range(span * t, span * (t + 1))
        ]
        block = jnp.concatenate(rows).astype(BF16)
        made = lax.dot_general(eye[...], block, NT, preferred_element_type=F32)
        here = slice(t * 128, (t + 1) * 128)
        planes[chunk, :, :, here] = made.reshape(16, 8, 128).astype(BF16)


def edge_rows(chunk, stack, low, high):
    rows = lax.broadcasted_iota(jnp.int32, (PLANES, LANES), 0)
    bottom, top = jnp.zeros((PLANES, LANES), F32), jnp.zeros((PLANES, LANES), F32)
    for g in range(PLANES):
        plane = stack[chunk, g].astype(F32)
        bottom = jnp.where(rows == g, plane[0:1], bottom)
        top = jnp.where(rows == g, plane[7:8], top)
    low[chunk] = bottom.astype(BF16)
    high[chunk] = top.astype(BF16)


def depth_scores(chunk, stack, scores):
    def one(g, carry):
        lower = stack[chunk, jnp.maximum(g - 1, 0)].astype(F32)
        upper = stack[chunk, jnp.minimum(g + 1, PLANES - 1)].astype(F32)
        scores[chunk, g] = (upper - lower) * (upper - lower)
        return carry

    lax.fori_loop(0, PLANES, one, 0, unroll=2)


def row_scores(chunk, stack, scores, north, south, first, last):
    row = lax.broadcasted_iota(jnp.int32, (8, LANES), 0)
    norths, souths = north[chunk].astype(F32), south[chunk].astype(F32)
    for g in range(PLANES):
        centre = stack[chunk, g].astype(F32)
        before = jnp.where(first, centre[0:1], norths[g : g + 1])
        after = jnp.where(last, centre[7:8], souths[g : g + 1])
        above = jnp.where(row == 0, before, pltpu.roll(centre, 1, 0))
        below = jnp.where(row == 7, after, pltpu.roll(centre, 7, 0))
        scores[chunk, g] = scores[chunk, g] + (below - above) * (below - above)


def side_scores(chunk, stack, scores):
    lane = lax.broadcasted_iota(jnp.int32, (8, LANES), 1)
    start, end = lax.rem(lane, PART) == 0, lax.rem(lane, PART) == PART - 1

    def one(g, carry):
        centre = stack[chunk, g].astype(F32)
        before = stack[(chunk - 1) % CHUNKS, g].astype(F32)
        after = stack[(chunk + 1) % CHUNKS, g].astype(F32)
        if chunk:
            before = pltpu.roll(before, LANES - PART + 1, 1)
        else:
            before = jnp.where(lane == 0, centre, pltpu.roll(before, 1, 1))
        if chunk < CHUNKS - 1:
            after = pltpu.roll(after, PART - 1, 1)
        else:
            after = jnp.where(lane == LANES - 1, centre, pltpu.roll(after, LANES - 1, 1))
        west = jnp.where(start, before, pltpu.roll(centre, 1, 1))
        east = jnp.where(end, after, pltpu.roll(centre, LANES - 1, 1))
        scores[chunk, g] = scores[chunk, g] + (east - west) * (east - west)
        return carry

    lax.fori_loop(0, PLANES, one, 0, unroll=2)


def sharpest(scores, natural, piece):
    best = [jnp.max(scores[chunk], axis=0) / 8.0 for chunk in range(CHUNKS)]
    width = 128 // CHUNKS
    lane = lax.broadcasted_iota(jnp.int32, (8, 128), 1)
    tiles = []
    for t in range(32):
        here = slice(t // CHUNKS * 128, (t // CHUNKS + 1) * 128)
        made = jnp.zeros((8, 128), F32)
        for chunk in range(CHUNKS):
            shift = (chunk - t) % CHUNKS * width
            moved = best[chunk][:, here]
            moved = pltpu.roll(moved, shift, 1) if shift else moved
            made = jnp.where(lane // width == chunk, moved, made)
        tiles.append(made)
    made = matmul_right(jnp.concatenate(tiles).astype(BF16), natural)
    for t in range(32):
        piece[:, t * 128 : (t + 1) * 128] = made[t * 8 : (t + 1) * 8].astype(BF16)


def whole_kernel(
    hologram_in, background_in, exact_in, ahead_in, back_in, both_in, eye_in, natural_in, out,
    hologram, background, open_exact, ahead, back, both, eye, natural, load_sem,
    sections, columns, passing, wide, middle, other, cosines, sines, k_real, k_imag,
    blocks, staged, gathered, planes, opposite, stack, scores, low, high, north, south, piece,
    send1, recv1, relay1_send, relay1_recv, send2, recv2, relay_send, relay_recv,
    send3, recv3, far_send, far_recv, send4, recv4, send5, recv5, own_sem,
):
    at = {name: lax.axis_index(name) for name in AXES}
    x, y, c, zh, zl = at["x"], at["y"], at["c"], at["zh"], at["zl"]
    yc, z = y * 2 + c, zh * 4 + zl
    me, slab = x * 8 + yc, zl * 8 + yc
    xs = lax.rem(x - zl + 4, 4)
    q = (slab * 4 + zh) * 4 + xs

    def near(dy, dc, turn):
        layer = lax.rem(z + turn + 16, 16)
        return {
            "zh": layer // 4,
            "x": x,
            "zl": lax.rem(layer, 4),
            "y": lax.rem(y + dy + 4, 4),
            "c": lax.rem(c + dc, 2),
        }

    def level(dx, dy, dc):
        return {
            "zh": zh,
            "x": lax.rem(x + dx + 4, 4),
            "zl": zl,
            "y": lax.rem(y + dy + 4, 4),
            "c": lax.rem(c + dc, 2),
        }

    def number(device):
        return device["x"] * 8 + device["y"] * 2 + device["c"]

    def slab_of(device):
        return device["zl"] * 8 + device["y"] * 2 + device["c"]

    def above(layer):
        return {**at, "zh": layer // 4, "zl": lax.rem(layer, 4)}

    def up(turn):
        return lax.rem(z + turn + 16, 16)

    def block_owner(index):
        owner = index // 16
        low_z = owner // 8
        return {
            "zh": lax.rem(index // 4, 4),
            "x": lax.rem(lax.rem(index, 4) + low_z, 4),
            "zl": low_z,
            "y": lax.rem(owner // 2, 4),
            "c": lax.rem(owner, 2),
        }

    moves, hops = [], []
    for turn in (2, 1, -1, 0):
        for dc in (1, 0):
            toward = -2 if turn == 2 and dc else turn
            hops.append((-1 if dc else 1, dc, toward))
            for dy in (1, -1, 0):
                if (dy, dc, turn) != (0, 0, 0):
                    moves.append((dy, dc, toward))
    relayed, direct = [], []
    for dx in (2, 1, 3, 0):
        for dy in (2, 1, 3, 0):
            for dc in (1, 0):
                if 2 in (dx, dy):
                    side = -1 if dc else 1
                    hop = [side if d == 2 else (-1 if d == 3 else d) for d in (dx, dy)]
                    rest = [side if d == 2 else 0 for d in (dx, dy)]
                    relayed.append((hop[0], hop[1], dc, rest[0], rest[1]))
                elif (dx, dy, dc) != (0, 0, 0):
                    direct.append((-1 if dx == 3 else dx, -1 if dy == 3 else dy, dc))
    distant = [(hx + rx, hy + ry, dc) for hx, hy, dc, rx, ry in relayed]
    turns = (7, -7, 6, -6, 5, -5, 4, -4, 3, -3, 2, -2, 1, -1)
    ahead_q, behind_q = block_owner(lax.rem(q + 1, 512)), block_owner(lax.rem(q + 511, 512))

    pairs = (
        (hologram_in, hologram), (background_in, background), (eye_in, eye),
        (exact_in, open_exact), (ahead_in, ahead), (back_in, back), (both_in, both),
        (natural_in, natural),
    )
    loads = [
        pltpu.make_async_copy(source, target, load_sem.at[index])
        for index, (source, target) in enumerate(pairs)
    ]
    for copy in loads:
        copy.start()
    barrier = pltpu.get_barrier_semaphore()
    everyone = [near(-dy, dc, -turn) for dy, dc, turn in moves + hops]
    everyone += [level(dx, dy, dc) for dx in range(4) for dy in range(4) for dc in range(2)][1:]
    everyone += [above(up(turn)) for turn in turns]
    everyone += [ahead_q, behind_q]
    for device in everyone:
        pl.semaphore_signal(barrier, inc=1, device_id=device, device_id_type=MESH)
    for copy in loads:
        copy.wait()
    row_pass(x, hologram, background, open_exact, ahead, eye, wide, middle, sections)
    pl.semaphore_wait(barrier, len(everyone))

    sent = []
    for index, (side, dc, turn) in enumerate(hops):
        target = near(2, dc, turn)
        sent.append(
            remote(
                sections.at[target["y"] * 2 + target["c"]],
                passing.at[index],
                relay1_send.at[index],
                relay1_recv.at[index],
                near(side, dc, turn),
            )
        )
        sent[-1].start()
    for index, (dy, dc, turn) in enumerate(moves):
        target = near(dy, dc, turn)
        sent.append(
            remote(
                sections.at[target["y"] * 2 + target["c"]],
                columns.at[slab],
                send1.at[index],
                recv1.at[slab],
                target,
            )
        )
        sent[-1].start()
    own = pltpu.make_async_copy(sections.at[yc], columns.at[slab], own_sem)
    own.start()
    make_tables(me, z, cosines, sines, k_real, k_imag)
    own.wait()
    widen(slab, columns, wide)
    for index, (side, dc, turn) in enumerate(hops):
        source = near(-side, dc, -turn)
        slot = passing.at[index]
        remote(slot, slot, own_sem, relay1_recv.at[index], source).wait_recv()
        sent.append(
            remote(
                slot,
                columns.at[slab_of(source)],
                send1.at[len(moves) + index],
                recv1.at[slab_of(source)],
                level(0, side, 0),
            )
        )
        sent[-1].start()
    arrivals = [(-dy, dc, -turn) for dy, dc, turn in reversed(moves)]
    arrivals += [(2, dc, -turn) for side, dc, turn in hops]
    for dy, dc, turn in arrivals:
        source = near(dy, dc, turn)
        origin = slab_of(source)
        slot = columns.at[origin]
        remote(slot, slot, own_sem, recv1.at[origin], source).wait_recv()
        widen(origin, columns, wide)
    for copy in sent:
        copy.wait_send()

    tables = (open_exact, ahead, back)
    column_pass(me, tables, wide, middle, other, k_real, k_imag, cosines, sines)

    sent = []

    def send_relayed(chunk, index):
        hx, hy, dc, rx, ry = relayed[index]
        sent.append(
            remote(
                blocks.at[number(level(hx + rx, hy + ry, dc)), chunk],
                staged.at[chunk, index],
                relay_send.at[chunk, index],
                relay_recv.at[chunk, index],
                level(hx, hy, dc),
            )
        )
        sent[-1].start()

    def send_direct(chunk, index):
        device = level(*(direct + distant)[index])
        sent.append(
            remote(
                blocks.at[number(device), chunk],
                gathered.at[me, chunk],
                send2.at[chunk, index],
                recv2.at[me, chunk],
                device,
            )
        )
        sent[-1].start()

    def make(device):
        make_block(me, number(device), both, middle, cosines, sines, blocks)

    for index, (hx, hy, dc, rx, ry) in enumerate(relayed):
        make(level(hx + rx, hy + ry, dc))
        if index % 2:
            send_relayed(0, index - 1)
            send_relayed(0, index)
    for index, offset in enumerate(direct):
        make(level(*offset))
        if index % 2:
            send_direct(0, index - 1)
            send_direct(0, index)
    send_direct(0, len(direct) - 1)
    make(level(0, 0, 0))
    own = pltpu.make_async_copy(blocks.at[me], gathered.at[me], own_sem)
    own.start()
    own.wait()

    def part(chunk, layer):
        return planes.at[chunk, lax.rem(layer, 4) * 4 + layer // 4]

    lanes = (pl.ds(0, LANES // 2), pl.ds(LANES // 2, LANES // 2))

    def forward_far(chunk):
        for side, turn in enumerate((4, -4)):
            slot = opposite.at[chunk, side]
            remote(slot, slot, own_sem, far_recv.at[chunk, side], above(up(-turn))).wait_recv()
            sent.append(
                remote(
                    slot,
                    stack.at[chunk, up(-turn), :, lanes[side]],
                    far_send.at[chunk, 2 + side],
                    recv3.at[chunk, up(-turn), side],
                    above(up(turn)),
                )
            )
            sent[-1].start()

    for chunk in range(CHUNKS):
        for index, (hx, hy, dc, rx, ry) in enumerate(relayed if chunk == 0 else []):
            source = level(-hx, -hy, dc)
            slot = staged.at[chunk, index]
            remote(slot, slot, own_sem, relay_recv.at[chunk, index], source).wait_recv()
            sent.append(
                remote(
                    slot,
                    gathered.at[number(source), chunk],
                    send2.at[chunk, len(direct) + index],
                    recv2.at[number(source), chunk],
                    level(rx, ry, 0),
                )
            )
            sent[-1].start()
        if chunk + 1 < CHUNKS:
            for index in reversed(range(len(direct + distant))):
                send_direct(chunk + 1, index)
        place_block(me, chunk, gathered, other)
        arrivals = [(-dx, -dy, dc) for dx, dy, dc in direct]
        arrivals += [(-hx - rx, -hy - ry, dc) for hx, hy, dc, rx, ry in relayed]
        for dx, dy, dc in arrivals:
            device = level(dx, dy, dc)
            source = number(device)
            slot = gathered.at[source, chunk]
            remote(slot, slot, own_sem, recv2.at[source, chunk], device).wait_recv()
            place_block(source, chunk, gathered, other)
        close_rows(chunk, back, eye, other, wide, planes)
        if chunk:
            forward_far(chunk - 1)
        far = up(8)
        for side, turn in enumerate((4, -4)):
            sent.append(
                remote(
                    part(chunk, far).at[:, lanes[side]],
                    opposite.at[chunk, side],
                    far_send.at[chunk, side],
                    far_recv.at[chunk, side],
                    above(up(turn)),
                )
            )
            sent[-1].start()
        for index, turn in enumerate(turns):
            layer = up(turn)
            sent.append(
                remote(
                    part(chunk, layer),
                    stack.at[chunk, z],
                    send3.at[chunk, index],
                    recv3.at[chunk, z, 0],
                    above(layer),
                )
            )
            sent[-1].start()
        own = pltpu.make_async_copy(part(chunk, z), stack.at[chunk, z], own_sem)
        own.start()
        own.wait()
    forward_far(CHUNKS - 1)

    def edges(chunk):
        edge_rows(chunk, stack, low, high)
        pair = [
            remote(
                high.at[chunk], north.at[chunk],
                send4.at[chunk, 0], recv4.at[chunk, 0], ahead_q,
            ),
            remote(
                low.at[chunk], south.at[chunk],
                send4.at[chunk, 1], recv4.at[chunk, 1], behind_q,
            ),
        ]
        for copy in pair:
            copy.start()
        return pair

    for chunk in range(CHUNKS):
        for turn in reversed(turns):
            slot = stack.at[chunk, up(turn)]
            remote(slot, slot, own_sem, recv3.at[chunk, up(turn), 0], above(up(turn))).wait_recv()
        for side, turn in enumerate((-4, 4)):
            slot = stack.at[chunk, up(8), :, lanes[side]]
            remote(slot, slot, own_sem, recv3.at[chunk, up(8), side], above(up(turn))).wait_recv()
        pair = edges(chunk)
        depth_scores(chunk, stack, scores)
        if chunk > 1:
            side_scores(chunk - 1, stack, scores)
        if chunk == CHUNKS - 1:
            side_scores(0, stack, scores)
            side_scores(chunk, stack, scores)
        for copy in pair:
            copy.wait()
        row_scores(chunk, stack, scores, north, south, q == 0, q == 511)
    for copy in sent:
        copy.wait_send()
    sharpest(scores, natural, piece)

    left, right = pl.ds(0, N // 2), pl.ds(N // 2, N // 2)
    halves = (left, right)
    sent = []

    def across(step):
        return {**at, "x": lax.rem(x + step + 4, 4)}

    def along(step):
        return {**at, "zh": lax.rem(zh + step + 4, 4)}

    def row_of(place):
        return lax.rem(place - zl + 4, 4)

    def send(source, target, sem, device):
        sent.append(remote(source, target, send5.at[len(sent)], sem, device))
        sent[-1].start()

    def arrive(place, high_z, half, device):
        slot = out.at[high_z, row_of(place)]
        slot = slot if half is None else slot.at[:, halves[half]]
        sem = recv5.at[place, high_z, half or 0]
        remote(slot, slot, own_sem, sem, device).wait_recv()

    for step in (1, -1):
        send(piece, out.at[zh, xs], recv5.at[x, zh, 0], along(step))
    for step in (1, -1):
        send(piece, out.at[zh, xs], recv5.at[x, zh, 0], across(step))
    own = pltpu.make_async_copy(piece, out.at[zh, xs], own_sem)
    own.start()
    for half, step in enumerate((1, -1)):
        from_z = lax.rem(zh - step + 4, 4)
        arrive(x, from_z, None, along(-step))
        slot = out.at[from_z, xs, :, halves[half]]
        send(slot, slot, recv5.at[x, from_z, half], along(step))
        for turn in (1, -1):
            slot = out.at[from_z, xs]
            send(slot, slot, recv5.at[x, from_z, 0], across(turn))
    far_z = lax.rem(zh + 2, 4)
    for high_z in (zh, lax.rem(zh + 3, 4), lax.rem(zh + 1, 4), far_z):
        if high_z is far_z:
            for half, step in enumerate((1, -1)):
                arrive(x, far_z, half, along(-step))
            for turn in (1, -1):
                slot = out.at[far_z, xs]
                send(slot, slot, recv5.at[x, far_z, 0], across(turn))
        for half, step in enumerate((1, -1)):
            place = lax.rem(x - step + 4, 4)
            arrive(place, high_z, None, across(-step))
            slot = out.at[high_z, row_of(place), :, halves[half]]
            send(slot, slot, recv5.at[place, high_z, half], across(step))
    for high_z in (zh, lax.rem(zh + 3, 4), lax.rem(zh + 1, 4), far_z):
        for half, step in enumerate((1, -1)):
            arrive(lax.rem(x + 2, 4), high_z, half, across(-step))
    own.wait()
    for copy in sent:
        copy.wait_send()


def shards(hologram, background):
    vmem, dma = pltpu.VMEM, pltpu.SemaphoreType.DMA
    table = vmem((RADIX, RADIX, 128), F32)
    merged = pl.pallas_call(
        whole_kernel,
        name="whole",
        out_shape=jax.ShapeDtypeStruct((4, 4, 8, N), BF16),
        in_specs=[pl.BlockSpec(memory_space=pltpu.HBM)] * 8,
        out_specs=pl.BlockSpec(memory_space=vmem),
        scratch_shapes=[
            vmem((128, N), BF16),
            vmem((128, N), BF16),
            vmem((128, RADIX), F32),
            vmem((128, 128), BF16),
            vmem((128, 128), BF16),
            vmem((2, 256, 256), BF16),
            vmem((128, 128), BF16),
            vmem((128, 128), BF16),
            dma((8,)),
            vmem((8, 128, 128), BF16),
            vmem((32, 128, 128), BF16),
            vmem((8, 128, 128), BF16),
            vmem((RADIX * WIDE, 128), F32),
            vmem((2 * RADIX * WIDE, 128), F32),
            vmem((2 * RADIX * WIDE, 128), F32),
            table,
            table,
            vmem((N, 128), F32),
            vmem((N, 128), F32),
            vmem((32, CHUNKS, 4, PART, 128), BF16),
            vmem((CHUNKS, 14, 4, PART, 128), BF16),
            vmem((32, CHUNKS, 4, PART, 128), BF16),
            vmem((CHUNKS, 16, 8, LANES), BF16),
            vmem((CHUNKS, 2, 8, LANES // 2), BF16),
            vmem((CHUNKS, PLANES, 8, LANES), BF16),
            vmem((CHUNKS, PLANES, 8, LANES), F32),
            *[vmem((CHUNKS, PLANES, LANES), BF16)] * 4,
            vmem((8, N), BF16),
            dma((31,)),
            dma((32,)),
            dma((8,)),
            dma((8,)),
            dma((CHUNKS, 31)),
            dma((32, CHUNKS)),
            dma((CHUNKS, 14)),
            dma((CHUNKS, 14)),
            dma((CHUNKS, 14)),
            dma((CHUNKS, 16, 2)),
            dma((CHUNKS, 4)),
            dma((CHUNKS, 2)),
            dma((CHUNKS, 2)),
            dma((CHUNKS, 2)),
            dma((20,)),
            dma((4, 4, 2)),
            dma,
        ],
        compiler_params=pltpu.CompilerParams(
            collective_id=0, has_side_effects=True, vmem_limit_bytes=65400000
        ),
    )(hologram, background, *pass_tables())
    return merged.reshape(128, N).astype(F32)


def solution(mesh):
    fine = Mesh(mesh.devices.reshape(SIZES), AXES)
    spec = P(("zl", "y", "c"), None)
    return jax.shard_map(
        shards, mesh=fine, in_specs=(spec, spec), out_specs=spec, check_vma=False
    )
```
